32 devices in a mesh: dp: 4 (over y, x), ctx: 2 (over core), tp: 4 (over z).
Axes of the slice: x: 2, y: 2, z: 4, core: 2. Of those that a mesh axis runs over, the one named last changes fastest.
Arguments:
- tokens: bfloat16 [4, 512, 1024], P('dp', 'ctx'), may hold values from -6 to 6
- segments: int32 [4, 512], P('dp'), may hold values from 0 to 2, never falling along the last dimension, each value on 1 to 384 neighbouring positions
- cotangent: bfloat16 [4, 512, 1024], P('dp', 'ctx'), may hold values from -6 to 6
- mixer_gain: bfloat16 [1024], P(('dp', 'ctx')), may hold values from 0.5 to 1.5
- mlp_gain: bfloat16 [1024], P(('dp', 'ctx')), may hold values from 0.5 to 1.5
- query_weight: bfloat16 [1024, 1024], P(('dp', 'ctx'), 'tp'), may hold values from -0.1875 to 0.1875
- key_weight: bfloat16 [1024, 1024], P(('dp', 'ctx'), 'tp'), may hold values from -0.1875 to 0.1875
- value_weight: bfloat16 [1024, 2048], P(('dp', 'ctx'), 'tp'), may hold values from -0.1875 to 0.1875
- gate_weight: bfloat16 [1024, 2048], P(('dp', 'ctx'), 'tp'), may hold values from -0.1875 to 0.1875
- decay_weight: bfloat16 [1024, 8], P(('dp', 'ctx'), 'tp'), may hold values from -0.1875 to 0.1875
- beta_weight: bfloat16 [1024, 8], P(('dp', 'ctx'), 'tp'), may hold values from -0.1875 to 0.1875
- output_weight: bfloat16 [1024, 2048], P(('dp', 'ctx'), 'tp'), may hold values from -0.125 to 0.125
- conv_query: float32 [4, 1024], P(None, 'tp'), may hold values from -3 to 3
- conv_key: float32 [4, 1024], P(None, 'tp'), may hold values from -3 to 3
- conv_value: float32 [4, 2048], P(None, 'tp'), may hold values from -3 to 3
- decay_log: float32 [8], P('tp'), may hold values from -7 to -3
- decay_bias: float32 [8], P('tp'), may hold values from -2 to 1
- head_gain: float32 [256], replicated, may hold values from 0.5 to 1.5
- hidden_gate: bfloat16 [1024, 2816], P(('dp', 'ctx'), 'tp'), may hold values from -0.1875 to 0.1875
- hidden_up: bfloat16 [1024, 2816], P(('dp', 'ctx'), 'tp'), may hold values from -0.1875 to 0.1875
- hidden_down: bfloat16 [1024, 2816], P(('dp', 'ctx'), 'tp'), may hold values from -0.109375 to 0.109375
Outputs:
- block_out: bfloat16 [4, 512, 1024], P('dp', 'ctx')
- tokens_grad: float32 [4, 512, 1024], P('dp', 'ctx')
- mixer_gain_grad: float32 [1024], P(('dp', 'ctx'))
- mlp_gain_grad: float32 [1024], P(('dp', 'ctx'))
- query_grad: float32 [1024, 1024], P(('dp', 'ctx'), 'tp')
- key_grad: float32 [1024, 1024], P(('dp', 'ctx'), 'tp')
- value_grad: float32 [1024, 2048], P(('dp', 'ctx'), 'tp')
- gate_grad: float32 [1024, 2048], P(('dp', 'ctx'), 'tp')
- decay_grad: float32 [1024, 8], P(('dp', 'ctx'), 'tp')
- beta_grad: float32 [1024, 8], P(('dp', 'ctx'), 'tp')
- output_grad: float32 [1024, 2048], P(('dp', 'ctx'), 'tp')
- conv_query_grad: float32 [4, 1024], P(None, 'tp')
- conv_key_grad: float32 [4, 1024], P(None, 'tp')
- conv_value_grad: float32 [4, 2048], P(None, 'tp')
- decay_log_grad: float32 [8], P('tp')
- decay_bias_grad: float32 [8], P('tp')
- head_gain_grad: float32 [256], replicated
- hidden_gate_grad: float32 [1024, 2816], P(('dp', 'ctx'), 'tp')
- hidden_up_grad: float32 [1024, 2816], P(('dp', 'ctx'), 'tp')
- hidden_down_grad: float32 [1024, 2816], P(('dp', 'ctx'), 'tp')
The draws below stay inside these ranges and needn't reach their ends.
Inputs may be any that keep to these rules, and one draw needn't show every extreme that they name: `segments`: along each sequence the numbers start at 0, never fall and rise by one at each document's first token; every document has 1 to 384 tokens and one has exactly 384.
All inputs are finite; a program needn't handle non-finite values.
Results may differ from the reference program's by a relative error of at most 0.014.
The reference program's roundings to bfloat16 on the way count: a program that leaves them out, or rounds other values in their place, can miss the bound.
Values may be sent and summed in bfloat16 or wider, within the bound.
A program may use at most 128 MiB of HBM per device.

```python
import math
from functools import partial
import jax
import jax.numpy as jnp
import numpy as np
from jax import lax

D = 1024
HEADS = 8
KEY_DIM = 128
VALUE_DIM = 256
FF = 2816
CONV = 4
GROUP = 64
SEQ_LEN = 512
SEQS = 4
DOCS = 3
DOC_MOST = 384


def shard_levels(key, dims, split, smallest, high):
    loudness = 1.0
    for dim, parts in split:
        heights = jax.random.uniform(jax.random.fold_in(jax.random.fold_in(key, 6), dim), (parts,), jnp.float32, smallest / len(split), high / len(split))
        loudness = loudness * jnp.repeat(jnp.exp(heights), dims[dim] // parts).reshape((-1,) + (1,) * (len(dims) - 1 - dim))
    return loudness


def split_up(count, total, limit, slope):
    portions = [(1 << 20) // math.isqrt(grade ** slope) + 1 for grade in range(2, count + 1)]
    surplus, counts = total - limit - (count - 1), [1] * (count - 1)
    while surplus > 0:
        candidates = [i for i in range(count - 1) if counts[i] < limit]
        whole, budget = sum([portions[i] for i in candidates]), surplus
        for i in candidates:
            addition = min(limit - counts[i], max(1, budget * portions[i] // whole), surplus)
            counts[i] = counts[i] + addition
            surplus = surplus - addition
    return np.array([limit] + counts)


def uneven_parts(rng, amount, total, limit, lean):
    if amount == 2:
        one = jax.random.randint(rng, (), max(1, total - limit), min(limit, total - 1) + 1)
        return jnp.stack([one, total - one])
    sizes = jnp.asarray(split_up(amount, total, limit, lean), jnp.int32)
    pairs = (amount - 1) // 2
    donor, receiver = sizes[1:1 + 2 * pairs:2], sizes[2:2 + 2 * pairs:2]
    room = jnp.minimum(donor - 1, limit - receiver)
    moved = jax.random.randint(jax.random.fold_in(rng, 1), (pairs,), 0, 1 << 20) % (room + 1)
    sizes = sizes.at[1:1 + 2 * pairs:2].set(donor - moved).at[2:2 + 2 * pairs:2].set(receiver + moved)
    return sizes[jax.random.permutation(jax.random.fold_in(rng, 2), amount)]


def bell_draw(stream_key, dims, scale, limit, cuts=(), held_as=jnp.bfloat16):
    level = shard_levels(stream_key, dims, cuts, -0.22, 0.18) if cuts else 1.0
    values = jax.random.normal(stream_key, dims, jnp.float32) * scale * level
    return jnp.minimum(jnp.maximum(values, -limit), limit).astype(held_as)


def setup_inputs(seed: int = 0) -> dict:
    arg_keys = jax.random.split(jax.random.key(seed), 22)
    tokens = bell_draw(arg_keys[0], (SEQS, SEQ_LEN, D), 1.0, 6.0, ((0, 4), (1, 2)))
    segments = jax.vmap(lambda own: jnp.searchsorted(jnp.cumsum(uneven_parts(own, DOCS, SEQ_LEN, DOC_MOST, 2)), jnp.arange(SEQ_LEN), side="right"))(jax.random.split(arg_keys[1], SEQS)).reshape((SEQS, SEQ_LEN)).astype(jnp.int32)
    cotangent = bell_draw(arg_keys[2], (SEQS, SEQ_LEN, D), 1.0, 6.0, ((0, 4), (1, 2)))
    mixer_gain = jnp.clip(1.0 + 0.1 * jax.random.normal(arg_keys[3], (D,), jnp.float32), 0.5, 1.5).astype(jnp.bfloat16)
    mlp_gain = jnp.clip(1.0 + 0.1 * jax.random.normal(arg_keys[4], (D,), jnp.float32), 0.5, 1.5).astype(jnp.bfloat16)
    query_weight = bell_draw(arg_keys[5], (D, HEADS * KEY_DIM), D ** -0.5, 0.1875, ((0, 8), (1, 4)))
    key_weight = bell_draw(arg_keys[6], (D, HEADS * KEY_DIM), D ** -0.5, 0.1875, ((0, 8), (1, 4)))
    value_weight = bell_draw(arg_keys[7], (D, HEADS * VALUE_DIM), D ** -0.5, 0.1875, ((0, 8), (1, 4)))
    gate_weight = bell_draw(arg_keys[8], (D, HEADS * VALUE_DIM), D ** -0.5, 0.1875, ((0, 8), (1, 4)))
    decay_weight = bell_draw(arg_keys[9], (D, HEADS), D ** -0.5, 0.1875, ((0, 8), (1, 4)))
    beta_weight = bell_draw(arg_keys[10], (D, HEADS), D ** -0.5, 0.1875, ((0, 8), (1, 4)))
    output_weight = bell_draw(arg_keys[11], (D, HEADS * VALUE_DIM), (HEADS * VALUE_DIM) ** -0.5, 0.125, ((0, 8), (1, 4)))
    conv_query = bell_draw(arg_keys[12], (CONV, HEADS * KEY_DIM), CONV ** -0.5, 3.0, ((1, 4),), jnp.float32)
    conv_key = bell_draw(arg_keys[13], (CONV, HEADS * KEY_DIM), CONV ** -0.5, 3.0, ((1, 4),), jnp.float32)
    conv_value = bell_draw(arg_keys[14], (CONV, HEADS * VALUE_DIM), CONV ** -0.5, 3.0, ((1, 4),), jnp.float32)
    decay_log = jnp.clip(-7.0 + 4.0 * jax.random.uniform(arg_keys[15], (HEADS,), jnp.float32) ** shard_levels(arg_keys[15], (HEADS,), ((0, 4),), -0.2, 0.2), -7.0, -3.0)
    decay_bias = jnp.clip(-2.0 + 3.0 * jax.random.uniform(arg_keys[16], (HEADS,), jnp.float32) ** shard_levels(arg_keys[16], (HEADS,), ((0, 4),), -0.2, 0.2), -2.0, 1.0)
    head_gain = jnp.clip(1.0 + 0.1 * jax.random.normal(arg_keys[17], (VALUE_DIM,), jnp.float32), 0.5, 1.5)
    hidden_gate = bell_draw(arg_keys[18], (D, FF), D ** -0.5, 0.1875, ((0, 8), (1, 4)))
    hidden_up = bell_draw(arg_keys[19], (D, FF), D ** -0.5, 0.1875, ((0, 8), (1, 4)))
    hidden_down = bell_draw(arg_keys[20], (D, FF), FF ** -0.5, 0.109375, ((0, 8), (1, 4)))
    return dict(tokens=tokens, segments=segments, cotangent=cotangent, mixer_gain=mixer_gain, mlp_gain=mlp_gain, query_weight=query_weight, key_weight=key_weight, value_weight=value_weight, gate_weight=gate_weight, decay_weight=decay_weight, beta_weight=beta_weight, output_weight=output_weight, conv_query=conv_query, conv_key=conv_key, conv_value=conv_value, decay_log=decay_log, decay_bias=decay_bias, head_gain=head_gain, hidden_gate=hidden_gate, hidden_up=hidden_up, hidden_down=hidden_down)


EPSILON = 1e-06
HIGHEST = lax.Precision.HIGHEST

def features(pre_ext, seg_ext, conv_weight, decay_lin, beta_lin, decay_log, decay_bias, key_dim):
    margin = conv_weight.shape[0] - 1
    row_count = pre_ext.shape[0] - margin
    head_count = decay_lin.shape[1]
    own_segment = seg_ext[margin:]
    convolved = jnp.zeros((row_count, pre_ext.shape[1]), jnp.float32)
    for lag in range(margin + 1):
        first_row = margin - lag
        same_doc = (seg_ext[first_row:first_row + row_count] == own_segment).astype(jnp.float32)
        convolved = convolved + conv_weight[lag][None, :] * pre_ext[first_row:first_row + row_count] * same_doc[:, None]
    activated = jax.nn.silu(convolved)
    query_cols = head_count * key_dim
    queries = activated[:, :query_cols].reshape(row_count, head_count, key_dim)
    key_rows = activated[:, query_cols:2 * query_cols].reshape(row_count, head_count, key_dim)
    value_rows = activated[:, 2 * query_cols:].reshape(row_count, head_count, -1)
    queries = queries * lax.rsqrt(lax.optimization_barrier(jnp.sum(queries * queries, -1, keepdims=True)) + EPSILON) * key_dim ** (-0.5)
    key_rows = key_rows * lax.rsqrt(lax.optimization_barrier(jnp.sum(key_rows * key_rows, -1, keepdims=True)) + EPSILON)
    decay_rate = -jnp.exp(decay_log)[None, :] * jax.nn.softplus(decay_lin + decay_bias[None, :])
    beta_gate = jax.nn.sigmoid(beta_lin)
    starts = (own_segment != seg_ext[margin - 1:margin - 1 + row_count]).astype(jnp.float32)
    return (queries, key_rows, value_rows, decay_rate, beta_gate, starts)

def unit_lower_inverse(lower_part):
    order = lower_part.shape[-1]
    negated = -lower_part
    inverse = jnp.eye(order, dtype=jnp.float32)[None] + negated
    power = negated
    span = 2
    while span < order:
        power = jnp.einsum('hij,hjk->hik', power, power, precision=HIGHEST)
        inverse = inverse + jnp.einsum('hij,hjk->hik', inverse, power, precision=HIGHEST)
        span = span * 2
    return inverse

def group_update(memory, inputs):
    queries, key_rows, value_rows, decay_rate, beta_gate, starts = inputs
    order = queries.shape[0]
    cumulative = jnp.cumsum(decay_rate, axis=0)
    counted = jnp.cumsum(starts)
    position = jnp.arange(order)
    same_doc = (counted[:, None] == counted[None, :]) & (position[None, :] <= position[:, None])
    strictly = (same_doc & (position[None, :] < position[:, None])).astype(jnp.float32)
    spread = cumulative[:, None, :] - cumulative[None, :, :]
    decay_pair = jnp.exp(jnp.where(same_doc[:, :, None], spread, 0.0)) * same_doc.astype(jnp.float32)[:, :, None]
    anchor = jnp.exp(cumulative) * (counted == 0).astype(jnp.float32)[:, None]
    closing = decay_pair[order - 1]
    key_gram = jnp.einsum('thd,jhd->htj', key_rows, key_rows, precision=HIGHEST)
    lower_part = jnp.transpose(beta_gate)[:, :, None] * jnp.transpose(decay_pair, (2, 0, 1)) * key_gram * strictly[None]
    inverse = unit_lower_inverse(lower_part)
    key_state = jnp.einsum('thd,hdw->thw', key_rows, memory, precision=HIGHEST)
    target = beta_gate[:, :, None] * (value_rows - anchor[:, :, None] * key_state)
    updates = jnp.einsum('htj,jhw->thw', inverse, target, precision=HIGHEST)
    query_state = jnp.einsum('thd,hdw->thw', queries, memory, precision=HIGHEST)
    query_key = jnp.einsum('thd,jhd->tjh', queries, key_rows, precision=HIGHEST) * decay_pair
    output_rows = anchor[:, :, None] * query_state + jnp.einsum('tjh,jhw->thw', query_key, updates, precision=HIGHEST)
    new_memory = anchor[order - 1][:, None, None] * memory + jnp.einsum('jhd,jhw->hdw', key_rows * closing[:, :, None], updates, precision=HIGHEST)
    return (new_memory, output_rows)

def delta_run(queries, key_rows, value_rows, decay_rate, beta_gate, starts, memory, group):
    row_count = queries.shape[0]
    blocks = row_count // group
    pieces = tuple((member.reshape((blocks, group) + member.shape[1:]) for member in (queries, key_rows, value_rows, decay_rate, beta_gate, starts)))
    last_memory, outputs = lax.scan(group_update, memory, pieces)
    return (last_memory, outputs.reshape((row_count,) + outputs.shape[2:]))

def gated(output_rows, gate_lin, head_gain):
    row_count, head_count, value_dim = output_rows.shape
    scaled = output_rows * lax.rsqrt(lax.optimization_barrier(jnp.mean(output_rows * output_rows, -1, keepdims=True)) + EPSILON)
    gate_rows = gate_lin.reshape(row_count, head_count, value_dim)
    return (scaled * head_gain * jax.nn.silu(gate_rows)).reshape(row_count, head_count * value_dim)

def mixer(pre_ext, gate_lin, decay_lin, beta_lin, conv_weight, decay_log, decay_bias, head_gain, seg_ext, key_dim, group):
    queries, key_rows, value_rows, decay_rate, beta_gate, starts = features(pre_ext, seg_ext, conv_weight, decay_lin, beta_lin, decay_log, decay_bias, key_dim)
    memory = jnp.zeros((decay_lin.shape[1], key_dim, value_rows.shape[2]), jnp.float32)
    last_memory, output_rows = delta_run(queries, key_rows, value_rows, decay_rate, beta_gate, starts, memory, group)
    return gated(output_rows, gate_lin, head_gain)

def reference(tokens, segments, cotangent, mixer_gain, mlp_gain, query_weight, key_weight, value_weight, gate_weight, decay_weight, beta_weight, output_weight, conv_query, conv_key, conv_value, decay_log, decay_bias, head_gain, hidden_gate, hidden_up, hidden_down):
    in_weights = jnp.concatenate([query_weight, key_weight, value_weight, gate_weight, decay_weight, beta_weight], 1)
    conv_weight = jnp.concatenate([conv_query, conv_key, conv_value], 1)
    query_cols = HEADS * KEY_DIM
    value_cols = HEADS * VALUE_DIM
    conv_cols = 2 * query_cols + value_cols
    margin = CONV - 1
    gain_one = mixer_gain.astype(jnp.float32)
    gain_two = mlp_gain.astype(jnp.float32)

    def one_sequence(items):
        token_rows, seg_row, grad_rows = items
        inputs = token_rows.astype(jnp.float32)
        rms_one = lax.rsqrt(lax.optimization_barrier(jnp.mean(inputs * inputs, -1, keepdims=True)) + EPSILON)
        normed_one = inputs * rms_one
        hidden_one = (normed_one * gain_one).astype(jnp.bfloat16)
        projected = jnp.dot(hidden_one, in_weights, preferred_element_type=jnp.float32)
        pre_conv = projected[:, :conv_cols].astype(jnp.bfloat16)
        gate_lin = projected[:, conv_cols:conv_cols + value_cols]
        decay_lin = projected[:, conv_cols + value_cols:conv_cols + value_cols + HEADS]
        beta_lin = projected[:, conv_cols + value_cols + HEADS:]
        pre_ext = jnp.concatenate([jnp.zeros((margin, conv_cols), jnp.float32), pre_conv.astype(jnp.float32)], 0)
        seg_ext = jnp.concatenate([jnp.full((margin,), -1, jnp.int32), seg_row.astype(jnp.int32)], 0)
        mixer_fn = partial(mixer, seg_ext=seg_ext, key_dim=KEY_DIM, group=GROUP)
        mixed, mixer_back = jax.vjp(mixer_fn, pre_ext, gate_lin, decay_lin, beta_lin, conv_weight, decay_log, decay_bias, head_gain)
        mixed_b = mixed.astype(jnp.bfloat16)
        middle = inputs + jnp.dot(mixed_b, output_weight.T, preferred_element_type=jnp.float32)
        rms_two = lax.rsqrt(lax.optimization_barrier(jnp.mean(middle * middle, -1, keepdims=True)) + EPSILON)
        normed_two = middle * rms_two
        hidden_two = (normed_two * gain_two).astype(jnp.bfloat16)
        gate_pre = jnp.dot(hidden_two, hidden_gate, preferred_element_type=jnp.float32)
        up_pre = jnp.dot(hidden_two, hidden_up, preferred_element_type=jnp.float32)
        sigma = jax.nn.sigmoid(gate_pre)
        swish = gate_pre * sigma
        activ = (swish * up_pre).astype(jnp.bfloat16)
        block_rows = (middle + jnp.dot(activ, hidden_down.T, preferred_element_type=jnp.float32)).astype(jnp.bfloat16)
        grad_out = grad_rows.astype(jnp.float32)
        d_activ = jnp.dot(grad_rows, hidden_down, preferred_element_type=jnp.float32)
        d_gate_pre = (d_activ * up_pre * sigma * (1.0 + gate_pre * (1.0 - sigma))).astype(jnp.bfloat16)
        d_up_pre = (d_activ * swish).astype(jnp.bfloat16)
        grad_down = jnp.dot(grad_rows.T, activ, preferred_element_type=jnp.float32)
        grad_hgate = jnp.dot(hidden_two.T, d_gate_pre, preferred_element_type=jnp.float32)
        grad_hup = jnp.dot(hidden_two.T, d_up_pre, preferred_element_type=jnp.float32)
        d_hidden_two = jnp.dot(d_gate_pre, hidden_gate.T, preferred_element_type=jnp.float32) + jnp.dot(d_up_pre, hidden_up.T, preferred_element_type=jnp.float32)
        grad_gain_two = lax.optimization_barrier(jnp.sum(d_hidden_two * normed_two, 0))
        dn_two = d_hidden_two * gain_two
        d_middle = grad_out + rms_two * (dn_two - normed_two * lax.optimization_barrier(jnp.mean(dn_two * normed_two, -1, keepdims=True)))
        d_middle_b = d_middle.astype(jnp.bfloat16)
        d_mixed = jnp.dot(d_middle_b, output_weight, preferred_element_type=jnp.float32)
        grad_output = jnp.dot(d_middle_b.T, mixed_b, preferred_element_type=jnp.float32)
        d_pre_ext, d_gate, d_decay, d_beta, d_conv, d_log, d_bias, d_head = mixer_back(d_mixed)
        d_proj = jnp.concatenate([d_pre_ext[margin:], d_gate, d_decay, d_beta], 1).astype(jnp.bfloat16)
        grad_input = jnp.dot(hidden_one.T, d_proj, preferred_element_type=jnp.float32)
        d_hidden_one = jnp.dot(d_proj, in_weights.T, preferred_element_type=jnp.float32)
        grad_gain_one = lax.optimization_barrier(jnp.sum(d_hidden_one * normed_one, 0))
        dn_one = d_hidden_one * gain_one
        grad_tokens = d_middle + rms_one * (dn_one - normed_one * lax.optimization_barrier(jnp.mean(dn_one * normed_one, -1, keepdims=True)))
        grads = (grad_gain_one, grad_gain_two, grad_input, grad_output, d_conv, d_log, d_bias, d_head, grad_hgate, grad_hup, grad_down)
        return (block_rows, grad_tokens, grads)
    block_out, tokens_grad, stacked = lax.map(one_sequence, (tokens, segments, cotangent))
    grad_gain_one, grad_gain_two, grad_input, grad_output, d_conv, d_log, d_bias, d_head, grad_hgate, grad_hup, grad_down = tuple((lax.optimization_barrier(jnp.sum(member, 0)) for member in stacked))
    splits = [0, query_cols, 2 * query_cols, conv_cols, conv_cols + value_cols, conv_cols + value_cols + HEADS, conv_cols + value_cols + 2 * HEADS]
    return (block_out, tokens_grad, grad_gain_one, grad_gain_two, grad_input[:, splits[0]:splits[1]], grad_input[:, splits[1]:splits[2]], grad_input[:, splits[2]:splits[3]], grad_input[:, splits[3]:splits[4]], grad_input[:, splits[4]:splits[5]], grad_input[:, splits[5]:splits[6]], grad_output, d_conv[:, :query_cols], d_conv[:, query_cols:2 * query_cols], d_conv[:, 2 * query_cols:], d_log, d_bias, d_head, grad_hgate, grad_hup, grad_down)
```

```python
from functools import partial

import jax
import jax.numpy as jnp
from jax import lax
from jax.experimental import pallas as pl
from jax.experimental.pallas import tpu as pltpu
from jax.sharding import PartitionSpec as P

EPSILON = 1e-06
HIGHEST = lax.Precision.HIGHEST
LANES = 128


def peer_of(axes, sizes, distance):
    flat = 0
    total = 1
    for axis, size in zip(axes, sizes):
        flat = flat * size + lax.axis_index(axis)
        total = total * size
    other = lax.rem(flat + distance, total)
    where = {}
    for axis, size in reversed(list(zip(axes, sizes))):
        where[axis] = lax.rem(other, size)
        other = other // size
    return where


def greet(axes, sizes, peers):
    barrier = pltpu.get_barrier_semaphore()
    for distance in range(1, peers + 1):
        pl.semaphore_signal(
            barrier,
            inc=1,
            device_id=peer_of(axes, sizes, distance),
            device_id_type=pl.DeviceIdType.MESH,
        )
    pl.semaphore_wait(barrier, peers)


def sum_kernel(axis, size, x_ref, out_ref, parts, mine, got, send, recv, send_two, recv_two):
    peers = size - 1
    me = lax.axis_index(axis)
    rows = x_ref.shape[0] // size
    greet((axis,), (size,), peers)

    def block(index):
        return pl.ds(pl.multiple_of(index * rows, rows), rows)

    copies = []
    for distance in range(1, size):
        other = lax.rem(me + distance, size)
        copy = pltpu.make_async_remote_copy(
            src_ref=x_ref.at[block(other)],
            dst_ref=parts.at[distance - 1],
            send_sem=send.at[distance - 1],
            recv_sem=recv.at[distance - 1],
            device_id={axis: other},
            device_id_type=pl.DeviceIdType.MESH,
        )
        copy.start()
        copies.append(copy)
    total = x_ref[block(me)].astype(jnp.float32)
    for distance in range(1, size):
        copies[distance - 1].wait_recv()
        total = total + parts[distance - 1].astype(jnp.float32)
    total = total.astype(out_ref.dtype)
    mine[...] = total
    out_ref[block(me)] = total
    more = []
    for distance in range(1, size):
        copy = pltpu.make_async_remote_copy(
            src_ref=mine,
            dst_ref=got.at[distance - 1],
            send_sem=send_two.at[distance - 1],
            recv_sem=recv_two.at[distance - 1],
            device_id={axis: lax.rem(me + distance, size)},
            device_id_type=pl.DeviceIdType.MESH,
        )
        copy.start()
        more.append(copy)
    for distance in range(1, size):
        more[distance - 1].wait_recv()
        out_ref[block(lax.rem(me + size - distance, size))] = got[distance - 1]
    for copy in copies + more:
        copy.wait_send()


def summed(value, axis, call):
    size = lax.axis_size(axis)
    if size == 1:
        return value
    rows, cols = value.shape
    piece = (size - 1, rows // size, cols)
    sems = pltpu.SemaphoreType.DMA((size - 1,))
    return pl.pallas_call(
        partial(sum_kernel, axis, size),
        out_shape=jax.ShapeDtypeStruct(value.shape, value.dtype),
        in_specs=[pl.BlockSpec(memory_space=pltpu.VMEM)],
        out_specs=pl.BlockSpec(memory_space=pltpu.VMEM),
        scratch_shapes=[
            pltpu.VMEM(piece, value.dtype),
            pltpu.VMEM(piece[1:], value.dtype),
            pltpu.VMEM(piece, value.dtype),
            sems,
            sems,
            sems,
            sems,
        ],
        cost_estimate=pl.CostEstimate(
            flops=value.size * 40000, bytes_accessed=value.size * 300, transcendentals=0
        ),
        compiler_params=pltpu.CompilerParams(collective_id=call, has_side_effects=True),
        name=f"tp_sum_{call}",
    )(value)


def small_kernel(axes, sizes, peers, x_ref, out_ref, parts, send, recv):
    greet(axes, sizes, peers)
    copies = []
    for distance in range(1, peers + 1):
        copy = pltpu.make_async_remote_copy(
            src_ref=x_ref,
            dst_ref=parts.at[distance - 1],
            send_sem=send.at[distance - 1],
            recv_sem=recv.at[distance - 1],
            device_id=peer_of(axes, sizes, distance),
            device_id_type=pl.DeviceIdType.MESH,
        )
        copy.start()
        copies.append(copy)
    flat = 0
    for axis, size in zip(axes, sizes):
        flat = flat * size + lax.axis_index(axis)
    for copy in copies:
        copy.wait()
    parts[peers] = x_ref[...]
    total = jnp.zeros(x_ref.shape, jnp.float32)
    for owner in range(peers + 1):
        slot = lax.rem(flat + 2 * (peers + 1) - owner - 1, peers + 1)
        total = total + parts[slot]
    out_ref[...] = total


def small_sum(value, axes, call):
    sizes = tuple(lax.axis_size(axis) for axis in axes)
    peers = 1
    for size in sizes:
        peers = peers * size
    peers = peers - 1
    if peers == 0:
        return value
    return pl.pallas_call(
        partial(small_kernel, axes, sizes, peers),
        out_shape=jax.ShapeDtypeStruct(value.shape, value.dtype),
        in_specs=[pl.BlockSpec(memory_space=pltpu.VMEM)],
        out_specs=pl.BlockSpec(memory_space=pltpu.VMEM),
        scratch_shapes=[
            pltpu.VMEM((peers + 1,) + value.shape, value.dtype),
            pltpu.SemaphoreType.DMA((peers,)),
            pltpu.SemaphoreType.DMA((peers,)),
        ],
        cost_estimate=pl.CostEstimate(
            flops=1000000, bytes_accessed=20000000, transcendentals=0
        ),
        compiler_params=pltpu.CompilerParams(collective_id=call, has_side_effects=True),
        name=f"small_sum_{call}",
    )(value)


def passed_along(value, axis, by):
    devices = lax.axis_size(axis)
    pairs = [(i, i + by) for i in range(devices) if 0 <= i + by < devices]
    return lax.ppermute(value, axis, pairs)


EDGE = 16


def halves(value):
    high = value.astype(jnp.bfloat16)
    low = (value - high.astype(jnp.float32)).astype(jnp.bfloat16)
    return high, low


def product(left, right, over=(1, 0)):
    dims = (((over[0],), (over[1],)), ((), ()))

    def one(a, b):
        return lax.dot_general(a, b, dims, preferred_element_type=jnp.float32)

    return one(left[0], right[0]) + (one(left[0], right[1]) + one(left[1], right[0]))


def exact_sum(ones, value, over=(1, 0)):
    dims = (((over[0],), (over[1],)), ((), ()))
    high = value.astype(jnp.bfloat16)
    rest = value - high.astype(jnp.float32)
    middle = rest.astype(jnp.bfloat16)
    low = (rest - middle.astype(jnp.float32)).astype(jnp.bfloat16)
    total = None
    for part in (low, middle, high):
        term = lax.dot_general(ones, part, dims, preferred_element_type=jnp.float32)
        total = term if total is None else total + term
    return total


def logistic(value):
    return 1.0 / (1.0 + jnp.exp(-value))


def row_sum(value):
    return jnp.sum(value, axis=1, keepdims=True)


def iotas(count):
    row = lax.broadcasted_iota(jnp.int32, (count, count), 0)
    col = lax.broadcasted_iota(jnp.int32, (count, count), 1)
    return row, col


def in_lane(lane, index, column):
    return jnp.where(lane == index, column, 0.0)


def lower_inverse_of(lower, row, col):
    order = lower.shape[0]
    apart = row ^ col
    inverse = jnp.where(row == col, 1.0, 0.0) - jnp.where(apart == 1, lower, 0.0)
    level = 1
    while (1 << level) < order:
        cross = jnp.where((apart >> level) == 1, lower, 0.0)
        both = halves(inverse)
        inverse = inverse - product(both, halves(product(halves(cross), both)))
        level += 1
    return inverse


def head_params(params_ref, tail, heads, lane):
    softened = tail + params_ref[1:2, :]
    soft = jnp.maximum(softened, 0.0) + jnp.log1p(jnp.exp(-jnp.abs(softened)))
    rate = jnp.where(lane < heads, -jnp.exp(params_ref[0:1, :]) * soft, 0.0)
    return rate, softened


def enter_kernel(
    heads,
    key_dim,
    chained,
    proj_ref,
    edge_ref,
    same_ref,
    taps_ref,
    params_ref,
    conv_ref,
    query_ref,
    key_ref,
    decay_ref,
    gram_ref,
    score_ref,
    inverse_ref,
    from_key_ref,
    from_value_ref,
    carried_ref,
    local_ref,
    offset_ref,
    cols_ref,
    *rest,
):
    ext = rest[-1]
    rows, conv_cols = conv_ref.shape
    query_cols = heads * key_dim
    value_dim = from_value_ref.shape[2]
    ext[0:EDGE, :] = edge_ref[...].astype(jnp.float32)
    ext[EDGE : EDGE + rows, :] = (
        proj_ref[:, 0:conv_cols].astype(jnp.bfloat16).astype(jnp.float32)
    )
    convolved = taps_ref[0:1, :] * ext[EDGE : EDGE + rows, :]
    for lag in range(1, taps_ref.shape[0]):
        convolved = convolved + taps_ref[lag : lag + 1, :] * (
            ext[EDGE - lag : EDGE - lag + rows, :] * same_ref[:, lag : lag + 1]
        )
    conv_ref[...] = convolved
    lane = lax.broadcasted_iota(jnp.int32, (rows, LANES), 1)
    row, col = iotas(rows)
    tail = proj_ref[:, conv_cols + heads * value_dim :]
    rate, _ = head_params(params_ref, tail, heads, lane)
    beta_all = logistic(tail)
    summed_in = rate + in_lane(lane, heads, 1.0 - same_ref[:, 1:2])
    until = jnp.where(col <= row, 1.0, 0.0).astype(jnp.bfloat16)
    total = exact_sum(until, summed_in)
    total_rows = total.T
    counted = total[:, heads : heads + 1]
    same = (jnp.abs(counted - total_rows[heads : heads + 1, :]) < 0.5) & (col <= row)
    strict = same & (col < row)
    first = jnp.where(counted < 0.5, 1.0, 0.0)
    cols = jnp.zeros((rows, LANES), jnp.float32)
    for head in range(heads):
        keys_at = slice(head * key_dim, (head + 1) * key_dim)
        queries = convolved[:, keys_at]
        queries = queries * logistic(queries)
        queries = (
            queries * lax.rsqrt(row_sum(queries * queries) + EPSILON) * key_dim ** (-0.5)
        )
        keys = convolved[:, query_cols + head * key_dim : query_cols + (head + 1) * key_dim]
        keys = keys * logistic(keys)
        keys = keys * lax.rsqrt(row_sum(keys * keys) + EPSILON)
        base = 2 * query_cols + head * value_dim
        values = convolved[:, base : base + value_dim]
        values = values * logistic(values)
        query_ref[:, keys_at] = queries
        key_ref[:, keys_at] = keys
        cumulative = total[:, head : head + 1]
        spread = cumulative - total_rows[head : head + 1, :]
        decay = jnp.where(same, jnp.exp(jnp.where(same, spread, 0.0)), 0.0)
        anchor = jnp.exp(cumulative) * first
        beta = beta_all[:, heads + head : heads + head + 1]
        decay_ref[head] = decay
        key_parts = halves(keys)
        gram = jnp.where(strict, product(key_parts, key_parts, (1, 1)) * decay, 0.0)
        gram_ref[head] = gram
        score = product(halves(queries), key_parts, (1, 1)) * decay
        score_ref[head] = score
        inverse = lower_inverse_of(beta * gram, row, col)
        inverse_ref[head] = inverse
        inverse_parts = halves(inverse)
        from_key = product(inverse_parts, halves((-beta * anchor) * keys))
        from_value = product(inverse_parts, halves(beta * values))
        from_key_ref[head] = from_key
        from_value_ref[head] = from_value
        score_parts = halves(score)
        value_parts = halves(from_value)
        from_key_parts = halves(from_key)
        carried_ref[head] = product(score_parts, from_key_parts) + anchor * queries
        local_ref[head] = product(score_parts, value_parts)
        last_count = counted[rows - 1 : rows, :]
        last_total = cumulative[rows - 1 : rows, :]
        matches = jnp.abs(counted - last_count) < 0.5
        closing = jnp.where(
            matches, jnp.exp(jnp.where(matches, last_total - cumulative, 0.0)), 0.0
        )
        closed = halves(closing * keys)
        offset_ref[head] = product(closed, value_parts, (0, 0))
        if chained:
            transfer_row, transfer_col = iotas(key_dim)
            rest[0][head] = product(closed, from_key_parts, (0, 0)) + jnp.where(
                transfer_row == transfer_col, anchor[rows - 1 : rows, :], 0.0
            )
        cols = (
            cols
            + in_lane(lane, head, anchor)
            + in_lane(lane, heads + head, beta)
            + in_lane(lane, 2 * heads + head, closing)
        )
    cols_ref[...] = cols


def leave_kernel(
    heads,
    carried_ref,
    local_ref,
    initial_ref,
    proj_ref,
    gain_ref,
    y_ref,
    mixed_ref,
):
    rows = y_ref.shape[0]
    value_dim = local_ref.shape[2]
    first_col = proj_ref.shape[1] - LANES - heads * value_dim
    for head in range(heads):
        at = slice(head * value_dim, (head + 1) * value_dim)
        mixed = local_ref[head] + product(
            halves(carried_ref[head]), halves(initial_ref[head])
        )
        mixed_ref[:, at] = mixed
        scale = lax.rsqrt(row_sum(mixed * mixed) / value_dim + EPSILON)
        gate = proj_ref[:, first_col + head * value_dim : first_col + (head + 1) * value_dim]
        y_ref[:, at] = (
            mixed * scale * gain_ref[...] * (gate * logistic(gate))
        ).astype(jnp.bfloat16)


def leave_back_kernel(
    heads,
    d_y_ref,
    mixed_ref,
    proj_ref,
    gain_ref,
    carried_ref,
    d_mixed_ref,
    d_gate_ref,
    d_gain_ref,
    d_initial_ref,
):
    rows = d_y_ref.shape[0]
    value_dim = d_mixed_ref.shape[1] // heads
    first_col = proj_ref.shape[1] - LANES - heads * value_dim
    d_gain = jnp.zeros((1, value_dim), jnp.float32)
    for head in range(heads):
        at = slice(head * value_dim, (head + 1) * value_dim)
        mixed = mixed_ref[:, at]
        scale = lax.rsqrt(row_sum(mixed * mixed) / value_dim + EPSILON)
        normed = mixed * scale
        gate = proj_ref[:, first_col + head * value_dim : first_col + (head + 1) * value_dim]
        sigma = logistic(gate)
        d_y = d_y_ref[:, at]
        d_gain = d_gain + jnp.sum(d_y * normed * (gate * sigma), axis=0, keepdims=True)
        scaled = d_y * gain_ref[...]
        d_gate_ref[:, at] = (
            scaled * normed * (sigma * (1.0 + gate * (1.0 - sigma)))
        ).astype(jnp.bfloat16)
        d_normed = scaled * (gate * sigma)
        d_mixed = scale * (d_normed - normed * (row_sum(d_normed * normed) / value_dim))
        d_mixed_ref[:, at] = d_mixed
        d_initial_ref[head] = product(
            halves(carried_ref[head]), halves(d_mixed), (0, 0)
        )
    d_gain_ref[...] = jnp.broadcast_to(d_gain, d_gain_ref.shape)


def enter_back_kernel(
    heads,
    key_dim,
    d_mixed_ref,
    d_gate_ref,
    d_end_ref,
    initial_ref,
    proj_ref,
    edge_ref,
    same_ref,
    taps_ref,
    params_ref,
    conv_ref,
    query_ref,
    key_ref,
    decay_ref,
    gram_ref,
    score_ref,
    inverse_ref,
    from_key_ref,
    from_value_ref,
    cols_ref,
    d_proj_ref,
    d_last_ref,
    d_edge_ref,
    d_taps_ref,
    d_params_ref,
    ext,
    d_ext,
):
    rows, conv_cols = conv_ref.shape
    query_cols = heads * key_dim
    value_dim = from_value_ref.shape[2]
    value_cols = heads * value_dim
    margin = taps_ref.shape[0]
    lane = lax.broadcasted_iota(jnp.int32, (rows, LANES), 1)
    row, col = iotas(rows)
    last_row = lax.broadcasted_iota(jnp.int32, (rows, 1), 0) == rows - 1
    d_total = jnp.zeros((rows, LANES), jnp.float32)
    d_tail = jnp.zeros((rows, LANES), jnp.float32)
    d_active = []
    for head in range(heads):
        keys_at = slice(head * key_dim, (head + 1) * key_dim)
        queries, keys = query_ref[:, keys_at], key_ref[:, keys_at]
        base = 2 * query_cols + head * value_dim
        values = conv_ref[:, base : base + value_dim]
        values = values * logistic(values)
        anchor = cols_ref[:, head : head + 1]
        beta = cols_ref[:, heads + head : heads + head + 1]
        closing = cols_ref[:, 2 * heads + head : 2 * heads + head + 1]
        decay, gram, score = decay_ref[head], gram_ref[head], score_ref[head]
        initial = initial_ref[head]
        d_end = d_end_ref[head]
        d_mixed = d_mixed_ref[:, head * value_dim : (head + 1) * value_dim]
        initial_parts, end_parts = halves(initial), halves(d_end)
        mixed_parts = halves(d_mixed)
        key_parts, query_parts = halves(keys), halves(queries)
        updates = from_value_ref[head] + product(halves(from_key_ref[head]), initial_parts)
        update_parts = halves(updates)
        key_state = product(key_parts, initial_parts)
        query_state = product(query_parts, initial_parts)
        d_updates = product(halves(score), mixed_parts, (0, 0)) + product(
            halves(closing * keys), end_parts
        )
        d_target = product(halves(inverse_ref[head]), halves(d_updates), (0, 0))
        d_delta = beta * d_target
        delta = values - anchor * key_state
        d_lower = -product(halves(d_target), update_parts, (1, 1))
        d_score = product(mixed_parts, update_parts, (1, 1))
        d_pair = halves(d_score * decay)
        d_lower_gram = d_lower * gram
        d_beta = row_sum(d_target * delta) + row_sum(d_lower_gram)
        d_gram = halves(jnp.where(col < row, d_lower * (beta * decay), 0.0))
        back = halves(anchor * d_delta)
        d_query = product(d_pair, key_parts) + anchor * product(
            mixed_parts, initial_parts, (1, 1)
        )
        d_closed = product(update_parts, end_parts, (1, 1))
        d_key = (
            product(d_pair, query_parts, (0, 0))
            + product(d_gram, key_parts)
            + product(d_gram, key_parts, (0, 0))
            + closing * d_closed
            - product(back, initial_parts, (1, 1))
        )
        d_anchor = row_sum(d_mixed * query_state) - row_sum(d_delta * key_state)
        d_anchor = d_anchor + jnp.where(last_row, jnp.sum(d_end * initial), 0.0)
        d_closing = closing * row_sum(keys * d_closed)
        flow = d_score * score + beta * d_lower_gram
        into = jnp.broadcast_to(jnp.sum(flow, axis=0, keepdims=True), (LANES, rows)).T
        d_cumulative = row_sum(flow) - into[:, 0:1] + anchor * d_anchor - d_closing
        d_cumulative = d_cumulative + jnp.where(last_row, jnp.sum(d_closing), 0.0)
        d_total = d_total + in_lane(lane, head, d_cumulative)
        d_tail = d_tail + in_lane(lane, heads + head, d_beta * beta * (1.0 - beta))
        raw_query = conv_ref[:, keys_at]
        raw_key = conv_ref[:, query_cols + head * key_dim : query_cols + (head + 1) * key_dim]
        query_sigma, key_sigma = logistic(raw_query), logistic(raw_key)
        active = raw_query * query_sigma
        scale = lax.rsqrt(row_sum(active * active) + EPSILON)
        unit = active * scale
        d_unit = d_query * key_dim ** (-0.5)
        d_raw_query = (
            scale
            * (d_unit - unit * row_sum(d_unit * unit))
            * (query_sigma * (1.0 + raw_query * (1.0 - query_sigma)))
        )
        active = raw_key * key_sigma
        scale = lax.rsqrt(row_sum(active * active) + EPSILON)
        d_raw_key = (
            scale
            * (d_key - keys * row_sum(d_key * keys))
            * (key_sigma * (1.0 + raw_key * (1.0 - key_sigma)))
        )
        raw_value = conv_ref[:, base : base + value_dim]
        value_sigma = logistic(raw_value)
        d_raw_value = d_delta * (value_sigma * (1.0 + raw_value * (1.0 - value_sigma)))
        d_active.append((d_raw_query, d_raw_key, d_raw_value))
    tail = proj_ref[:, conv_cols + value_cols :]
    rate, softened = head_params(params_ref, tail, heads, lane)
    since = jnp.where(col >= row, 1.0, 0.0).astype(jnp.bfloat16)
    d_rate = exact_sum(since, d_total)
    d_decay = jnp.where(
        lane < heads, d_rate * (-jnp.exp(params_ref[0:1, :])) * logistic(softened), 0.0
    )
    d_params_ref[0:1, :] = jnp.sum(d_rate * rate, axis=0, keepdims=True)
    d_params_ref[1:2, :] = jnp.sum(d_decay, axis=0, keepdims=True)
    d_params_ref[2:, :] = jnp.zeros((d_params_ref.shape[0] - 2, LANES), jnp.float32)
    d_proj_ref[:, conv_cols + value_cols :] = (d_decay + d_tail).astype(jnp.bfloat16)
    d_proj_ref[:, conv_cols : conv_cols + value_cols] = d_gate_ref[...]
    d_convolved = jnp.concatenate(
        [part[0] for part in d_active]
        + [part[1] for part in d_active]
        + [part[2] for part in d_active],
        axis=1,
    )
    ext[0:EDGE, :] = edge_ref[...].astype(jnp.float32)
    ext[EDGE : EDGE + rows, :] = (
        proj_ref[:, 0:conv_cols].astype(jnp.bfloat16).astype(jnp.float32)
    )
    zeros = jnp.zeros((EDGE, conv_cols), jnp.float32)
    d_ext[0:EDGE, :] = zeros
    d_ext[EDGE + rows :, :] = zeros
    d_taps_ref[...] = jnp.zeros(d_taps_ref.shape, jnp.float32)
    d_taps_ref[0:1, :] = jnp.sum(
        d_convolved * ext[EDGE : EDGE + rows, :], axis=0, keepdims=True
    )
    d_pre = taps_ref[0:1, :] * d_convolved
    d_edge = zeros
    for lag in range(1, margin):
        kept = d_convolved * same_ref[:, lag : lag + 1]
        d_taps_ref[lag : lag + 1, :] = jnp.sum(
            kept * ext[EDGE - lag : EDGE - lag + rows, :], axis=0, keepdims=True
        )
        d_ext[EDGE : EDGE + rows, :] = kept
        weight = taps_ref[lag : lag + 1, :]
        d_pre = d_pre + weight * d_ext[EDGE + lag : EDGE + lag + rows, :]
        d_edge = d_edge + weight * d_ext[lag : lag + EDGE, :]
    d_proj_ref[:, 0:conv_cols] = d_pre.astype(jnp.bfloat16)
    d_last_ref[...] = d_pre[rows - EDGE :, :]
    d_edge_ref[...] = d_edge


VMEM_MOST = 40 * 1024 * 1024


def on_core(kernel, name, shapes, scratch=()):
    return pl.pallas_call(
        kernel,
        out_shape=[jax.ShapeDtypeStruct(shape, dtype) for shape, dtype in shapes],
        scratch_shapes=[pltpu.VMEM(shape, dtype) for shape, dtype in scratch],
        compiler_params=pltpu.CompilerParams(vmem_limit_bytes=VMEM_MOST),
        name=name,
    )


def apply_map(matrix, addend, incoming):
    return jnp.einsum("hde,hew->hdw", matrix, incoming, precision=HIGHEST) + addend


def local(
    tokens,
    segments,
    cotangent,
    mixer_gain,
    mlp_gain,
    query_weight,
    key_weight,
    value_weight,
    gate_weight,
    decay_weight,
    beta_weight,
    output_weight,
    conv_query,
    conv_key,
    conv_value,
    decay_log,
    decay_bias,
    head_gain,
    hidden_gate,
    hidden_up,
    hidden_down,
):
    width = tokens.shape[-1]
    inputs = tokens.reshape(-1, width).astype(jnp.float32)
    row_count = inputs.shape[0]
    query_cols = query_weight.shape[1]
    value_cols = value_weight.shape[1]
    head_count = decay_weight.shape[1]
    ff_cols = hidden_gate.shape[1]
    axes = ("dp", "ctx")
    used = 2 * query_cols + 2 * value_cols + 2 * head_count + 2
    pad_cols = -used % LANES
    own_rows = query_weight.shape[0]
    in_weights = lax.all_gather(
        jnp.concatenate(
            [
                query_weight,
                key_weight,
                value_weight,
                gate_weight,
                decay_weight,
                beta_weight,
                mixer_gain[:, None],
                mlp_gain[:, None],
                jnp.zeros((own_rows, pad_cols), jnp.bfloat16),
            ],
            1,
        ),
        axes,
        axis=0,
        tiled=True,
    )
    full_output = lax.all_gather(output_weight, axes, axis=0, tiled=True)
    full_gate_up = lax.all_gather(
        jnp.concatenate([hidden_gate, hidden_up], 1), axes, axis=0, tiled=True
    )
    full_hidden_down = lax.all_gather(hidden_down, axes, axis=0, tiled=True)
    gain_one = in_weights[:, used - 2].astype(jnp.float32)
    gain_two = in_weights[:, used - 1].astype(jnp.float32)
    conv_cols = 2 * query_cols + value_cols
    key_dim = query_cols // head_count
    rms_one = lax.rsqrt(jnp.mean(inputs * inputs, -1, keepdims=True) + EPSILON)
    normed_one = inputs * rms_one
    hidden_one = (normed_one * gain_one).astype(jnp.bfloat16)
    projected = jnp.dot(hidden_one, in_weights, preferred_element_type=jnp.float32)
    conv_weight = jnp.concatenate([conv_query, conv_key, conv_value], 1)
    taps = conv_weight.shape[0]
    margin = taps - 1
    last_rows = projected[row_count - EDGE :, :conv_cols].astype(jnp.bfloat16)
    edge_rows = passed_along(last_rows, "ctx", 1)
    seg_padded = jnp.concatenate([jnp.full((margin,), -1, jnp.int32), segments.reshape(-1)], 0)
    seg_ext = lax.dynamic_slice_in_dim(
        seg_padded, lax.axis_index("ctx") * row_count, row_count + margin
    )
    same_doc = jnp.stack(
        [
            (seg_ext[margin - lag : margin - lag + row_count] == seg_ext[margin:])
            for lag in range(taps)
        ],
        1,
    ).astype(jnp.float32)
    lane_pad = (0, LANES - head_count)
    params = jnp.stack([jnp.pad(decay_log, lane_pad), jnp.pad(decay_bias, lane_pad)])
    value_dim = value_cols // head_count
    ctx_size = lax.axis_size("ctx")
    chained = ctx_size > 2
    square = ((head_count, row_count, row_count), jnp.float32)
    tall_key = ((head_count, row_count, key_dim), jnp.float32)
    tall_value = ((head_count, row_count, value_dim), jnp.float32)
    flat_key = ((row_count, query_cols), jnp.float32)
    state = ((head_count, key_dim, value_dim), jnp.float32)
    entered = on_core(
        partial(enter_kernel, head_count, key_dim, chained),
        "mixer_enter",
        [
            ((row_count, conv_cols), jnp.float32),
            flat_key,
            flat_key,
            square,
            square,
            square,
            square,
            tall_key,
            tall_value,
            tall_key,
            tall_value,
            state,
            ((row_count, LANES), jnp.float32),
        ]
        + ([((head_count, key_dim, key_dim), jnp.float32)] if chained else []),
        [((EDGE + row_count, conv_cols), jnp.float32)],
    )(projected, edge_rows, same_doc, conv_weight, params)
    convolved, queries, key_rows, decay_pair, gram, score, inverse = entered[:7]
    from_key, from_value, carried, local_out, offset, mixer_cols = entered[7:13]

    initial = jnp.zeros_like(offset)
    for hop in range(ctx_size - 1):
        leaving = offset if hop == 0 else apply_map(entered[13], offset, initial)
        initial = passed_along(leaving, "ctx", 1)
    gain_row = head_gain[None, :]
    mixed_b, mixed = on_core(
        partial(leave_kernel, head_count),
        "mixer_leave",
        [((row_count, value_cols), jnp.bfloat16), ((row_count, value_cols), jnp.float32)],
    )(carried, local_out, initial, projected, gain_row)
    mixer_part = jnp.einsum("rc,dc->rd", mixed_b, full_output, preferred_element_type=jnp.float32)
    attention = summed(mixer_part.astype(jnp.bfloat16), "tp", 0).astype(jnp.float32)
    middle = inputs + attention
    rms_two = lax.rsqrt(jnp.mean(middle * middle, -1, keepdims=True) + EPSILON)
    normed_two = middle * rms_two
    hidden_two = (normed_two * gain_two).astype(jnp.bfloat16)
    gate_up = jnp.dot(hidden_two, full_gate_up, preferred_element_type=jnp.float32)
    gate_pre = gate_up[:, :ff_cols]
    up_pre = gate_up[:, ff_cols:]
    sigma = jax.nn.sigmoid(gate_pre)
    swish = gate_pre * sigma
    activ = (swish * up_pre).astype(jnp.bfloat16)
    feed_part = jnp.einsum("rf,df->rd", activ, full_hidden_down, preferred_element_type=jnp.float32)
    grad_rows = cotangent.reshape(-1, width)
    grad_out = grad_rows.astype(jnp.float32)
    d_activ = jnp.dot(grad_rows, full_hidden_down, preferred_element_type=jnp.float32)
    d_gate_pre = (d_activ * up_pre * sigma * (1.0 + gate_pre * (1.0 - sigma))).astype(jnp.bfloat16)
    d_up_pre = (d_activ * swish).astype(jnp.bfloat16)
    grad_down = jnp.einsum("rd,rf->df", grad_rows, activ, preferred_element_type=jnp.float32)
    d_gate_up = jnp.concatenate([d_gate_pre, d_up_pre], 1)
    grad_gate_up = jnp.einsum(
        "rd,rf->df", hidden_two, d_gate_up, preferred_element_type=jnp.float32
    )
    two_part = jnp.einsum("rf,df->rd", d_gate_up, full_gate_up, preferred_element_type=jnp.float32)
    both = summed(jnp.concatenate([two_part, feed_part], 0).astype(jnp.bfloat16), "tp", 1)
    d_hidden_two = both[:row_count].astype(jnp.float32)
    feed = both[row_count:].astype(jnp.float32)
    block_out = (middle + feed).astype(jnp.bfloat16).reshape(tokens.shape)

    def scattered(member):
        total = lax.psum_scatter(
            member.astype(jnp.bfloat16), axes, scatter_dimension=0, tiled=True
        )
        return total.astype(jnp.float32)

    down_own = scattered(grad_down)
    gate_up_own = scattered(grad_gate_up)
    grad_gain_two = jnp.sum(d_hidden_two * normed_two, 0)
    dn_two = d_hidden_two * gain_two
    d_middle = grad_out + rms_two * (
        dn_two - normed_two * jnp.mean(dn_two * normed_two, -1, keepdims=True)
    )
    d_middle_b = d_middle.astype(jnp.bfloat16)
    d_mixed = jnp.dot(d_middle_b, full_output, preferred_element_type=jnp.float32)
    grad_output = jnp.einsum("rd,rc->dc", d_middle_b, mixed_b, preferred_element_type=jnp.float32)
    d_out, d_gate, d_head, init_grad = on_core(
        partial(leave_back_kernel, head_count),
        "mixer_leave_back",
        [
            ((row_count, value_cols), jnp.float32),
            ((row_count, value_cols), jnp.bfloat16),
            ((8, value_dim), jnp.float32),
            state,
        ],
    )(d_mixed, mixed, projected, gain_row, carried)
    d_head = d_head[0]
    end_grad = jnp.zeros_like(offset)
    for hop in range(ctx_size - 1):
        leaving = (
            init_grad
            if hop == 0
            else apply_map(jnp.swapaxes(entered[13], 1, 2), init_grad, end_grad)
        )
        end_grad = passed_along(leaving, "ctx", -1)
    edge_shape = ((EDGE, conv_cols), jnp.float32)
    d_proj, d_last, d_edge, d_conv, d_params = on_core(
        partial(enter_back_kernel, head_count, key_dim),
        "mixer_enter_back",
        [
            (projected.shape, jnp.bfloat16),
            edge_shape,
            edge_shape,
            ((8, conv_cols), jnp.float32),
            ((8, LANES), jnp.float32),
        ],
        [
            ((EDGE + row_count, conv_cols), jnp.float32),
            ((2 * EDGE + row_count, conv_cols), jnp.float32),
        ],
    )(
        d_out,
        d_gate,
        end_grad,
        initial,
        projected,
        edge_rows,
        same_doc,
        conv_weight,
        params,
        convolved,
        queries,
        key_rows,
        decay_pair,
        gram,
        score,
        inverse,
        from_key,
        from_value,
        mixer_cols,
    )
    d_conv = d_conv[:taps]
    d_log, d_bias = d_params[0, :head_count], d_params[1, :head_count]
    edge_back = passed_along(d_edge, "ctx", -1)
    d_proj = lax.dynamic_update_slice(
        d_proj, (d_last + edge_back).astype(jnp.bfloat16), (row_count - EDGE, 0)
    )
    grad_input = jnp.einsum("rd,rc->dc", hidden_one, d_proj, preferred_element_type=jnp.float32)
    one_part = jnp.einsum("rc,dc->rd", d_proj, in_weights, preferred_element_type=jnp.float32)
    one_part, down_own = lax.optimization_barrier((one_part, down_own))
    one_sum = summed(one_part.astype(jnp.bfloat16), "tp", 2)
    one_sum, gate_up_own = lax.optimization_barrier((one_sum, gate_up_own))
    d_hidden_one = one_sum.astype(jnp.float32)
    grad_gain_one = jnp.sum(d_hidden_one * normed_one, 0)
    dn_one = d_hidden_one * gain_one
    tokens_grad = d_middle + rms_one * (
        dn_one - normed_one * jnp.mean(dn_one * normed_one, -1, keepdims=True)
    )
    tokens_grad = tokens_grad.reshape(tokens.shape)
    edges = [
        0,
        query_cols,
        2 * query_cols,
        conv_cols,
        conv_cols + value_cols,
        conv_cols + value_cols + head_count,
        conv_cols + value_cols + 2 * head_count,
    ]

    column = jnp.arange(grad_input.shape[1])[None, :]
    grad_input = jnp.where(column == used - 2, grad_gain_one[:, None], grad_input)
    grad_input = jnp.where(column == used - 1, grad_gain_two[:, None], grad_input)
    output_own = scattered(grad_output)
    input_own = scattered(grad_input)
    reduced = (
        input_own[:, used - 2],
        input_own[:, used - 1],
        *(input_own[:, edges[i] : edges[i + 1]] for i in range(6)),
        output_own,
        gate_up_own[:, :ff_cols],
        gate_up_own[:, ff_cols:],
        down_own,
    )
    conv_width = d_conv.shape[1]
    rest = jnp.concatenate([d_head, d_log, d_bias])
    pad_row = jnp.zeros((-rest.shape[0] % conv_width,), jnp.float32)
    rest = jnp.concatenate([rest, pad_row]).reshape(-1, conv_width)
    packed = jnp.concatenate([d_conv, rest], 0)
    lines = packed.shape[0]
    packed = jnp.concatenate([packed, jnp.zeros((-lines % 8, conv_width), jnp.float32)], 0)
    packed = small_sum(packed, ("dp", "ctx"), 3)
    conv_total = packed[:taps]
    rest = packed[taps:lines].reshape(-1)
    log_total = rest[value_dim : value_dim + head_count]
    bias_total = rest[value_dim + head_count : value_dim + 2 * head_count]
    head_total = small_sum(
        jnp.broadcast_to(rest[None, :value_dim], (8, value_dim)), ("tp",), 4
    )[0]
    return (
        block_out,
        tokens_grad,
        reduced[0],
        reduced[1],
        reduced[2],
        reduced[3],
        reduced[4],
        reduced[5],
        reduced[6],
        reduced[7],
        reduced[8],
        conv_total[:, :query_cols],
        conv_total[:, query_cols : 2 * query_cols],
        conv_total[:, 2 * query_cols :],
        log_total,
        bias_total,
        head_total,
        reduced[9],
        reduced[10],
        reduced[11],
    )


def solution(mesh):
    return jax.shard_map(
        local,
        mesh=mesh,
        in_specs=(
            P("dp", "ctx", None),
            P("dp", None),
            P("dp", "ctx", None),
            P(("dp", "ctx")),
            P(("dp", "ctx")),
            P(("dp", "ctx"), "tp"),
            P(("dp", "ctx"), "tp"),
            P(("dp", "ctx"), "tp"),
            P(("dp", "ctx"), "tp"),
            P(("dp", "ctx"), "tp"),
            P(("dp", "ctx"), "tp"),
            P(("dp", "ctx"), "tp"),
            P(None, "tp"),
            P(None, "tp"),
            P(None, "tp"),
            P("tp"),
            P("tp"),
            P(),
            P(("dp", "ctx"), "tp"),
            P(("dp", "ctx"), "tp"),
            P(("dp", "ctx"), "tp"),
        ),
        out_specs=(
            P("dp", "ctx", None),
            P("dp", "ctx", None),
            P(("dp", "ctx")),
            P(("dp", "ctx")),
            P(("dp", "ctx"), "tp"),
            P(("dp", "ctx"), "tp"),
            P(("dp", "ctx"), "tp"),
            P(("dp", "ctx"), "tp"),
            P(("dp", "ctx"), "tp"),
            P(("dp", "ctx"), "tp"),
            P(("dp", "ctx"), "tp"),
            P(None, "tp"),
            P(None, "tp"),
            P(None, "tp"),
            P("tp"),
            P("tp"),
            P(),
            P(("dp", "ctx"), "tp"),
            P(("dp", "ctx"), "tp"),
            P(("dp", "ctx"), "tp"),
        ),
        check_vma=False,
    )
```

```python
from functools import partial

import jax
import jax.numpy as jnp
from jax import lax
from jax.experimental import pallas as pl
from jax.experimental.pallas import tpu as pltpu
from jax.sharding import PartitionSpec as P

EPSILON = 1e-06
HIGHEST = lax.Precision.HIGHEST
LANES = 128


def peer_of(axes, sizes, distance):
    flat = 0
    total = 1
    for axis, size in zip(axes, sizes):
        flat = flat * size + lax.axis_index(axis)
        total = total * size
    other = lax.rem(flat + distance, total)
    where = {}
    for axis, size in reversed(list(zip(axes, sizes))):
        where[axis] = lax.rem(other, size)
        other = other // size
    return where


def greet(axes, sizes, peers):
    barrier = pltpu.get_barrier_semaphore()
    for distance in range(1, peers + 1):
        pl.semaphore_signal(
            barrier,
            inc=1,
            device_id=peer_of(axes, sizes, distance),
            device_id_type=pl.DeviceIdType.MESH,
        )
    pl.semaphore_wait(barrier, peers)


def sum_kernel(axis, size, x_ref, out_ref, parts, mine, got, send, recv, send_two, recv_two):
    peers = size - 1
    me = lax.axis_index(axis)
    rows = x_ref.shape[0] // size
    greet((axis,), (size,), peers)

    def block(index):
        return pl.ds(pl.multiple_of(index * rows, rows), rows)

    copies = []
    for distance in range(1, size):
        other = lax.rem(me + distance, size)
        copy = pltpu.make_async_remote_copy(
            src_ref=x_ref.at[block(other)],
            dst_ref=parts.at[distance - 1],
            send_sem=send.at[distance - 1],
            recv_sem=recv.at[distance - 1],
            device_id={axis: other},
            device_id_type=pl.DeviceIdType.MESH,
        )
        copy.start()
        copies.append(copy)
    total = x_ref[block(me)].astype(jnp.float32)
    for distance in range(1, size):
        copies[distance - 1].wait_recv()
        total = total + parts[distance - 1].astype(jnp.float32)
    total = total.astype(out_ref.dtype)
    mine[...] = total
    out_ref[block(me)] = total
    more = []
    for distance in range(1, size):
        copy = pltpu.make_async_remote_copy(
            src_ref=mine,
            dst_ref=got.at[distance - 1],
            send_sem=send_two.at[distance - 1],
            recv_sem=recv_two.at[distance - 1],
            device_id={axis: lax.rem(me + distance, size)},
            device_id_type=pl.DeviceIdType.MESH,
        )
        copy.start()
        more.append(copy)
    for distance in range(1, size):
        more[distance - 1].wait_recv()
        out_ref[block(lax.rem(me + size - distance, size))] = got[distance - 1]
    for copy in copies + more:
        copy.wait_send()


def summed(value, axis, call):
    size = lax.axis_size(axis)
    if size == 1:
        return value
    rows, cols = value.shape
    if size == 4 and rows % 128 == 0:
        return line_summed(value, axis, call, 4)
    piece = (size - 1, rows // size, cols)
    sems = pltpu.SemaphoreType.DMA((size - 1,))
    return pl.pallas_call(
        partial(sum_kernel, axis, size),
        out_shape=jax.ShapeDtypeStruct(value.shape, value.dtype),
        in_specs=[pl.BlockSpec(memory_space=pltpu.VMEM)],
        out_specs=pl.BlockSpec(memory_space=pltpu.VMEM),
        scratch_shapes=[
            pltpu.VMEM(piece, value.dtype),
            pltpu.VMEM(piece[1:], value.dtype),
            pltpu.VMEM(piece, value.dtype),
            sems,
            sems,
            sems,
            sems,
        ],
        cost_estimate=pl.CostEstimate(
            flops=value.size * 40000, bytes_accessed=value.size * 300, transcendentals=0
        ),
        compiler_params=pltpu.CompilerParams(collective_id=call, has_side_effects=True),
        name=f"tp_sum_{call}",
    )(value)


def small_kernel(axes, sizes, peers, x_ref, out_ref, parts, send, recv):
    greet(axes, sizes, peers)
    copies = []
    for distance in range(1, peers + 1):
        copy = pltpu.make_async_remote_copy(
            src_ref=x_ref,
            dst_ref=parts.at[distance - 1],
            send_sem=send.at[distance - 1],
            recv_sem=recv.at[distance - 1],
            device_id=peer_of(axes, sizes, distance),
            device_id_type=pl.DeviceIdType.MESH,
        )
        copy.start()
        copies.append(copy)
    flat = 0
    for axis, size in zip(axes, sizes):
        flat = flat * size + lax.axis_index(axis)
    for copy in copies:
        copy.wait()
    parts[peers] = x_ref[...]
    total = jnp.zeros(x_ref.shape, jnp.float32)
    for owner in range(peers + 1):
        slot = lax.rem(flat + 2 * (peers + 1) - owner - 1, peers + 1)
        total = total + parts[slot]
    out_ref[...] = total


def small_sum(value, axes, call):
    sizes = tuple(lax.axis_size(axis) for axis in axes)
    peers = 1
    for size in sizes:
        peers = peers * size
    peers = peers - 1
    if peers == 0:
        return value
    return pl.pallas_call(
        partial(small_kernel, axes, sizes, peers),
        out_shape=jax.ShapeDtypeStruct(value.shape, value.dtype),
        in_specs=[pl.BlockSpec(memory_space=pltpu.VMEM)],
        out_specs=pl.BlockSpec(memory_space=pltpu.VMEM),
        scratch_shapes=[
            pltpu.VMEM((peers + 1,) + value.shape, value.dtype),
            pltpu.SemaphoreType.DMA((peers,)),
            pltpu.SemaphoreType.DMA((peers,)),
        ],
        cost_estimate=pl.CostEstimate(
            flops=1000000, bytes_accessed=20000000, transcendentals=0
        ),
        compiler_params=pltpu.CompilerParams(collective_id=call, has_side_effects=True),
        name=f"small_sum_{call}",
    )(value)


def passed_along(value, axis, by):
    devices = lax.axis_size(axis)
    pairs = [(i, i + by) for i in range(devices) if 0 <= i + by < devices]
    return lax.ppermute(value, axis, pairs)


EDGE = 16


def halves(value):
    high = value.astype(jnp.bfloat16)
    low = (value - high.astype(jnp.float32)).astype(jnp.bfloat16)
    return high, low


def product(left, right, over=(1, 0)):
    dims = (((over[0],), (over[1],)), ((), ()))

    def one(a, b):
        return lax.dot_general(a, b, dims, preferred_element_type=jnp.float32)

    return one(left[0], right[0]) + (one(left[0], right[1]) + one(left[1], right[0]))


def exact_sum(ones, value, over=(1, 0)):
    dims = (((over[0],), (over[1],)), ((), ()))
    high = value.astype(jnp.bfloat16)
    rest = value - high.astype(jnp.float32)
    middle = rest.astype(jnp.bfloat16)
    low = (rest - middle.astype(jnp.float32)).astype(jnp.bfloat16)
    total = None
    for part in (low, middle, high):
        term = lax.dot_general(ones, part, dims, preferred_element_type=jnp.float32)
        total = term if total is None else total + term
    return total


def logistic(value):
    return 1.0 / (1.0 + jnp.exp(-value))


def row_sum(value):
    return jnp.sum(value, axis=1, keepdims=True)


def iotas(count):
    row = lax.broadcasted_iota(jnp.int32, (count, count), 0)
    col = lax.broadcasted_iota(jnp.int32, (count, count), 1)
    return row, col


def in_lane(lane, index, column):
    return jnp.where(lane == index, column, 0.0)


def lower_inverse_of(lower, row, col):
    order = lower.shape[0]
    apart = row ^ col
    inverse = jnp.where(row == col, 1.0, 0.0) - jnp.where(apart == 1, lower, 0.0)
    level = 1
    while (1 << level) < order:
        cross = jnp.where((apart >> level) == 1, lower, 0.0)
        both = halves(inverse)
        inverse = inverse - product(both, halves(product(halves(cross), both)))
        level += 1
    return inverse


def head_params(params_ref, tail, heads, lane):
    softened = tail + params_ref[1:2, :]
    soft = jnp.maximum(softened, 0.0) + jnp.log1p(jnp.exp(-jnp.abs(softened)))
    rate = jnp.where(lane < heads, -jnp.exp(params_ref[0:1, :]) * soft, 0.0)
    return rate, softened


def enter_kernel(
    heads,
    key_dim,
    chained,
    proj_ref,
    edge_ref,
    same_ref,
    taps_ref,
    params_ref,
    conv_ref,
    query_ref,
    key_ref,
    decay_ref,
    gram_ref,
    score_ref,
    inverse_ref,
    from_key_ref,
    from_value_ref,
    carried_ref,
    local_ref,
    offset_ref,
    cols_ref,
    *rest,
):
    ext = rest[-1]
    rows, conv_cols = conv_ref.shape
    query_cols = heads * key_dim
    value_dim = from_value_ref.shape[2]
    ext[0:EDGE, :] = edge_ref[...].astype(jnp.float32)
    ext[EDGE : EDGE + rows, :] = (
        proj_ref[:, 0:conv_cols].astype(jnp.bfloat16).astype(jnp.float32)
    )
    convolved = taps_ref[0:1, :] * ext[EDGE : EDGE + rows, :]
    for lag in range(1, taps_ref.shape[0]):
        convolved = convolved + taps_ref[lag : lag + 1, :] * (
            ext[EDGE - lag : EDGE - lag + rows, :] * same_ref[:, lag : lag + 1]
        )
    conv_ref[...] = convolved
    lane = lax.broadcasted_iota(jnp.int32, (rows, LANES), 1)
    row, col = iotas(rows)
    tail = proj_ref[:, conv_cols + heads * value_dim :]
    rate, _ = head_params(params_ref, tail, heads, lane)
    beta_all = logistic(tail)
    summed_in = rate + in_lane(lane, heads, 1.0 - same_ref[:, 1:2])
    until = jnp.where(col <= row, 1.0, 0.0).astype(jnp.bfloat16)
    total = exact_sum(until, summed_in)
    total_rows = total.T
    counted = total[:, heads : heads + 1]
    same = (jnp.abs(counted - total_rows[heads : heads + 1, :]) < 0.5) & (col <= row)
    strict = same & (col < row)
    first = jnp.where(counted < 0.5, 1.0, 0.0)
    cols = jnp.zeros((rows, LANES), jnp.float32)
    for head in range(heads):
        keys_at = slice(head * key_dim, (head + 1) * key_dim)
        queries = convolved[:, keys_at]
        queries = queries * logistic(queries)
        queries = (
            queries * lax.rsqrt(row_sum(queries * queries) + EPSILON) * key_dim ** (-0.5)
        )
        keys = convolved[:, query_cols + head * key_dim : query_cols + (head + 1) * key_dim]
        keys = keys * logistic(keys)
        keys = keys * lax.rsqrt(row_sum(keys * keys) + EPSILON)
        base = 2 * query_cols + head * value_dim
        values = convolved[:, base : base + value_dim]
        values = values * logistic(values)
        query_ref[:, keys_at] = queries
        key_ref[:, keys_at] = keys
        cumulative = total[:, head : head + 1]
        spread = cumulative - total_rows[head : head + 1, :]
        decay = jnp.where(same, jnp.exp(jnp.where(same, spread, 0.0)), 0.0)
        anchor = jnp.exp(cumulative) * first
        beta = beta_all[:, heads + head : heads + head + 1]
        decay_ref[head] = decay
        key_parts = halves(keys)
        gram = jnp.where(strict, product(key_parts, key_parts, (1, 1)) * decay, 0.0)
        gram_ref[head] = gram
        score = product(halves(queries), key_parts, (1, 1)) * decay
        score_ref[head] = score
        inverse = lower_inverse_of(beta * gram, row, col)
        inverse_ref[head] = inverse
        inverse_parts = halves(inverse)
        from_key = product(inverse_parts, halves((-beta * anchor) * keys))
        from_value = product(inverse_parts, halves(beta * values))
        from_key_ref[head] = from_key
        from_value_ref[head] = from_value
        score_parts = halves(score)
        value_parts = halves(from_value)
        from_key_parts = halves(from_key)
        carried_ref[head] = product(score_parts, from_key_parts) + anchor * queries
        local_ref[head] = product(score_parts, value_parts)
        last_count = counted[rows - 1 : rows, :]
        last_total = cumulative[rows - 1 : rows, :]
        matches = jnp.abs(counted - last_count) < 0.5
        closing = jnp.where(
            matches, jnp.exp(jnp.where(matches, last_total - cumulative, 0.0)), 0.0
        )
        closed = halves(closing * keys)
        offset_ref[head] = product(closed, value_parts, (0, 0))
        if chained:
            transfer_row, transfer_col = iotas(key_dim)
            rest[0][head] = product(closed, from_key_parts, (0, 0)) + jnp.where(
                transfer_row == transfer_col, anchor[rows - 1 : rows, :], 0.0
            )
        cols = (
            cols
            + in_lane(lane, head, anchor)
            + in_lane(lane, heads + head, beta)
            + in_lane(lane, 2 * heads + head, closing)
        )
    cols_ref[...] = cols


def leave_kernel(
    heads,
    carried_ref,
    local_ref,
    initial_ref,
    proj_ref,
    gain_ref,
    y_ref,
    mixed_ref,
):
    rows = y_ref.shape[0]
    value_dim = local_ref.shape[2]
    first_col = proj_ref.shape[1] - LANES - heads * value_dim
    for head in range(heads):
        at = slice(head * value_dim, (head + 1) * value_dim)
        mixed = local_ref[head] + product(
            halves(carried_ref[head]), halves(initial_ref[head])
        )
        mixed_ref[:, at] = mixed
        scale = lax.rsqrt(row_sum(mixed * mixed) / value_dim + EPSILON)
        gate = proj_ref[:, first_col + head * value_dim : first_col + (head + 1) * value_dim]
        y_ref[:, at] = (
            mixed * scale * gain_ref[...] * (gate * logistic(gate))
        ).astype(jnp.bfloat16)


def leave_back_kernel(
    heads,
    d_y_ref,
    mixed_ref,
    proj_ref,
    gain_ref,
    carried_ref,
    d_mixed_ref,
    d_gate_ref,
    d_gain_ref,
    d_initial_ref,
):
    rows = d_y_ref.shape[0]
    value_dim = d_mixed_ref.shape[1] // heads
    first_col = proj_ref.shape[1] - LANES - heads * value_dim
    d_gain = jnp.zeros((1, value_dim), jnp.float32)
    for head in range(heads):
        at = slice(head * value_dim, (head + 1) * value_dim)
        mixed = mixed_ref[:, at]
        scale = lax.rsqrt(row_sum(mixed * mixed) / value_dim + EPSILON)
        normed = mixed * scale
        gate = proj_ref[:, first_col + head * value_dim : first_col + (head + 1) * value_dim]
        sigma = logistic(gate)
        d_y = d_y_ref[:, at]
        d_gain = d_gain + jnp.sum(d_y * normed * (gate * sigma), axis=0, keepdims=True)
        scaled = d_y * gain_ref[...]
        d_gate_ref[:, at] = (
            scaled * normed * (sigma * (1.0 + gate * (1.0 - sigma)))
        ).astype(jnp.bfloat16)
        d_normed = scaled * (gate * sigma)
        d_mixed = scale * (d_normed - normed * (row_sum(d_normed * normed) / value_dim))
        d_mixed_ref[:, at] = d_mixed
        d_initial_ref[head] = product(
            halves(carried_ref[head]), halves(d_mixed), (0, 0)
        )
    d_gain_ref[...] = jnp.broadcast_to(d_gain, d_gain_ref.shape)


def enter_back_kernel(
    heads,
    key_dim,
    d_mixed_ref,
    d_gate_ref,
    d_end_ref,
    initial_ref,
    proj_ref,
    edge_ref,
    same_ref,
    taps_ref,
    params_ref,
    conv_ref,
    query_ref,
    key_ref,
    decay_ref,
    gram_ref,
    score_ref,
    inverse_ref,
    from_key_ref,
    from_value_ref,
    cols_ref,
    d_proj_ref,
    d_last_ref,
    d_edge_ref,
    d_taps_ref,
    d_params_ref,
    ext,
    d_ext,
):
    rows, conv_cols = conv_ref.shape
    query_cols = heads * key_dim
    value_dim = from_value_ref.shape[2]
    value_cols = heads * value_dim
    margin = taps_ref.shape[0]
    lane = lax.broadcasted_iota(jnp.int32, (rows, LANES), 1)
    row, col = iotas(rows)
    last_row = lax.broadcasted_iota(jnp.int32, (rows, 1), 0) == rows - 1
    d_total = jnp.zeros((rows, LANES), jnp.float32)
    d_tail = jnp.zeros((rows, LANES), jnp.float32)
    d_active = []
    for head in range(heads):
        keys_at = slice(head * key_dim, (head + 1) * key_dim)
        queries, keys = query_ref[:, keys_at], key_ref[:, keys_at]
        base = 2 * query_cols + head * value_dim
        values = conv_ref[:, base : base + value_dim]
        values = values * logistic(values)
        anchor = cols_ref[:, head : head + 1]
        beta = cols_ref[:, heads + head : heads + head + 1]
        closing = cols_ref[:, 2 * heads + head : 2 * heads + head + 1]
        decay, gram, score = decay_ref[head], gram_ref[head], score_ref[head]
        initial = initial_ref[head]
        d_end = d_end_ref[head]
        d_mixed = d_mixed_ref[:, head * value_dim : (head + 1) * value_dim]
        initial_parts, end_parts = halves(initial), halves(d_end)
        mixed_parts = halves(d_mixed)
        key_parts, query_parts = halves(keys), halves(queries)
        updates = from_value_ref[head] + product(halves(from_key_ref[head]), initial_parts)
        update_parts = halves(updates)
        key_state = product(key_parts, initial_parts)
        query_state = product(query_parts, initial_parts)
        d_updates = product(halves(score), mixed_parts, (0, 0)) + product(
            halves(closing * keys), end_parts
        )
        d_target = product(halves(inverse_ref[head]), halves(d_updates), (0, 0))
        d_delta = beta * d_target
        delta = values - anchor * key_state
        d_lower = -product(halves(d_target), update_parts, (1, 1))
        d_score = product(mixed_parts, update_parts, (1, 1))
        d_pair = halves(d_score * decay)
        d_lower_gram = d_lower * gram
        d_beta = row_sum(d_target * delta) + row_sum(d_lower_gram)
        d_gram = halves(jnp.where(col < row, d_lower * (beta * decay), 0.0))
        back = halves(anchor * d_delta)
        d_query = product(d_pair, key_parts) + anchor * product(
            mixed_parts, initial_parts, (1, 1)
        )
        d_closed = product(update_parts, end_parts, (1, 1))
        d_key = (
            product(d_pair, query_parts, (0, 0))
            + product(d_gram, key_parts)
            + product(d_gram, key_parts, (0, 0))
            + closing * d_closed
            - product(back, initial_parts, (1, 1))
        )
        d_anchor = row_sum(d_mixed * query_state) - row_sum(d_delta * key_state)
        d_anchor = d_anchor + jnp.where(last_row, jnp.sum(d_end * initial), 0.0)
        d_closing = closing * row_sum(keys * d_closed)
        flow = d_score * score + beta * d_lower_gram
        into = jnp.broadcast_to(jnp.sum(flow, axis=0, keepdims=True), (LANES, rows)).T
        d_cumulative = row_sum(flow) - into[:, 0:1] + anchor * d_anchor - d_closing
        d_cumulative = d_cumulative + jnp.where(last_row, jnp.sum(d_closing), 0.0)
        d_total = d_total + in_lane(lane, head, d_cumulative)
        d_tail = d_tail + in_lane(lane, heads + head, d_beta * beta * (1.0 - beta))
        raw_query = conv_ref[:, keys_at]
        raw_key = conv_ref[:, query_cols + head * key_dim : query_cols + (head + 1) * key_dim]
        query_sigma, key_sigma = logistic(raw_query), logistic(raw_key)
        active = raw_query * query_sigma
        scale = lax.rsqrt(row_sum(active * active) + EPSILON)
        unit = active * scale
        d_unit = d_query * key_dim ** (-0.5)
        d_raw_query = (
            scale
            * (d_unit - unit * row_sum(d_unit * unit))
            * (query_sigma * (1.0 + raw_query * (1.0 - query_sigma)))
        )
        active = raw_key * key_sigma
        scale = lax.rsqrt(row_sum(active * active) + EPSILON)
        d_raw_key = (
            scale
            * (d_key - keys * row_sum(d_key * keys))
            * (key_sigma * (1.0 + raw_key * (1.0 - key_sigma)))
        )
        raw_value = conv_ref[:, base : base + value_dim]
        value_sigma = logistic(raw_value)
        d_raw_value = d_delta * (value_sigma * (1.0 + raw_value * (1.0 - value_sigma)))
        d_active.append((d_raw_query, d_raw_key, d_raw_value))
    tail = proj_ref[:, conv_cols + value_cols :]
    rate, softened = head_params(params_ref, tail, heads, lane)
    since = jnp.where(col >= row, 1.0, 0.0).astype(jnp.bfloat16)
    d_rate = exact_sum(since, d_total)
    d_decay = jnp.where(
        lane < heads, d_rate * (-jnp.exp(params_ref[0:1, :])) * logistic(softened), 0.0
    )
    d_params_ref[0:1, :] = jnp.sum(d_rate * rate, axis=0, keepdims=True)
    d_params_ref[1:2, :] = jnp.sum(d_decay, axis=0, keepdims=True)
    d_params_ref[2:, :] = jnp.zeros((d_params_ref.shape[0] - 2, LANES), jnp.float32)
    d_proj_ref[:, conv_cols + value_cols :] = (d_decay + d_tail).astype(jnp.bfloat16)
    d_proj_ref[:, conv_cols : conv_cols + value_cols] = d_gate_ref[...]
    d_convolved = jnp.concatenate(
        [part[0] for part in d_active]
        + [part[1] for part in d_active]
        + [part[2] for part in d_active],
        axis=1,
    )
    ext[0:EDGE, :] = edge_ref[...].astype(jnp.float32)
    ext[EDGE : EDGE + rows, :] = (
        proj_ref[:, 0:conv_cols].astype(jnp.bfloat16).astype(jnp.float32)
    )
    zeros = jnp.zeros((EDGE, conv_cols), jnp.float32)
    d_ext[0:EDGE, :] = zeros
    d_ext[EDGE + rows :, :] = zeros
    d_taps_ref[...] = jnp.zeros(d_taps_ref.shape, jnp.float32)
    d_taps_ref[0:1, :] = jnp.sum(
        d_convolved * ext[EDGE : EDGE + rows, :], axis=0, keepdims=True
    )
    d_pre = taps_ref[0:1, :] * d_convolved
    d_edge = zeros
    for lag in range(1, margin):
        kept = d_convolved * same_ref[:, lag : lag + 1]
        d_taps_ref[lag : lag + 1, :] = jnp.sum(
            kept * ext[EDGE - lag : EDGE - lag + rows, :], axis=0, keepdims=True
        )
        d_ext[EDGE : EDGE + rows, :] = kept
        weight = taps_ref[lag : lag + 1, :]
        d_pre = d_pre + weight * d_ext[EDGE + lag : EDGE + lag + rows, :]
        d_edge = d_edge + weight * d_ext[lag : lag + EDGE, :]
    d_proj_ref[:, 0:conv_cols] = d_pre.astype(jnp.bfloat16)
    d_last_ref[...] = d_pre[rows - EDGE :, :]
    d_edge_ref[...] = d_edge


VMEM_MOST = 40 * 1024 * 1024


def on_core(kernel, name, shapes, scratch=()):
    return pl.pallas_call(
        kernel,
        out_shape=[jax.ShapeDtypeStruct(shape, dtype) for shape, dtype in shapes],
        scratch_shapes=[pltpu.VMEM(shape, dtype) for shape, dtype in scratch],
        compiler_params=pltpu.CompilerParams(vmem_limit_bytes=VMEM_MOST),
        name=name,
    )


MESH = pl.DeviceIdType.MESH


class Links:
    def __init__(self, send, recv):
        self.send, self.recv, self.used = send, recv, 0

    def take(self, count=1):
        first = self.used
        self.used = first + count
        return first

    def copy(self, index, source, target, where):
        return pltpu.make_async_remote_copy(
            src_ref=source,
            dst_ref=target,
            send_sem=self.send.at[index],
            recv_sem=self.recv.at[index],
            device_id=where,
            device_id_type=MESH,
        )


def meet(places):
    barrier = pltpu.get_barrier_semaphore()
    for place in places:
        pl.semaphore_signal(barrier, inc=1, device_id=place, device_id_type=MESH)
    pl.semaphore_wait(barrier, len(places))


def flipped(index, bit):
    step = 1 << bit
    return index + step - 2 * step * lax.rem(index // step, 2)


def line_places(axis):
    me = lax.axis_index(axis)
    return [{axis: lax.rem(me + distance, 4)} for distance in range(1, 4)]


class LineSum:
    def __init__(self, axis, pieces, x_ref, out_ref, bufs, links):
        self.pieces, self.x_ref, self.out_ref, self.links = pieces, x_ref, out_ref, links
        self.from_end, self.to_mate, self.from_mate, self.keep = bufs
        me = lax.axis_index(axis)
        self.inner = (me == 1) | (me == 2)
        self.partner = {axis: flipped(me, 0)}
        self.mate = {axis: 3 - me}
        self.mine = me // 2
        self.size = x_ref.shape[0] // pieces
        self.half = self.size // 2
        self.ends = links.take(pieces)
        self.pairs = links.take(pieces)
        self.totals = links.take(pieces)
        self.backs = links.take(pieces)
        self.others = links.take(pieces)

    def rows(self, piece, part):
        start = piece * self.size + part * self.half
        return pl.ds(pl.multiple_of(start, self.half), self.half)

    def end_copy(self, piece):
        return self.links.copy(
            self.ends + piece,
            self.x_ref.at[pl.ds(piece * self.size, self.size)],
            self.from_end.at[piece],
            self.partner,
        )

    def pair_copy(self, piece):
        return self.links.copy(
            self.pairs + piece, self.to_mate.at[piece], self.from_mate.at[piece], self.mate
        )

    def out_copy(self, base, piece, part, where):
        ref = self.out_ref.at[self.rows(piece, part)]
        return self.links.copy(base + piece, ref, ref, where)

    def start(self):
        @pl.when(jnp.logical_not(self.inner))
        def _():
            for piece in range(self.pieces):
                self.end_copy(piece).start()

    def first(self, piece):
        @pl.when(self.inner)
        def _():
            self.end_copy(piece).wait_recv()
            arrived = self.from_end.at[piece]

            def pair(part):
                at = pl.ds(pl.multiple_of(part * self.half, self.half), self.half)
                return self.x_ref[self.rows(piece, part)].astype(jnp.float32) + arrived[
                    at
                ].astype(jnp.float32)

            self.to_mate[piece] = pair(1 - self.mine).astype(self.to_mate.dtype)
            self.pair_copy(piece).start()
            self.keep[piece] = pair(self.mine)

    def second(self, piece):
        @pl.when(self.inner)
        def _():
            self.pair_copy(piece).wait_recv()
            total = self.keep[piece] + self.from_mate[piece].astype(jnp.float32)
            self.out_ref[self.rows(piece, self.mine)] = total.astype(self.out_ref.dtype)
            self.out_copy(self.totals, piece, self.mine, self.mate).start()
            self.out_copy(self.backs, piece, self.mine, self.partner).start()

    def third(self, piece):
        @pl.when(self.inner)
        def _():
            self.out_copy(self.totals, piece, 1 - self.mine, self.mate).wait_recv()
            self.out_copy(self.others, piece, 1 - self.mine, self.partner).start()

    def step(self, number):
        if number < self.pieces:
            self.first(number)
        if 0 <= number - 1 < self.pieces:
            self.second(number - 1)
        if 0 <= number - 2 < self.pieces:
            self.third(number - 2)

    def steps(self):
        return self.pieces + 2

    def finish(self):
        @pl.when(self.inner)
        def _():
            for piece in range(self.pieces):
                self.pair_copy(piece).wait_send()
                self.out_copy(self.totals, piece, self.mine, self.mate).wait_send()
                self.out_copy(self.backs, piece, self.mine, self.partner).wait_send()
                self.out_copy(self.others, piece, 1 - self.mine, self.partner).wait_send()

        @pl.when(jnp.logical_not(self.inner))
        def _():
            for piece in range(self.pieces):
                self.out_copy(self.backs, piece, self.mine, self.partner).wait_recv()
                self.out_copy(self.others, piece, 1 - self.mine, self.partner).wait_recv()
                self.end_copy(piece).wait_send()


def line_buffers(pieces, shape, dtype):
    size = shape[0] // pieces
    return [
        pltpu.VMEM((pieces, size, shape[1]), dtype),
        pltpu.VMEM((pieces, size // 2, shape[1]), dtype),
        pltpu.VMEM((pieces, size // 2, shape[1]), dtype),
        pltpu.VMEM((pieces, size // 2, shape[1]), jnp.float32),
    ]


def line_kernel(axis, pieces, x_ref, out_ref, *rest):
    links = Links(rest[4], rest[5])
    meet(line_places(axis))
    line = LineSum(axis, pieces, x_ref, out_ref, rest[:4], links)
    line.start()
    for number in range(line.steps()):
        line.step(number)
    line.finish()


def in_vmem(count):
    return [pl.BlockSpec(memory_space=pltpu.VMEM)] * count


def line_summed(value, axis, call, pieces):
    sems = pltpu.SemaphoreType.DMA((5 * pieces,))
    return pl.pallas_call(
        partial(line_kernel, axis, pieces),
        out_shape=jax.ShapeDtypeStruct(value.shape, value.dtype),
        in_specs=in_vmem(1),
        out_specs=in_vmem(1)[0],
        scratch_shapes=line_buffers(pieces, value.shape, value.dtype) + [sems, sems],
        cost_estimate=pl.CostEstimate(
            flops=value.size * 40000, bytes_accessed=value.size * 300, transcendentals=0
        ),
        compiler_params=pltpu.CompilerParams(
            collective_id=call, has_side_effects=True, vmem_limit_bytes=VMEM_MOST
        ),
        name=f"tp_line_{call}",
    )(value)


def square_places(axes):
    first, second = axes
    where, core = lax.axis_index(first), lax.axis_index(second)
    sibling = {second: 1 - core}
    beside = {first: flipped(where, 0)}
    across = {first: flipped(where, 1)}
    return where, core, sibling, beside, across


def gather_kernel(axes, groups, tail_cols, *refs):
    count = sum(len(splits) for splits in groups)
    parts, tail_ref = refs[:count], refs[count]
    outs, gains_ref = refs[count + 1 : count + 1 + len(groups)], refs[-3]
    where, core, sibling, beside, across = square_places(axes)
    rows = parts[0].shape[0]
    half = rows // 2
    mine = pl.ds(pl.multiple_of((where * 2 + core) * rows, rows), rows)
    used = 0
    for splits, out_ref in zip(groups, outs):
        at = 0
        for width in splits:
            out_ref[mine, at : at + width] = parts[used][...]
            at += width
            used += 1
    last = tail_ref[...].astype(jnp.float32)
    outs[0][mine, outs[0].shape[1] - tail_cols :] = last.T.astype(jnp.bfloat16)
    meet([sibling, beside, across])
    links = Links(refs[-2], refs[-1])
    started = []

    def go(out_ref, flip, place, start=0, size=rows):
        owner = where
        for bit in range(2):
            if flip >> bit & 1:
                owner = flipped(owner, bit)
        begin = (owner * 2 + core) * rows + start
        ref = out_ref.at[pl.ds(pl.multiple_of(begin, size), size)]
        copy = links.copy(links.take(), ref, ref, place)
        copy.start()
        started.append(copy)
        return copy

    from_beside = [go(out_ref, 0, beside) for out_ref in outs]
    from_across = [go(out_ref, 0, across) for out_ref in outs]
    siblings = [go(out_ref, 0, sibling) for out_ref in outs]
    upper, lower = [], []
    for number, out_ref in enumerate(outs):
        from_beside[number].wait_recv()
        upper.append(go(out_ref, 1, across, 0, half))
        siblings.append(go(out_ref, 1, sibling))
        from_across[number].wait_recv()
        lower.append(go(out_ref, 2, beside, half, half))
        siblings.append(go(out_ref, 2, sibling))
    for number, out_ref in enumerate(outs):
        upper[number].wait_recv()
        siblings.append(go(out_ref, 3, sibling, 0, half))
        lower[number].wait_recv()
        siblings.append(go(out_ref, 3, sibling, half, half))
    for copy in siblings:
        copy.wait_recv()
    tail = outs[0][:, outs[0].shape[1] - tail_cols :].astype(jnp.float32).T
    gains_ref[...] = tail[0 : gains_ref.shape[0]]
    for copy in started:
        copy.wait_send()


def gathered(groups, tail_rows, axes, call):
    rows = groups[0][0].shape[0]
    tail_cols = tail_rows.shape[0]
    splits = tuple(tuple(part.shape[1] for part in group) for group in groups)
    widths = [sum(split) for split in splits]
    widths[0] += tail_cols
    sems = pltpu.SemaphoreType.DMA((9 * len(groups),))
    parts = [part for group in groups for part in group]
    return pl.pallas_call(
        partial(gather_kernel, axes, splits, tail_cols),
        out_shape=[
            jax.ShapeDtypeStruct((8 * rows, width), jnp.bfloat16) for width in widths
        ]
        + [jax.ShapeDtypeStruct((8, 8 * rows), jnp.float32)],
        in_specs=in_vmem(len(parts) + 1),
        out_specs=in_vmem(len(groups) + 1),
        scratch_shapes=[sems, sems],
        cost_estimate=pl.CostEstimate(
            flops=10000000000, bytes_accessed=60000000, transcendentals=0
        ),
        compiler_params=pltpu.CompilerParams(
            collective_id=call, has_side_effects=True, vmem_limit_bytes=VMEM_MOST
        ),
        name=f"weights_{call}",
    )(*parts, tail_rows)


class SquareSum:
    def __init__(self, axes, g_ref, columns, out_ref, bufs, links):
        self.where, self.core, self.sibling, self.beside, self.across = square_places(axes)
        self.g_ref, self.out_ref, self.columns, self.links = g_ref, out_ref, columns, links
        self.from_core, self.sums, self.from_chip, self.ends = bufs
        self.rows = g_ref.shape[0] // 8
        self.half = self.rows // 2
        self.core_ids = links.take(4)
        self.chip_ids = links.take(4)
        self.end_ids = links.take(2)

    def block(self, flip, of_core):
        owner = self.where
        for bit in range(2):
            if flip >> bit & 1:
                owner = flipped(owner, bit)
        begin = (owner * 2 + of_core) * self.rows
        return pl.ds(pl.multiple_of(begin, self.rows), self.rows)

    def core_copy(self, flip):
        return self.links.copy(
            self.core_ids + flip,
            self.g_ref.at[self.block(flip, 1 - self.core), self.columns],
            self.from_core.at[flip],
            self.sibling,
        )

    def chip_copy(self, slot):
        flip, start, where = (
            (1, 0, self.beside),
            (3, 0, self.beside),
            (2, self.half, self.across),
            (3, self.half, self.across),
        )[slot]
        return self.links.copy(
            self.chip_ids + slot,
            self.sums.at[flip, pl.ds(start, self.half)],
            self.from_chip.at[slot],
            where,
        )

    def end_copy(self, slot):
        flip, start, where = ((2, 0, self.across), (1, self.half, self.beside))[slot]
        return self.links.copy(
            self.end_ids + slot,
            self.sums.at[flip, pl.ds(start, self.half)],
            self.ends.at[slot],
            where,
        )

    def start(self):
        for flip in (3, 1, 2, 0):
            self.core_copy(flip).start()

    def add_core(self, flip):
        self.core_copy(flip).wait_recv()
        own = self.g_ref[self.block(flip, self.core), self.columns].astype(jnp.float32)
        self.sums[flip] = (own + self.from_core[flip].astype(jnp.float32)).astype(
            self.sums.dtype
        )

    def first(self):
        self.add_core(3)
        self.chip_copy(1).start()
        self.chip_copy(3).start()
        self.add_core(1)
        self.chip_copy(0).start()
        self.add_core(2)
        self.chip_copy(2).start()
        self.core_copy(0).wait_recv()

    def second(self):
        half = self.half
        self.chip_copy(1).wait_recv()
        self.sums[2, 0:half] = (
            self.sums[2, 0:half].astype(jnp.float32) + self.from_chip[1].astype(jnp.float32)
        ).astype(self.sums.dtype)
        self.end_copy(0).start()
        self.chip_copy(3).wait_recv()
        self.sums[1, half:] = (
            self.sums[1, half:].astype(jnp.float32) + self.from_chip[3].astype(jnp.float32)
        ).astype(self.sums.dtype)
        self.end_copy(1).start()

    def third(self):
        half = self.half
        own = self.g_ref[self.block(0, self.core), self.columns].astype(jnp.float32)
        own = own + self.from_core[0].astype(jnp.float32)
        for slot, part in ((0, slice(0, half)), (1, slice(half, 2 * half))):
            self.chip_copy(2 * slot).wait_recv()
            self.end_copy(slot).wait_recv()
            self.out_ref[part, self.columns] = (
                own[part]
                + self.from_chip[2 * slot].astype(jnp.float32)
                + self.ends[slot].astype(jnp.float32)
            )

    def finish(self):
        for flip in range(4):
            self.core_copy(flip).wait_send()
        for slot in range(4):
            self.chip_copy(slot).wait_send()
        for slot in range(2):
            self.end_copy(slot).wait_send()


def square_buffers(rows, width):
    return [
        pltpu.VMEM((4, rows, width), jnp.bfloat16),
        pltpu.VMEM((4, rows, width), jnp.bfloat16),
        pltpu.VMEM((4, rows // 2, width), jnp.bfloat16),
        pltpu.VMEM((2, rows // 2, width), jnp.bfloat16),
    ]


def last_kernel(axes, axis, pieces, cuts, x_ref, g_ref, h_ref, small_ref, *rest):
    out_ref, g_out, h_out, small_out = rest[:4]
    line_bufs, rest = rest[4:8], rest[8:]
    square_bufs = [rest[4 * i : 4 * i + 4] for i in range(len(cuts))]
    small_bufs, send, recv = rest[-4:-2], rest[-2], rest[-1]
    where, core, sibling, beside, across = square_places(axes)
    me = lax.axis_index(axis)
    links = Links(send, recv)
    line = LineSum(axis, pieces, x_ref, out_ref, line_bufs, links)
    squares = [
        SquareSum(
            axes, (g_ref, h_ref)[which], pl.ds(begin, size), (g_out, h_out)[which], bufs, links
        )
        for (which, begin, size), bufs in zip(cuts, square_bufs)
    ]
    steps = [sibling, beside, across, {axis: flipped(me, 0)}, {axis: flipped(me, 1)}]
    ids = links.take(len(steps))
    here, there = small_bufs
    common = here.shape[1] // 2

    def small_copy(number):
        if number < 3:
            return links.copy(ids + number, here.at[number], there.at[number], steps[number])
        part = pl.ds(common, common)
        return links.copy(
            ids + number, here.at[number, part], there.at[number, part], steps[number]
        )

    def small_step(number):
        small_copy(number).wait_recv()
        if number < 3:
            here[number + 1] = here[number] + there[number]
        else:
            here[number + 1, common:] = here[number, common:] + there[number, common:]
        if number + 1 < len(steps):
            small_copy(number + 1).start()

    here[0] = small_ref[...]
    meet([sibling, beside, across] + line_places(axis))
    line.start()
    squares[0].start()
    small_copy(0).start()
    for square in squares[1:]:
        square.start()
    for number in range(max(line.steps(), len(squares))):
        if number < len(squares):
            squares[number].first()
        if number < line.steps():
            line.step(number)
        if number < len(steps):
            small_step(number)
    for square in squares:
        square.second()
    for square in squares:
        square.third()
    line.finish()
    small_out[0:common, :] = here[3, 0:common]
    small_out[common:, :] = here[len(steps), common:]
    for square in squares:
        square.finish()
    for number in range(len(steps)):
        small_copy(number).wait_send()


def last_sums(value, grad_in, grad_out, small, axes, axis, call, pieces, cuts):
    rows = grad_in.shape[0] // 8
    count = 5 * pieces + 10 * len(cuts) + 5
    sems = pltpu.SemaphoreType.DMA((count,))
    scratch = line_buffers(pieces, value.shape, value.dtype)
    for _, _, size in cuts:
        scratch = scratch + square_buffers(rows, size)
    scratch = scratch + [
        pltpu.VMEM((6,) + small.shape, small.dtype),
        pltpu.VMEM((5,) + small.shape, small.dtype),
        sems,
        sems,
    ]
    return pl.pallas_call(
        partial(last_kernel, axes, axis, pieces, cuts),
        out_shape=[
            jax.ShapeDtypeStruct(value.shape, value.dtype),
            jax.ShapeDtypeStruct((rows, grad_in.shape[1]), jnp.float32),
            jax.ShapeDtypeStruct((rows, grad_out.shape[1]), jnp.float32),
            jax.ShapeDtypeStruct(small.shape, jnp.float32),
        ],
        in_specs=in_vmem(4),
        out_specs=in_vmem(4),
        scratch_shapes=scratch,
        cost_estimate=pl.CostEstimate(
            flops=20000000000, bytes_accessed=100000000, transcendentals=0
        ),
        compiler_params=pltpu.CompilerParams(
            collective_id=call, has_side_effects=True, vmem_limit_bytes=VMEM_MOST
        ),
        name=f"last_sums_{call}",
    )(value, grad_in, grad_out, small)


def apply_map(matrix, addend, incoming):
    return jnp.einsum("hde,hew->hdw", matrix, incoming, precision=HIGHEST) + addend


def local(
    tokens,
    segments,
    cotangent,
    mixer_gain,
    mlp_gain,
    query_weight,
    key_weight,
    value_weight,
    gate_weight,
    decay_weight,
    beta_weight,
    output_weight,
    conv_query,
    conv_key,
    conv_value,
    decay_log,
    decay_bias,
    head_gain,
    hidden_gate,
    hidden_up,
    hidden_down,
):
    width = tokens.shape[-1]
    inputs = tokens.reshape(-1, width).astype(jnp.float32)
    row_count = inputs.shape[0]
    query_cols = query_weight.shape[1]
    value_cols = value_weight.shape[1]
    head_count = decay_weight.shape[1]
    ff_cols = hidden_gate.shape[1]
    axes = ("dp", "ctx")
    used = 2 * query_cols + 2 * value_cols + 2 * head_count + 2
    pad_cols = -used % LANES
    own_rows = query_weight.shape[0]
    squared = lax.axis_size("dp") == 4 and lax.axis_size("ctx") == 2
    if squared:
        tail_rows = jnp.concatenate(
            [
                decay_weight.T,
                beta_weight.T,
                mixer_gain[None, :],
                mlp_gain[None, :],
                jnp.zeros((pad_cols, own_rows), jnp.bfloat16),
            ],
            0,
        )
        in_weights, full_output, gain_rows = gathered(
            [[query_weight, key_weight, value_weight, gate_weight], [output_weight]],
            tail_rows,
            axes,
            5,
        )
        gain_one = gain_rows[2 * head_count]
        gain_two = gain_rows[2 * head_count + 1]
    else:
        in_weights = lax.all_gather(
            jnp.concatenate(
                [
                    query_weight,
                    key_weight,
                    value_weight,
                    gate_weight,
                    decay_weight,
                    beta_weight,
                    mixer_gain[:, None],
                    mlp_gain[:, None],
                    jnp.zeros((own_rows, pad_cols), jnp.bfloat16),
                ],
                1,
            ),
            axes,
            axis=0,
            tiled=True,
        )
        full_output = lax.all_gather(output_weight, axes, axis=0, tiled=True)
        gain_one = in_weights[:, used - 2].astype(jnp.float32)
        gain_two = in_weights[:, used - 1].astype(jnp.float32)
    full_gate_up = lax.all_gather(
        jnp.concatenate([hidden_gate, hidden_up], 1), axes, axis=0, tiled=True
    )
    full_hidden_down = lax.all_gather(hidden_down, axes, axis=0, tiled=True)
    conv_cols = 2 * query_cols + value_cols
    key_dim = query_cols // head_count
    rms_one = lax.rsqrt(jnp.mean(inputs * inputs, -1, keepdims=True) + EPSILON)
    normed_one = inputs * rms_one
    hidden_one = (normed_one * gain_one).astype(jnp.bfloat16)
    projected = jnp.dot(hidden_one, in_weights, preferred_element_type=jnp.float32)
    conv_weight = jnp.concatenate([conv_query, conv_key, conv_value], 1)
    taps = conv_weight.shape[0]
    margin = taps - 1
    last_rows = projected[row_count - EDGE :, :conv_cols].astype(jnp.bfloat16)
    edge_rows = passed_along(last_rows, "ctx", 1)
    seg_padded = jnp.concatenate([jnp.full((margin,), -1, jnp.int32), segments.reshape(-1)], 0)
    seg_ext = lax.dynamic_slice_in_dim(
        seg_padded, lax.axis_index("ctx") * row_count, row_count + margin
    )
    same_doc = jnp.stack(
        [
            (seg_ext[margin - lag : margin - lag + row_count] == seg_ext[margin:])
            for lag in range(taps)
        ],
        1,
    ).astype(jnp.float32)
    lane_pad = (0, LANES - head_count)
    params = jnp.stack([jnp.pad(decay_log, lane_pad), jnp.pad(decay_bias, lane_pad)])
    value_dim = value_cols // head_count
    ctx_size = lax.axis_size("ctx")
    chained = ctx_size > 2
    square = ((head_count, row_count, row_count), jnp.float32)
    tall_key = ((head_count, row_count, key_dim), jnp.float32)
    tall_value = ((head_count, row_count, value_dim), jnp.float32)
    flat_key = ((row_count, query_cols), jnp.float32)
    state = ((head_count, key_dim, value_dim), jnp.float32)
    entered = on_core(
        partial(enter_kernel, head_count, key_dim, chained),
        "mixer_enter",
        [
            ((row_count, conv_cols), jnp.float32),
            flat_key,
            flat_key,
            square,
            square,
            square,
            square,
            tall_key,
            tall_value,
            tall_key,
            tall_value,
            state,
            ((row_count, LANES), jnp.float32),
        ]
        + ([((head_count, key_dim, key_dim), jnp.float32)] if chained else []),
        [((EDGE + row_count, conv_cols), jnp.float32)],
    )(projected, edge_rows, same_doc, conv_weight, params)
    convolved, queries, key_rows, decay_pair, gram, score, inverse = entered[:7]
    from_key, from_value, carried, local_out, offset, mixer_cols = entered[7:13]

    initial = jnp.zeros_like(offset)
    for hop in range(ctx_size - 1):
        leaving = offset if hop == 0 else apply_map(entered[13], offset, initial)
        initial = passed_along(leaving, "ctx", 1)
    gain_row = head_gain[None, :]
    mixed_b, mixed = on_core(
        partial(leave_kernel, head_count),
        "mixer_leave",
        [((row_count, value_cols), jnp.bfloat16), ((row_count, value_cols), jnp.float32)],
    )(carried, local_out, initial, projected, gain_row)
    mixer_part = jnp.einsum("rc,dc->rd", mixed_b, full_output, preferred_element_type=jnp.float32)
    attention = summed(mixer_part.astype(jnp.bfloat16), "tp", 0).astype(jnp.float32)
    middle = inputs + attention
    rms_two = lax.rsqrt(jnp.mean(middle * middle, -1, keepdims=True) + EPSILON)
    normed_two = middle * rms_two
    hidden_two = (normed_two * gain_two).astype(jnp.bfloat16)
    gate_up = jnp.dot(hidden_two, full_gate_up, preferred_element_type=jnp.float32)
    gate_pre = gate_up[:, :ff_cols]
    up_pre = gate_up[:, ff_cols:]
    sigma = jax.nn.sigmoid(gate_pre)
    swish = gate_pre * sigma
    activ = (swish * up_pre).astype(jnp.bfloat16)
    feed_part = jnp.einsum("rf,df->rd", activ, full_hidden_down, preferred_element_type=jnp.float32)
    grad_rows = cotangent.reshape(-1, width)
    grad_out = grad_rows.astype(jnp.float32)
    d_activ = jnp.dot(grad_rows, full_hidden_down, preferred_element_type=jnp.float32)
    d_gate_pre = (d_activ * up_pre * sigma * (1.0 + gate_pre * (1.0 - sigma))).astype(jnp.bfloat16)
    d_up_pre = (d_activ * swish).astype(jnp.bfloat16)
    grad_down = jnp.einsum("rd,rf->df", grad_rows, activ, preferred_element_type=jnp.float32)
    d_gate_up = jnp.concatenate([d_gate_pre, d_up_pre], 1)
    grad_gate_up = jnp.einsum(
        "rd,rf->df", hidden_two, d_gate_up, preferred_element_type=jnp.float32
    )
    two_part = jnp.einsum("rf,df->rd", d_gate_up, full_gate_up, preferred_element_type=jnp.float32)
    both = summed(jnp.concatenate([two_part, feed_part], 0).astype(jnp.bfloat16), "tp", 1)
    d_hidden_two = both[:row_count].astype(jnp.float32)
    feed = both[row_count:].astype(jnp.float32)
    block_out = (middle + feed).astype(jnp.bfloat16).reshape(tokens.shape)

    def scattered(member):
        total = lax.psum_scatter(
            member.astype(jnp.bfloat16), axes, scatter_dimension=0, tiled=True
        )
        return total.astype(jnp.float32)

    down_own = scattered(grad_down)
    gate_up_own = scattered(grad_gate_up)
    grad_gain_two = jnp.sum(d_hidden_two * normed_two, 0)
    dn_two = d_hidden_two * gain_two
    d_middle = grad_out + rms_two * (
        dn_two - normed_two * jnp.mean(dn_two * normed_two, -1, keepdims=True)
    )
    d_middle_b = d_middle.astype(jnp.bfloat16)
    d_mixed = jnp.dot(d_middle_b, full_output, preferred_element_type=jnp.float32)
    grad_output = jnp.einsum("rd,rc->dc", d_middle_b, mixed_b, preferred_element_type=jnp.float32)
    d_out, d_gate, d_head, init_grad = on_core(
        partial(leave_back_kernel, head_count),
        "mixer_leave_back",
        [
            ((row_count, value_cols), jnp.float32),
            ((row_count, value_cols), jnp.bfloat16),
            ((8, value_dim), jnp.float32),
            state,
        ],
    )(d_mixed, mixed, projected, gain_row, carried)
    d_head = d_head[0]
    end_grad = jnp.zeros_like(offset)
    for hop in range(ctx_size - 1):
        leaving = (
            init_grad
            if hop == 0
            else apply_map(jnp.swapaxes(entered[13], 1, 2), init_grad, end_grad)
        )
        end_grad = passed_along(leaving, "ctx", -1)
    edge_shape = ((EDGE, conv_cols), jnp.float32)
    d_proj, d_last, d_edge, d_conv, d_params = on_core(
        partial(enter_back_kernel, head_count, key_dim),
        "mixer_enter_back",
        [
            (projected.shape, jnp.bfloat16),
            edge_shape,
            edge_shape,
            ((8, conv_cols), jnp.float32),
            ((8, LANES), jnp.float32),
        ],
        [
            ((EDGE + row_count, conv_cols), jnp.float32),
            ((2 * EDGE + row_count, conv_cols), jnp.float32),
        ],
    )(
        d_out,
        d_gate,
        end_grad,
        initial,
        projected,
        edge_rows,
        same_doc,
        conv_weight,
        params,
        convolved,
        queries,
        key_rows,
        decay_pair,
        gram,
        score,
        inverse,
        from_key,
        from_value,
        mixer_cols,
    )
    d_conv = d_conv[:taps]
    d_log, d_bias = d_params[0, :head_count], d_params[1, :head_count]
    edge_back = passed_along(d_edge, "ctx", -1)
    d_proj = lax.dynamic_update_slice(
        d_proj, (d_last + edge_back).astype(jnp.bfloat16), (row_count - EDGE, 0)
    )
    grad_input = jnp.einsum("rd,rc->dc", hidden_one, d_proj, preferred_element_type=jnp.float32)
    one_part = jnp.einsum("rc,dc->rd", d_proj, in_weights, preferred_element_type=jnp.float32)
    small_width = max(conv_cols, width)

    def small_row(*members):
        member = jnp.concatenate([part.reshape(-1) for part in members])
        return jnp.pad(member, (0, small_width - member.shape[0]))[None, :]

    if squared:
        near = jnp.concatenate(
            [
                jnp.pad(d_conv, ((0, 0), (0, small_width - conv_cols))),
                small_row(d_log, d_bias),
                small_row(grad_gain_two),
            ],
            0,
        )
        wide = jnp.concatenate(
            [small_row(d_head), small_row(jnp.sum(one_part * normed_one, 0))], 0
        )
        lines = -(-near.shape[0] // 8) * 8
        small = jnp.concatenate(
            [
                jnp.pad(near, ((0, lines - near.shape[0]), (0, 0))),
                jnp.pad(wide, ((0, lines - wide.shape[0]), (0, 0))),
            ],
            0,
        )
        in_cols = grad_input.shape[1]
        first_cut = -(-in_cols // (2 * LANES)) * LANES
        cuts = ((0, 0, first_cut), (0, first_cut, in_cols - first_cut), (1, 0, value_cols))
        one_sum, input_own, output_own, small = last_sums(
            one_part.astype(jnp.bfloat16),
            grad_input.astype(jnp.bfloat16),
            grad_output.astype(jnp.bfloat16),
            small,
            axes,
            "tp",
            6,
            4,
            cuts,
        )
    else:
        one_part, down_own = lax.optimization_barrier((one_part, down_own))
        one_sum = summed(one_part.astype(jnp.bfloat16), "tp", 2)
        one_sum, gate_up_own = lax.optimization_barrier((one_sum, gate_up_own))
    d_hidden_one = one_sum.astype(jnp.float32)
    dn_one = d_hidden_one * gain_one
    tokens_grad = d_middle + rms_one * (
        dn_one - normed_one * jnp.mean(dn_one * normed_one, -1, keepdims=True)
    )
    tokens_grad = tokens_grad.reshape(tokens.shape)
    edges = [
        0,
        query_cols,
        2 * query_cols,
        conv_cols,
        conv_cols + value_cols,
        conv_cols + value_cols + head_count,
        conv_cols + value_cols + 2 * head_count,
    ]

    if squared:
        begin = (lax.axis_index("dp") * 2 + lax.axis_index("ctx")) * own_rows
        gain_one_own = lax.dynamic_slice_in_dim(small[lines + 1], begin, own_rows)
        gain_two_own = lax.dynamic_slice_in_dim(small[taps + 1], begin, own_rows)
        conv_total = small[:taps, :conv_cols]
        log_total = small[taps, :head_count]
        bias_total = small[taps, head_count : 2 * head_count]
        head_total = small[lines, :value_dim]
    else:
        grad_gain_one = jnp.sum(d_hidden_one * normed_one, 0)
        column = jnp.arange(grad_input.shape[1])[None, :]
        grad_input = jnp.where(column == used - 2, grad_gain_one[:, None], grad_input)
        grad_input = jnp.where(column == used - 1, grad_gain_two[:, None], grad_input)
        output_own = scattered(grad_output)
        input_own = scattered(grad_input)
        gain_one_own = input_own[:, used - 2]
        gain_two_own = input_own[:, used - 1]
        rest = jnp.concatenate([d_head, d_log, d_bias])
        pad_row = jnp.zeros((-rest.shape[0] % conv_cols,), jnp.float32)
        rest = jnp.concatenate([rest, pad_row]).reshape(-1, conv_cols)
        packed = jnp.concatenate([d_conv, rest], 0)
        lines = packed.shape[0]
        packed = jnp.concatenate([packed, jnp.zeros((-lines % 8, conv_cols), jnp.float32)], 0)
        packed = small_sum(packed, ("dp", "ctx"), 3)
        conv_total = packed[:taps]
        rest = packed[taps:lines].reshape(-1)
        log_total = rest[value_dim : value_dim + head_count]
        bias_total = rest[value_dim + head_count : value_dim + 2 * head_count]
        head_total = small_sum(
            jnp.broadcast_to(rest[None, :value_dim], (8, value_dim)), ("tp",), 4
        )[0]
    reduced = (
        gain_one_own,
        gain_two_own,
        *(input_own[:, edges[i] : edges[i + 1]] for i in range(6)),
        output_own,
        gate_up_own[:, :ff_cols],
        gate_up_own[:, ff_cols:],
        down_own,
    )
    return (
        block_out,
        tokens_grad,
        reduced[0],
        reduced[1],
        reduced[2],
        reduced[3],
        reduced[4],
        reduced[5],
        reduced[6],
        reduced[7],
        reduced[8],
        conv_total[:, :query_cols],
        conv_total[:, query_cols : 2 * query_cols],
        conv_total[:, 2 * query_cols :],
        log_total,
        bias_total,
        head_total,
        reduced[9],
        reduced[10],
        reduced[11],
    )


def solution(mesh):
    return jax.shard_map(
        local,
        mesh=mesh,
        in_specs=(
            P("dp", "ctx", None),
            P("dp", None),
            P("dp", "ctx", None),
            P(("dp", "ctx")),
            P(("dp", "ctx")),
            P(("dp", "ctx"), "tp"),
            P(("dp", "ctx"), "tp"),
            P(("dp", "ctx"), "tp"),
            P(("dp", "ctx"), "tp"),
            P(("dp", "ctx"), "tp"),
            P(("dp", "ctx"), "tp"),
            P(("dp", "ctx"), "tp"),
            P(None, "tp"),
            P(None, "tp"),
            P(None, "tp"),
            P("tp"),
            P("tp"),
            P(),
            P(("dp", "ctx"), "tp"),
            P(("dp", "ctx"), "tp"),
            P(("dp", "ctx"), "tp"),
        ),
        out_specs=(
            P("dp", "ctx", None),
            P("dp", "ctx", None),
            P(("dp", "ctx")),
            P(("dp", "ctx")),
            P(("dp", "ctx"), "tp"),
            P(("dp", "ctx"), "tp"),
            P(("dp", "ctx"), "tp"),
            P(("dp", "ctx"), "tp"),
            P(("dp", "ctx"), "tp"),
            P(("dp", "ctx"), "tp"),
            P(("dp", "ctx"), "tp"),
            P(None, "tp"),
            P(None, "tp"),
            P(None, "tp"),
            P("tp"),
            P("tp"),
            P(),
            P(("dp", "ctx"), "tp"),
            P(("dp", "ctx"), "tp"),
            P(("dp", "ctx"), "tp"),
        ),
        check_vma=False,
    )
```

```python
from functools import partial

import jax
import jax.numpy as jnp
from jax import lax
from jax.experimental import pallas as pl
from jax.experimental.pallas import tpu as pltpu
from jax.sharding import PartitionSpec as P

EPSILON = 1e-06
HIGHEST = lax.Precision.HIGHEST
LANES = 128


def peer_of(axes, sizes, distance):
    flat = 0
    total = 1
    for axis, size in zip(axes, sizes):
        flat = flat * size + lax.axis_index(axis)
        total = total * size
    other = lax.rem(flat + distance, total)
    where = {}
    for axis, size in reversed(list(zip(axes, sizes))):
        where[axis] = lax.rem(other, size)
        other = other // size
    return where


def greet(axes, sizes, peers):
    barrier = pltpu.get_barrier_semaphore()
    for distance in range(1, peers + 1):
        pl.semaphore_signal(
            barrier,
            inc=1,
            device_id=peer_of(axes, sizes, distance),
            device_id_type=pl.DeviceIdType.MESH,
        )
    pl.semaphore_wait(barrier, peers)


def sum_kernel(axis, size, x_ref, out_ref, parts, mine, got, send, recv, send_two, recv_two):
    peers = size - 1
    me = lax.axis_index(axis)
    rows = x_ref.shape[0] // size
    greet((axis,), (size,), peers)

    def block(index):
        return pl.ds(pl.multiple_of(index * rows, rows), rows)

    copies = []
    for distance in range(1, size):
        other = lax.rem(me + distance, size)
        copy = pltpu.make_async_remote_copy(
            src_ref=x_ref.at[block(other)],
            dst_ref=parts.at[distance - 1],
            send_sem=send.at[distance - 1],
            recv_sem=recv.at[distance - 1],
            device_id={axis: other},
            device_id_type=pl.DeviceIdType.MESH,
        )
        copy.start()
        copies.append(copy)
    total = x_ref[block(me)].astype(jnp.float32)
    for distance in range(1, size):
        copies[distance - 1].wait_recv()
        total = total + parts[distance - 1].astype(jnp.float32)
    total = total.astype(out_ref.dtype)
    mine[...] = total
    out_ref[block(me)] = total
    more = []
    for distance in range(1, size):
        copy = pltpu.make_async_remote_copy(
            src_ref=mine,
            dst_ref=got.at[distance - 1],
            send_sem=send_two.at[distance - 1],
            recv_sem=recv_two.at[distance - 1],
            device_id={axis: lax.rem(me + distance, size)},
            device_id_type=pl.DeviceIdType.MESH,
        )
        copy.start()
        more.append(copy)
    for distance in range(1, size):
        more[distance - 1].wait_recv()
        out_ref[block(lax.rem(me + size - distance, size))] = got[distance - 1]
    for copy in copies + more:
        copy.wait_send()


def summed(value, axis, call):
    size = lax.axis_size(axis)
    if size == 1:
        return value
    rows, cols = value.shape
    if size == 4 and rows % 128 == 0:
        return line_summed(value, axis, call, 4)
    piece = (size - 1, rows // size, cols)
    sems = pltpu.SemaphoreType.DMA((size - 1,))
    return pl.pallas_call(
        partial(sum_kernel, axis, size),
        out_shape=jax.ShapeDtypeStruct(value.shape, value.dtype),
        in_specs=[pl.BlockSpec(memory_space=pltpu.VMEM)],
        out_specs=pl.BlockSpec(memory_space=pltpu.VMEM),
        scratch_shapes=[
            pltpu.VMEM(piece, value.dtype),
            pltpu.VMEM(piece[1:], value.dtype),
            pltpu.VMEM(piece, value.dtype),
            sems,
            sems,
            sems,
            sems,
        ],
        cost_estimate=pl.CostEstimate(
            flops=value.size * 40000, bytes_accessed=value.size * 300, transcendentals=0
        ),
        compiler_params=pltpu.CompilerParams(collective_id=call, has_side_effects=True),
        name=f"tp_sum_{call}",
    )(value)


def small_kernel(axes, sizes, peers, x_ref, out_ref, parts, send, recv):
    greet(axes, sizes, peers)
    copies = []
    for distance in range(1, peers + 1):
        copy = pltpu.make_async_remote_copy(
            src_ref=x_ref,
            dst_ref=parts.at[distance - 1],
            send_sem=send.at[distance - 1],
            recv_sem=recv.at[distance - 1],
            device_id=peer_of(axes, sizes, distance),
            device_id_type=pl.DeviceIdType.MESH,
        )
        copy.start()
        copies.append(copy)
    flat = 0
    for axis, size in zip(axes, sizes):
        flat = flat * size + lax.axis_index(axis)
    for copy in copies:
        copy.wait()
    parts[peers] = x_ref[...]
    total = jnp.zeros(x_ref.shape, jnp.float32)
    for owner in range(peers + 1):
        slot = lax.rem(flat + 2 * (peers + 1) - owner - 1, peers + 1)
        total = total + parts[slot]
    out_ref[...] = total


def small_sum(value, axes, call):
    sizes = tuple(lax.axis_size(axis) for axis in axes)
    peers = 1
    for size in sizes:
        peers = peers * size
    peers = peers - 1
    if peers == 0:
        return value
    return pl.pallas_call(
        partial(small_kernel, axes, sizes, peers),
        out_shape=jax.ShapeDtypeStruct(value.shape, value.dtype),
        in_specs=[pl.BlockSpec(memory_space=pltpu.VMEM)],
        out_specs=pl.BlockSpec(memory_space=pltpu.VMEM),
        scratch_shapes=[
            pltpu.VMEM((peers + 1,) + value.shape, value.dtype),
            pltpu.SemaphoreType.DMA((peers,)),
            pltpu.SemaphoreType.DMA((peers,)),
        ],
        cost_estimate=pl.CostEstimate(
            flops=1000000, bytes_accessed=20000000, transcendentals=0
        ),
        compiler_params=pltpu.CompilerParams(collective_id=call, has_side_effects=True),
        name=f"small_sum_{call}",
    )(value)


def passed_along(value, axis, by):
    devices = lax.axis_size(axis)
    pairs = [(i, i + by) for i in range(devices) if 0 <= i + by < devices]
    return lax.ppermute(value, axis, pairs)


EDGE = 16


def halves(value):
    high = value.astype(jnp.bfloat16)
    low = (value - high.astype(jnp.float32)).astype(jnp.bfloat16)
    return high, low


def product(left, right, over=(1, 0)):
    dims = (((over[0],), (over[1],)), ((), ()))

    def one(a, b):
        return lax.dot_general(a, b, dims, preferred_element_type=jnp.float32)

    return one(left[0], right[0]) + (one(left[0], right[1]) + one(left[1], right[0]))


def exact_sum(ones, value, over=(1, 0)):
    dims = (((over[0],), (over[1],)), ((), ()))
    high = value.astype(jnp.bfloat16)
    rest = value - high.astype(jnp.float32)
    middle = rest.astype(jnp.bfloat16)
    low = (rest - middle.astype(jnp.float32)).astype(jnp.bfloat16)
    total = None
    for part in (low, middle, high):
        term = lax.dot_general(ones, part, dims, preferred_element_type=jnp.float32)
        total = term if total is None else total + term
    return total


def logistic(value):
    return 1.0 / (1.0 + jnp.exp(-value))


def row_sum(value):
    return jnp.sum(value, axis=1, keepdims=True)


def iotas(count):
    row = lax.broadcasted_iota(jnp.int32, (count, count), 0)
    col = lax.broadcasted_iota(jnp.int32, (count, count), 1)
    return row, col


def in_lane(lane, index, column):
    return jnp.where(lane == index, column, 0.0)


def lower_inverse_of(lower, row, col):
    order = lower.shape[0]
    apart = row ^ col
    inverse = jnp.where(row == col, 1.0, 0.0) - jnp.where(apart == 1, lower, 0.0)
    level = 1
    while (1 << level) < order:
        cross = jnp.where((apart >> level) == 1, lower, 0.0)
        both = halves(inverse)
        inverse = inverse - product(both, halves(product(halves(cross), both)))
        level += 1
    return inverse


def head_params(params_ref, tail, heads, lane):
    softened = tail + params_ref[1:2, :]
    soft = jnp.maximum(softened, 0.0) + jnp.log1p(jnp.exp(-jnp.abs(softened)))
    rate = jnp.where(lane < heads, -jnp.exp(params_ref[0:1, :]) * soft, 0.0)
    return rate, softened


def enter_kernel(
    heads,
    key_dim,
    chained,
    proj_ref,
    edge_ref,
    same_ref,
    taps_ref,
    params_ref,
    conv_ref,
    query_ref,
    key_ref,
    decay_ref,
    gram_ref,
    score_ref,
    inverse_ref,
    from_key_ref,
    from_value_ref,
    carried_ref,
    local_ref,
    offset_ref,
    cols_ref,
    *rest,
):
    ext = rest[-1]
    rows, conv_cols = conv_ref.shape
    query_cols = heads * key_dim
    value_dim = from_value_ref.shape[2]
    ext[0:EDGE, :] = edge_ref[...].astype(jnp.float32)
    ext[EDGE : EDGE + rows, :] = (
        proj_ref[:, 0:conv_cols].astype(jnp.bfloat16).astype(jnp.float32)
    )
    convolved = taps_ref[0:1, :] * ext[EDGE : EDGE + rows, :]
    for lag in range(1, taps_ref.shape[0]):
        convolved = convolved + taps_ref[lag : lag + 1, :] * (
            ext[EDGE - lag : EDGE - lag + rows, :] * same_ref[:, lag : lag + 1]
        )
    conv_ref[...] = convolved
    conv_ref.send()
    lane = lax.broadcasted_iota(jnp.int32, (rows, LANES), 1)
    row, col = iotas(rows)
    tail = proj_ref[:, conv_cols + heads * value_dim :]
    rate, _ = head_params(params_ref, tail, heads, lane)
    beta_all = logistic(tail)
    summed_in = rate + in_lane(lane, heads, 1.0 - same_ref[:, 1:2])
    until = jnp.where(col <= row, 1.0, 0.0).astype(jnp.bfloat16)
    total = exact_sum(until, summed_in)
    total_rows = total.T
    counted = total[:, heads : heads + 1]
    same = (jnp.abs(counted - total_rows[heads : heads + 1, :]) < 0.5) & (col <= row)
    strict = same & (col < row)
    first = jnp.where(counted < 0.5, 1.0, 0.0)
    cols = jnp.zeros((rows, LANES), jnp.float32)
    for head in range(heads):
        keys_at = slice(head * key_dim, (head + 1) * key_dim)
        queries = convolved[:, keys_at]
        queries = queries * logistic(queries)
        queries = (
            queries * lax.rsqrt(row_sum(queries * queries) + EPSILON) * key_dim ** (-0.5)
        )
        keys = convolved[:, query_cols + head * key_dim : query_cols + (head + 1) * key_dim]
        keys = keys * logistic(keys)
        keys = keys * lax.rsqrt(row_sum(keys * keys) + EPSILON)
        base = 2 * query_cols + head * value_dim
        values = convolved[:, base : base + value_dim]
        values = values * logistic(values)
        query_ref[:, keys_at] = queries
        key_ref[:, keys_at] = keys
        cumulative = total[:, head : head + 1]
        spread = cumulative - total_rows[head : head + 1, :]
        decay = jnp.where(same, jnp.exp(jnp.where(same, spread, 0.0)), 0.0)
        anchor = jnp.exp(cumulative) * first
        beta = beta_all[:, heads + head : heads + head + 1]
        decay_ref[head] = decay
        key_parts = halves(keys)
        gram = jnp.where(strict, product(key_parts, key_parts, (1, 1)) * decay, 0.0)
        gram_ref[head] = gram
        score = product(halves(queries), key_parts, (1, 1)) * decay
        score_ref[head] = score
        inverse = lower_inverse_of(beta * gram, row, col)
        inverse_ref[head] = inverse
        inverse_parts = halves(inverse)
        from_key = product(inverse_parts, halves((-beta * anchor) * keys))
        from_value = product(inverse_parts, halves(beta * values))
        from_key_ref[head] = from_key
        from_value_ref[head] = from_value
        score_parts = halves(score)
        value_parts = halves(from_value)
        from_key_parts = halves(from_key)
        carried_ref[head] = product(score_parts, from_key_parts) + anchor * queries
        local_ref[head] = product(score_parts, value_parts)
        last_count = counted[rows - 1 : rows, :]
        last_total = cumulative[rows - 1 : rows, :]
        matches = jnp.abs(counted - last_count) < 0.5
        closing = jnp.where(
            matches, jnp.exp(jnp.where(matches, last_total - cumulative, 0.0)), 0.0
        )
        closed = halves(closing * keys)
        offset_ref[head] = product(closed, value_parts, (0, 0))
        if chained:
            transfer_row, transfer_col = iotas(key_dim)
            rest[0][head] = product(closed, from_key_parts, (0, 0)) + jnp.where(
                transfer_row == transfer_col, anchor[rows - 1 : rows, :], 0.0
            )
        cols = (
            cols
            + in_lane(lane, head, anchor)
            + in_lane(lane, heads + head, beta)
            + in_lane(lane, 2 * heads + head, closing)
        )
        made = [decay_ref, gram_ref, score_ref, inverse_ref, from_key_ref]
        made += [from_value_ref, carried_ref, local_ref, offset_ref]
        for ref in made + list(rest[:-1]):
            ref.send(head)
    cols_ref[...] = cols


def leave_kernel(
    heads,
    carried_ref,
    local_ref,
    initial_ref,
    proj_ref,
    gain_ref,
    y_ref,
    mixed_ref,
):
    rows = y_ref.shape[0]
    value_dim = local_ref.shape[2]
    first_col = proj_ref.shape[1] - LANES - heads * value_dim
    for head in range(heads):
        at = slice(head * value_dim, (head + 1) * value_dim)
        mixed = local_ref[head] + product(
            halves(carried_ref[head]), halves(initial_ref[head])
        )
        mixed_ref[:, at] = mixed
        scale = lax.rsqrt(row_sum(mixed * mixed) / value_dim + EPSILON)
        gate = proj_ref[:, first_col + head * value_dim : first_col + (head + 1) * value_dim]
        y_ref[:, at] = (
            mixed * scale * gain_ref[...] * (gate * logistic(gate))
        ).astype(jnp.bfloat16)


def leave_back_kernel(
    heads,
    d_y_ref,
    mixed_ref,
    proj_ref,
    gain_ref,
    carried_ref,
    d_mixed_ref,
    d_gate_ref,
    d_gain_ref,
    d_initial_ref,
):
    rows = d_y_ref.shape[0]
    value_dim = d_mixed_ref.shape[1] // heads
    first_col = proj_ref.shape[1] - LANES - heads * value_dim
    d_gain = jnp.zeros((1, value_dim), jnp.float32)
    for head in range(heads):
        at = slice(head * value_dim, (head + 1) * value_dim)
        mixed = mixed_ref[:, at]
        scale = lax.rsqrt(row_sum(mixed * mixed) / value_dim + EPSILON)
        normed = mixed * scale
        gate = proj_ref[:, first_col + head * value_dim : first_col + (head + 1) * value_dim]
        sigma = logistic(gate)
        d_y = d_y_ref[:, at]
        d_gain = d_gain + jnp.sum(d_y * normed * (gate * sigma), axis=0, keepdims=True)
        scaled = d_y * gain_ref[...]
        d_gate_ref[:, at] = (
            scaled * normed * (sigma * (1.0 + gate * (1.0 - sigma)))
        ).astype(jnp.bfloat16)
        d_normed = scaled * (gate * sigma)
        d_mixed = scale * (d_normed - normed * (row_sum(d_normed * normed) / value_dim))
        d_mixed_ref[:, at] = d_mixed
        d_initial_ref[head] = product(
            halves(carried_ref[head]), halves(d_mixed), (0, 0)
        )
    d_gain_ref[...] = jnp.broadcast_to(d_gain, d_gain_ref.shape)


def enter_back_kernel(
    heads,
    key_dim,
    d_mixed_ref,
    d_gate_ref,
    d_end_ref,
    initial_ref,
    proj_ref,
    edge_ref,
    same_ref,
    taps_ref,
    params_ref,
    conv_ref,
    query_ref,
    key_ref,
    decay_ref,
    gram_ref,
    score_ref,
    inverse_ref,
    from_key_ref,
    from_value_ref,
    cols_ref,
    d_proj_ref,
    d_last_ref,
    d_edge_ref,
    d_taps_ref,
    d_params_ref,
    ext,
    d_ext,
):
    rows, conv_cols = conv_ref.shape
    query_cols = heads * key_dim
    value_dim = from_value_ref.shape[2]
    value_cols = heads * value_dim
    margin = taps_ref.shape[0]
    lane = lax.broadcasted_iota(jnp.int32, (rows, LANES), 1)
    row, col = iotas(rows)
    last_row = lax.broadcasted_iota(jnp.int32, (rows, 1), 0) == rows - 1
    d_total = jnp.zeros((rows, LANES), jnp.float32)
    d_tail = jnp.zeros((rows, LANES), jnp.float32)
    d_active = []
    for head in range(heads):
        keys_at = slice(head * key_dim, (head + 1) * key_dim)
        queries, keys = query_ref[:, keys_at], key_ref[:, keys_at]
        base = 2 * query_cols + head * value_dim
        values = conv_ref[:, base : base + value_dim]
        values = values * logistic(values)
        anchor = cols_ref[:, head : head + 1]
        beta = cols_ref[:, heads + head : heads + head + 1]
        closing = cols_ref[:, 2 * heads + head : 2 * heads + head + 1]
        decay, gram, score = decay_ref[head], gram_ref[head], score_ref[head]
        initial = initial_ref[head]
        d_end = d_end_ref[head]
        d_mixed = d_mixed_ref[:, head * value_dim : (head + 1) * value_dim]
        initial_parts, end_parts = halves(initial), halves(d_end)
        mixed_parts = halves(d_mixed)
        key_parts, query_parts = halves(keys), halves(queries)
        updates = from_value_ref[head] + product(halves(from_key_ref[head]), initial_parts)
        update_parts = halves(updates)
        key_state = product(key_parts, initial_parts)
        query_state = product(query_parts, initial_parts)
        d_updates = product(halves(score), mixed_parts, (0, 0)) + product(
            halves(closing * keys), end_parts
        )
        d_target = product(halves(inverse_ref[head]), halves(d_updates), (0, 0))
        d_delta = beta * d_target
        delta = values - anchor * key_state
        d_lower = -product(halves(d_target), update_parts, (1, 1))
        d_score = product(mixed_parts, update_parts, (1, 1))
        d_pair = halves(d_score * decay)
        d_lower_gram = d_lower * gram
        d_beta = row_sum(d_target * delta) + row_sum(d_lower_gram)
        d_gram = halves(jnp.where(col < row, d_lower * (beta * decay), 0.0))
        back = halves(anchor * d_delta)
        d_query = product(d_pair, key_parts) + anchor * product(
            mixed_parts, initial_parts, (1, 1)
        )
        d_closed = product(update_parts, end_parts, (1, 1))
        d_key = (
            product(d_pair, query_parts, (0, 0))
            + product(d_gram, key_parts)
            + product(d_gram, key_parts, (0, 0))
            + closing * d_closed
            - product(back, initial_parts, (1, 1))
        )
        d_anchor = row_sum(d_mixed * query_state) - row_sum(d_delta * key_state)
        d_anchor = d_anchor + jnp.where(last_row, jnp.sum(d_end * initial), 0.0)
        d_closing = closing * row_sum(keys * d_closed)
        flow = d_score * score + beta * d_lower_gram
        into = jnp.broadcast_to(jnp.sum(flow, axis=0, keepdims=True), (LANES, rows)).T
        d_cumulative = row_sum(flow) - into[:, 0:1] + anchor * d_anchor - d_closing
        d_cumulative = d_cumulative + jnp.where(last_row, jnp.sum(d_closing), 0.0)
        d_total = d_total + in_lane(lane, head, d_cumulative)
        d_tail = d_tail + in_lane(lane, heads + head, d_beta * beta * (1.0 - beta))
        raw_query = conv_ref[:, keys_at]
        raw_key = conv_ref[:, query_cols + head * key_dim : query_cols + (head + 1) * key_dim]
        query_sigma, key_sigma = logistic(raw_query), logistic(raw_key)
        active = raw_query * query_sigma
        scale = lax.rsqrt(row_sum(active * active) + EPSILON)
        unit = active * scale
        d_unit = d_query * key_dim ** (-0.5)
        d_raw_query = (
            scale
            * (d_unit - unit * row_sum(d_unit * unit))
            * (query_sigma * (1.0 + raw_query * (1.0 - query_sigma)))
        )
        active = raw_key * key_sigma
        scale = lax.rsqrt(row_sum(active * active) + EPSILON)
        d_raw_key = (
            scale
            * (d_key - keys * row_sum(d_key * keys))
            * (key_sigma * (1.0 + raw_key * (1.0 - key_sigma)))
        )
        raw_value = conv_ref[:, base : base + value_dim]
        value_sigma = logistic(raw_value)
        d_raw_value = d_delta * (value_sigma * (1.0 + raw_value * (1.0 - value_sigma)))
        d_active.append((d_raw_query, d_raw_key, d_raw_value))
    tail = proj_ref[:, conv_cols + value_cols :]
    rate, softened = head_params(params_ref, tail, heads, lane)
    since = jnp.where(col >= row, 1.0, 0.0).astype(jnp.bfloat16)
    d_rate = exact_sum(since, d_total)
    d_decay = jnp.where(
        lane < heads, d_rate * (-jnp.exp(params_ref[0:1, :])) * logistic(softened), 0.0
    )
    d_params_ref[0:1, :] = jnp.sum(d_rate * rate, axis=0, keepdims=True)
    d_params_ref[1:2, :] = jnp.sum(d_decay, axis=0, keepdims=True)
    d_params_ref[2:, :] = jnp.zeros((d_params_ref.shape[0] - 2, LANES), jnp.float32)
    d_proj_ref[:, conv_cols + value_cols :] = (d_decay + d_tail).astype(jnp.bfloat16)
    d_proj_ref[:, conv_cols : conv_cols + value_cols] = d_gate_ref[...]
    d_convolved = jnp.concatenate(
        [part[0] for part in d_active]
        + [part[1] for part in d_active]
        + [part[2] for part in d_active],
        axis=1,
    )
    ext[0:EDGE, :] = edge_ref[...].astype(jnp.float32)
    ext[EDGE : EDGE + rows, :] = (
        proj_ref[:, 0:conv_cols].astype(jnp.bfloat16).astype(jnp.float32)
    )
    zeros = jnp.zeros((EDGE, conv_cols), jnp.float32)
    d_ext[0:EDGE, :] = zeros
    d_ext[EDGE + rows :, :] = zeros
    d_taps_ref[...] = jnp.zeros(d_taps_ref.shape, jnp.float32)
    d_taps_ref[0:1, :] = jnp.sum(
        d_convolved * ext[EDGE : EDGE + rows, :], axis=0, keepdims=True
    )
    d_pre = taps_ref[0:1, :] * d_convolved
    d_edge = zeros
    for lag in range(1, margin):
        kept = d_convolved * same_ref[:, lag : lag + 1]
        d_taps_ref[lag : lag + 1, :] = jnp.sum(
            kept * ext[EDGE - lag : EDGE - lag + rows, :], axis=0, keepdims=True
        )
        d_ext[EDGE : EDGE + rows, :] = kept
        weight = taps_ref[lag : lag + 1, :]
        d_pre = d_pre + weight * d_ext[EDGE + lag : EDGE + lag + rows, :]
        d_edge = d_edge + weight * d_ext[lag : lag + EDGE, :]
    d_proj_ref[:, 0:conv_cols] = d_pre.astype(jnp.bfloat16)
    d_last_ref[...] = d_pre[rows - EDGE :, :]
    d_edge_ref[...] = d_edge


MIB = 1024 * 1024


class Arriving:
    def __init__(self, ref, buf, sem):
        self.buf, self.copy, self.here = buf, pltpu.make_async_copy(ref, buf, sem), False
        self.shape, self.dtype = buf.shape, buf.dtype
        self.copy.start()

    def settle(self):
        if not self.here:
            self.copy.wait()
            self.here = True

    def __getitem__(self, index):
        self.settle()
        return self.buf[index]


class Leaving:
    def __init__(self, ref, buf, sems, first):
        self.ref, self.buf, self.sems, self.first, self.copies = ref, buf, sems, first, []
        self.shape, self.dtype = buf.shape, buf.dtype

    def __getitem__(self, index):
        return self.buf[index]

    def __setitem__(self, index, value):
        self.buf[index] = value

    def send(self, part=None):
        source = self.buf if part is None else self.buf.at[part]
        target = self.ref if part is None else self.ref.at[part]
        sem = self.sems.at[self.first + len(self.copies)]
        self.copies.append(pltpu.make_async_copy(source, target, sem))
        self.copies[-1].start()

    def end(self):
        if not self.copies:
            self.send()
        for copy in self.copies:
            copy.wait()


PARTS = 4


def staged(kernel, ins, outs):
    def body(*refs):
        sems = refs[-1]
        given, made = refs[:ins], refs[ins : ins + outs]
        bufs = refs[ins + outs : 2 * (ins + outs)]
        arriving = [Arriving(given[i], bufs[i], sems.at[i]) for i in range(ins)]
        leaving = [
            Leaving(made[i], bufs[ins + i], sems, ins + PARTS * i) for i in range(outs)
        ]
        kernel(*arriving, *leaving, *refs[2 * (ins + outs) : -1])
        for member in arriving:
            member.settle()
        for member in leaving:
            member.end()

    return body


def on_core(kernel, name, shapes, scratch=()):
    def call(*args):
        made = [jax.ShapeDtypeStruct(shape, dtype) for shape, dtype in shapes]
        count = len(args) + len(made)
        return pl.pallas_call(
            staged(kernel, len(args), len(made)),
            out_shape=made,
            in_specs=[pl.BlockSpec(memory_space=pl.ANY)] * len(args),
            out_specs=[pl.BlockSpec(memory_space=pl.ANY)] * len(made),
            scratch_shapes=[pltpu.VMEM(x.shape, x.dtype) for x in (*args, *made)]
            + [pltpu.VMEM(shape, dtype) for shape, dtype in scratch]
            + [pltpu.SemaphoreType.DMA((len(args) + PARTS * len(made),))],
            compiler_params=pltpu.CompilerParams(vmem_limit_bytes=56 * MIB),
            name=name,
        )(*args)

    return call


MESH = pl.DeviceIdType.MESH


class Links:
    def __init__(self, send, recv):
        self.send, self.recv, self.used = send, recv, 0

    def take(self, count=1):
        first = self.used
        self.used = first + count
        return first

    def copy(self, index, source, target, where):
        return pltpu.make_async_remote_copy(
            src_ref=source,
            dst_ref=target,
            send_sem=self.send.at[index],
            recv_sem=self.recv.at[index],
            device_id=where,
            device_id_type=MESH,
        )


def meet(places):
    barrier = pltpu.get_barrier_semaphore()
    for place in places:
        pl.semaphore_signal(barrier, inc=1, device_id=place, device_id_type=MESH)
    pl.semaphore_wait(barrier, len(places))


def flipped(index, bit):
    step = 1 << bit
    return index + step - 2 * step * lax.rem(index // step, 2)


def line_places(axis):
    me = lax.axis_index(axis)
    return [{axis: lax.rem(me + distance, 4)} for distance in range(1, 4)]


class LineSum:
    def __init__(self, axis, pieces, x_ref, out_ref, bufs, links):
        self.pieces, self.x_ref, self.out_ref, self.links = pieces, x_ref, out_ref, links
        self.from_end, self.to_mate, self.from_mate, self.keep = bufs
        me = lax.axis_index(axis)
        self.inner = (me == 1) | (me == 2)
        self.partner = {axis: flipped(me, 0)}
        self.mate = {axis: 3 - me}
        self.mine = me // 2
        self.size = x_ref.shape[0] // pieces
        self.half = self.size // 2
        self.ends = links.take(pieces)
        self.pairs = links.take(pieces)
        self.totals = links.take(pieces)
        self.backs = links.take(pieces)
        self.others = links.take(pieces)

    def rows(self, piece, part):
        start = piece * self.size + part * self.half
        return pl.ds(pl.multiple_of(start, self.half), self.half)

    def end_copy(self, piece):
        return self.links.copy(
            self.ends + piece,
            self.x_ref.at[pl.ds(piece * self.size, self.size)],
            self.from_end.at[piece],
            self.partner,
        )

    def pair_copy(self, piece):
        return self.links.copy(
            self.pairs + piece, self.to_mate.at[piece], self.from_mate.at[piece], self.mate
        )

    def out_copy(self, base, piece, part, where):
        ref = self.out_ref.at[self.rows(piece, part)]
        return self.links.copy(base + piece, ref, ref, where)

    def start(self, piece):
        @pl.when(jnp.logical_not(self.inner))
        def _():
            self.end_copy(piece).start()

    def first(self, piece):
        @pl.when(self.inner)
        def _():
            self.end_copy(piece).wait_recv()
            arrived = self.from_end.at[piece]

            def pair(part):
                at = pl.ds(pl.multiple_of(part * self.half, self.half), self.half)
                return self.x_ref[self.rows(piece, part)].astype(jnp.float32) + arrived[
                    at
                ].astype(jnp.float32)

            self.to_mate[piece] = pair(1 - self.mine).astype(self.to_mate.dtype)
            self.pair_copy(piece).start()
            self.keep[piece] = pair(self.mine)

    def second(self, piece):
        @pl.when(self.inner)
        def _():
            self.pair_copy(piece).wait_recv()
            total = self.keep[piece] + self.from_mate[piece].astype(jnp.float32)
            self.out_ref[self.rows(piece, self.mine)] = total.astype(self.out_ref.dtype)
            self.out_copy(self.totals, piece, self.mine, self.mate).start()
            self.out_copy(self.backs, piece, self.mine, self.partner).start()

    def third(self, piece):
        @pl.when(self.inner)
        def _():
            self.out_copy(self.totals, piece, 1 - self.mine, self.mate).wait_recv()
            self.out_copy(self.others, piece, 1 - self.mine, self.partner).start()

    def step(self, number):
        if number < self.pieces:
            self.first(number)
        if 0 <= number - 1 < self.pieces:
            self.second(number - 1)
        if 0 <= number - 2 < self.pieces:
            self.third(number - 2)

    def steps(self):
        return self.pieces + 2

    def ready(self, piece):
        @pl.when(jnp.logical_not(self.inner))
        def _():
            self.out_copy(self.backs, piece, self.mine, self.partner).wait_recv()
            self.out_copy(self.others, piece, 1 - self.mine, self.partner).wait_recv()

    def finish(self):
        @pl.when(self.inner)
        def _():
            for piece in range(self.pieces):
                self.pair_copy(piece).wait_send()
                self.out_copy(self.totals, piece, self.mine, self.mate).wait_send()
                self.out_copy(self.backs, piece, self.mine, self.partner).wait_send()
                self.out_copy(self.others, piece, 1 - self.mine, self.partner).wait_send()

        @pl.when(jnp.logical_not(self.inner))
        def _():
            for piece in range(self.pieces):
                self.end_copy(piece).wait_send()


def line_buffers(pieces, shape, dtype):
    size = shape[0] // pieces
    return [
        pltpu.VMEM((pieces, size, shape[1]), dtype),
        pltpu.VMEM((pieces, size // 2, shape[1]), dtype),
        pltpu.VMEM((pieces, size // 2, shape[1]), dtype),
        pltpu.VMEM((pieces, size // 2, shape[1]), jnp.float32),
    ]


def line_kernel(axis, pieces, x_ref, out_ref, *rest):
    links = Links(rest[4], rest[5])
    meet(line_places(axis))
    line = LineSum(axis, pieces, x_ref, out_ref, rest[:4], links)
    for piece in range(pieces):
        line.start(piece)
    for number in range(line.steps()):
        line.step(number)
    for piece in range(pieces):
        line.ready(piece)
    line.finish()


def in_vmem(count):
    return [pl.BlockSpec(memory_space=pltpu.VMEM)] * count


def line_summed(value, axis, call, pieces):
    sems = pltpu.SemaphoreType.DMA((5 * pieces,))
    return pl.pallas_call(
        partial(line_kernel, axis, pieces),
        out_shape=jax.ShapeDtypeStruct(value.shape, value.dtype),
        in_specs=in_vmem(1),
        out_specs=in_vmem(1)[0],
        scratch_shapes=line_buffers(pieces, value.shape, value.dtype) + [sems, sems],
        cost_estimate=pl.CostEstimate(
            flops=value.size * 40000, bytes_accessed=value.size * 300, transcendentals=0
        ),
        compiler_params=pltpu.CompilerParams(
            collective_id=call, has_side_effects=True, vmem_limit_bytes=8 * MIB
        ),
        name=f"tp_line_{call}",
    )(value)


def square_places(axes):
    first, second = axes
    where, core = lax.axis_index(first), lax.axis_index(second)
    sibling = {second: 1 - core}
    beside = {first: flipped(where, 0)}
    across = {first: flipped(where, 1)}
    return where, core, sibling, beside, across


class SquareGather:
    def __init__(self, axes, out_refs, links):
        self.where, self.core, self.sibling, self.beside, self.across = square_places(axes)
        self.outs, self.links = out_refs, links
        self.rows = out_refs[0].shape[0] // 8
        begin = (self.where * 2 + self.core) * self.rows
        self.mine = pl.ds(pl.multiple_of(begin, self.rows), self.rows)
        self.started, self.siblings = [], []

    def go(self, out_ref, flip, place, start=0, size=None):
        size = size or self.rows
        owner = self.where
        for bit in range(2):
            if flip >> bit & 1:
                owner = flipped(owner, bit)
        begin = (owner * 2 + self.core) * self.rows + start
        ref = out_ref.at[pl.ds(pl.multiple_of(begin, size), size)]
        copy = self.links.copy(self.links.take(), ref, ref, place)
        copy.start()
        self.started.append(copy)
        return copy

    def start(self):
        self.from_beside, self.from_across, self.upper, self.lower = [], [], [], []
        for out_ref in self.outs:
            self.from_beside.append(self.go(out_ref, 0, self.beside))
            self.from_across.append(self.go(out_ref, 0, self.across))
        for out_ref in self.outs:
            self.siblings.append(self.go(out_ref, 0, self.sibling))

    def forward(self, number):
        out_ref, half = self.outs[number], self.rows // 2
        self.from_beside[number].wait_recv()
        self.upper.append(self.go(out_ref, 1, self.across, 0, half))
        self.siblings.append(self.go(out_ref, 1, self.sibling))
        self.from_across[number].wait_recv()
        self.lower.append(self.go(out_ref, 2, self.beside, half, half))
        self.siblings.append(self.go(out_ref, 2, self.sibling))

    def last(self, number):
        out_ref, half = self.outs[number], self.rows // 2
        self.upper[number].wait_recv()
        self.siblings.append(self.go(out_ref, 3, self.sibling, 0, half))
        self.lower[number].wait_recv()
        self.siblings.append(self.go(out_ref, 3, self.sibling, half, half))

    def finish(self):
        for copy in self.siblings:
            copy.wait_recv()
        for copy in self.started:
            copy.wait_send()

    def places(self):
        return [self.sibling, self.beside, self.across]


def gather_kernel(axes, groups, tail_cols, *refs):
    count = sum(len(splits) for splits in groups)
    parts, tail_ref = refs[:count], refs[count]
    outs, gains_ref = refs[count + 1 : count + 1 + len(groups)], refs[count + 1 + len(groups)]
    local, send, recv = refs[-3:]
    gather = SquareGather(axes, outs, Links(send, recv))
    mine, rows = gather.mine, gather.rows
    fills = []
    for splits, out_ref in zip(groups, outs):
        at = 0
        for width in splits:
            source = parts[len(fills)]
            target = out_ref.at[mine, pl.ds(at, width)]
            fills.append(pltpu.make_async_copy(source, target, local.at[len(fills)]))
            fills[-1].start()
            at += width
    tail_at = slice(outs[0].shape[1] - tail_cols, outs[0].shape[1])
    outs[0][mine, tail_at] = tail_ref[...].astype(jnp.float32).T.astype(jnp.bfloat16)
    meet(gather.places())
    for fill in fills:
        fill.wait()
    gather.start()
    for number in range(len(outs)):
        gather.forward(number)
    for number in range(len(outs)):
        gather.last(number)
    gather.finish()
    gains_ref[...] = outs[0][:, tail_at].astype(jnp.float32).T[0 : gains_ref.shape[0]]


def gathered(groups, tail_rows, axes, call):
    rows = groups[0][0].shape[0]
    tail_cols = tail_rows.shape[0]
    splits = tuple(tuple(part.shape[1] for part in group) for group in groups)
    widths = [sum(split) for split in splits]
    widths[0] += tail_cols
    sems = pltpu.SemaphoreType.DMA((9 * len(groups),))
    parts = [part for group in groups for part in group]
    anywhere = pl.BlockSpec(memory_space=pl.ANY)
    return pl.pallas_call(
        partial(gather_kernel, axes, splits, tail_cols),
        out_shape=[
            jax.ShapeDtypeStruct((8 * rows, width), jnp.bfloat16) for width in widths
        ]
        + [jax.ShapeDtypeStruct((8, 8 * rows), jnp.float32)],
        in_specs=[anywhere] * len(parts) + in_vmem(1),
        out_specs=in_vmem(len(groups) + 1),
        scratch_shapes=[pltpu.SemaphoreType.DMA((len(parts),)), sems, sems],
        cost_estimate=pl.CostEstimate(
            flops=10000000000, bytes_accessed=60000000, transcendentals=0
        ),
        compiler_params=pltpu.CompilerParams(
            collective_id=call, has_side_effects=True, vmem_limit_bytes=16 * MIB
        ),
        name=f"weights_{call}",
    )(*parts, tail_rows)


class SquareSum:
    def __init__(self, axes, g_ref, columns, out_ref, bufs, links):
        self.where, self.core, self.sibling, self.beside, self.across = square_places(axes)
        self.g_ref, self.out_ref, self.columns, self.links = g_ref, out_ref, columns, links
        self.from_core, self.sums, self.from_chip, self.ends = bufs
        self.rows = g_ref.shape[0] // 8
        self.half = self.rows // 2
        self.core_ids = links.take(4)
        self.chip_ids = links.take(4)
        self.end_ids = links.take(2)

    def block(self, flip, of_core):
        owner = self.where
        for bit in range(2):
            if flip >> bit & 1:
                owner = flipped(owner, bit)
        begin = (owner * 2 + of_core) * self.rows
        return pl.ds(pl.multiple_of(begin, self.rows), self.rows)

    def core_copy(self, flip):
        return self.links.copy(
            self.core_ids + flip,
            self.g_ref.at[self.block(flip, 1 - self.core), self.columns],
            self.from_core.at[flip],
            self.sibling,
        )

    def chip_copy(self, slot):
        flip, start, where = (
            (1, 0, self.beside),
            (3, 0, self.beside),
            (2, self.half, self.across),
            (3, self.half, self.across),
        )[slot]
        return self.links.copy(
            self.chip_ids + slot,
            self.sums.at[flip, pl.ds(start, self.half)],
            self.from_chip.at[slot],
            where,
        )

    def end_copy(self, slot):
        flip, start, where = ((2, 0, self.across), (1, self.half, self.beside))[slot]
        return self.links.copy(
            self.end_ids + slot,
            self.sums.at[flip, pl.ds(start, self.half)],
            self.ends.at[slot],
            where,
        )

    def start(self):
        for flip in (3, 1, 2, 0):
            self.core_copy(flip).start()

    def add_core(self, flip):
        self.core_copy(flip).wait_recv()
        own = self.g_ref[self.block(flip, self.core), self.columns].astype(jnp.float32)
        self.sums[flip] = (own + self.from_core[flip].astype(jnp.float32)).astype(
            self.sums.dtype
        )

    def first(self):
        self.add_core(3)
        self.chip_copy(1).start()
        self.chip_copy(3).start()
        self.add_core(1)
        self.chip_copy(0).start()
        self.add_core(2)
        self.chip_copy(2).start()
        self.core_copy(0).wait_recv()

    def second(self):
        half = self.half
        self.chip_copy(1).wait_recv()
        self.sums[2, 0:half] = (
            self.sums[2, 0:half].astype(jnp.float32) + self.from_chip[1].astype(jnp.float32)
        ).astype(self.sums.dtype)
        self.end_copy(0).start()
        self.chip_copy(3).wait_recv()
        self.sums[1, half:] = (
            self.sums[1, half:].astype(jnp.float32) + self.from_chip[3].astype(jnp.float32)
        ).astype(self.sums.dtype)
        self.end_copy(1).start()

    def third(self):
        half = self.half
        own = self.g_ref[self.block(0, self.core), self.columns].astype(jnp.float32)
        own = own + self.from_core[0].astype(jnp.float32)
        for slot, part in ((0, slice(0, half)), (1, slice(half, 2 * half))):
            self.chip_copy(2 * slot).wait_recv()
            self.end_copy(slot).wait_recv()
            self.out_ref[part, self.columns] = (
                own[part]
                + self.from_chip[2 * slot].astype(jnp.float32)
                + self.ends[slot].astype(jnp.float32)
            )

    def finish(self):
        for flip in range(4):
            self.core_copy(flip).wait_send()
        for slot in range(4):
            self.chip_copy(slot).wait_send()
        for slot in range(2):
            self.end_copy(slot).wait_send()


def square_buffers(rows, width):
    return [
        pltpu.VMEM((4, rows, width), jnp.bfloat16),
        pltpu.VMEM((4, rows, width), jnp.bfloat16),
        pltpu.VMEM((4, rows // 2, width), jnp.bfloat16),
        pltpu.VMEM((2, rows // 2, width), jnp.bfloat16),
    ]


def last_kernel(axes, axis, pieces, cuts, x_ref, g_ref, h_ref, small_ref, *rest):
    out_ref, g_out, h_out, small_out = rest[:4]
    line_bufs, rest = rest[4:8], rest[8:]
    square_bufs = [rest[4 * i : 4 * i + 4] for i in range(len(cuts))]
    small_bufs, send, recv = rest[-4:-2], rest[-2], rest[-1]
    where, core, sibling, beside, across = square_places(axes)
    me = lax.axis_index(axis)
    links = Links(send, recv)
    line = LineSum(axis, pieces, x_ref, out_ref, line_bufs, links)
    squares = [
        SquareSum(
            axes, (g_ref, h_ref)[which], pl.ds(begin, size), (g_out, h_out)[which], bufs, links
        )
        for (which, begin, size), bufs in zip(cuts, square_bufs)
    ]
    steps = [sibling, beside, across, {axis: flipped(me, 0)}, {axis: flipped(me, 1)}]
    ids = links.take(len(steps))
    here, there = small_bufs
    common = here.shape[1] // 2

    def small_copy(number):
        if number < 3:
            return links.copy(ids + number, here.at[number], there.at[number], steps[number])
        part = pl.ds(common, common)
        return links.copy(
            ids + number, here.at[number, part], there.at[number, part], steps[number]
        )

    def small_step(number):
        small_copy(number).wait_recv()
        if number < 3:
            here[number + 1] = here[number] + there[number]
        else:
            here[number + 1, common:] = here[number, common:] + there[number, common:]
        if number + 1 < len(steps):
            small_copy(number + 1).start()

    here[0] = small_ref[...]
    meet([sibling, beside, across] + line_places(axis))
    for piece in range(pieces):
        line.start(piece)
    squares[0].start()
    small_copy(0).start()
    for square in squares[1:]:
        square.start()
    for number in range(max(line.steps(), len(squares))):
        if number < len(squares):
            squares[number].first()
        if number < line.steps():
            line.step(number)
        if number < len(steps):
            small_step(number)
    for square in squares:
        square.second()
    for square in squares:
        square.third()
    for piece in range(pieces):
        line.ready(piece)
    line.finish()
    small_out[0:common, :] = here[3, 0:common]
    small_out[common:, :] = here[len(steps), common:]
    for square in squares:
        square.finish()
    for number in range(len(steps)):
        small_copy(number).wait_send()


def last_sums(value, grad_in, grad_out, small, axes, axis, call, pieces, cuts):
    rows = grad_in.shape[0] // 8
    count = 5 * pieces + 10 * len(cuts) + 5
    sems = pltpu.SemaphoreType.DMA((count,))
    scratch = line_buffers(pieces, value.shape, value.dtype)
    for _, _, size in cuts:
        scratch = scratch + square_buffers(rows, size)
    scratch = scratch + [
        pltpu.VMEM((6,) + small.shape, small.dtype),
        pltpu.VMEM((5,) + small.shape, small.dtype),
        sems,
        sems,
    ]
    return pl.pallas_call(
        partial(last_kernel, axes, axis, pieces, cuts),
        out_shape=[
            jax.ShapeDtypeStruct(value.shape, value.dtype),
            jax.ShapeDtypeStruct((rows, grad_in.shape[1]), jnp.float32),
            jax.ShapeDtypeStruct((rows, grad_out.shape[1]), jnp.float32),
            jax.ShapeDtypeStruct(small.shape, jnp.float32),
        ],
        in_specs=in_vmem(4),
        out_specs=in_vmem(4),
        scratch_shapes=scratch,
        cost_estimate=pl.CostEstimate(
            flops=20000000000, bytes_accessed=100000000, transcendentals=0
        ),
        compiler_params=pltpu.CompilerParams(
            collective_id=call, has_side_effects=True, vmem_limit_bytes=14 * MIB
        ),
        name=f"last_sums_{call}",
    )(value, grad_in, grad_out, small)


def middle_kernel(
    axis,
    pieces,
    group,
    y_ref,
    out_weight_ref,
    x_ref,
    d_out_ref,
    gain_ref,
    weight_ref,
    block_ref,
    d_middle_ref,
    d_mixed_ref,
    weight_grad_ref,
    out_grad_ref,
    gain_grad_ref,
    part,
    attention,
    two_part,
    two_sum,
    feed_part,
    feed_sum,
    middle,
    normed,
    scale,
    hidden,
    active,
    d_gate_ref,
    d_up_ref,
    d_active,
    *rest,
):
    rows, width = x_ref.shape
    units = weight_ref.shape[1] // 3
    size = rows // pieces
    gate_at, up_at, down_at = (slice(i * units, (i + 1) * units) for i in range(3))
    links = Links(rest[12], rest[13])
    lines = [
        LineSum(axis, pieces, source, target, rest[4 * i : 4 * i + 4], links)
        for i, (source, target) in enumerate(
            ((part, attention), (two_part, two_sum), (feed_part, feed_sum))
        )
    ]
    first, two, feed = lines

    def dot(left, right, over=(1, 0)):
        dims = (((over[0],), (over[1],)), ((), ()))
        return lax.dot_general(left, right, dims, preferred_element_type=jnp.float32)

    def rows_of(piece, count=1):
        return slice(piece * size, (piece + count) * size)

    meet(line_places(axis))
    for start in range(0, pieces, group):
        at = rows_of(start, group)
        part[at] = dot(y_ref[at], out_weight_ref[...], (1, 1)).astype(part.dtype)
        for piece in range(start, start + group):
            first.start(piece)
    d_active[...] = dot(d_out_ref[...], weight_ref[:, down_at])

    def feed_forward(start):
        at = rows_of(start, group)
        mid = x_ref[at].astype(jnp.float32) + attention[at].astype(jnp.float32)
        factor = lax.rsqrt(row_sum(mid * mid) / width + EPSILON)
        unit = mid * factor
        middle[at] = mid
        normed[at] = unit
        scale[at] = jnp.broadcast_to(factor, (group * size, LANES))
        inner = (unit * gain_ref[...]).astype(jnp.bfloat16)
        hidden[at] = inner
        gate = dot(inner, weight_ref[:, gate_at])
        up = dot(inner, weight_ref[:, up_at])
        sigma = logistic(gate)
        swish = gate * sigma
        act = (swish * up).astype(jnp.bfloat16)
        active[at] = act
        d_act = d_active[at]
        d_gate = (d_act * up * sigma * (1.0 + gate * (1.0 - sigma))).astype(jnp.bfloat16)
        d_up = (d_act * swish).astype(jnp.bfloat16)
        d_gate_ref[at] = d_gate
        d_up_ref[at] = d_up
        back = dot(d_gate, weight_ref[:, gate_at], (1, 1)) + dot(
            d_up, weight_ref[:, up_at], (1, 1)
        )
        two_part[at] = back.astype(two_part.dtype)
        for piece in range(start, start + group):
            two.start(piece)
        feed_part[at] = dot(act, weight_ref[:, down_at], (1, 1)).astype(feed_part.dtype)

    for number in range(first.steps()):
        first.step(number)
        if number >= 2:
            first.ready(number - 2)
            if (number - 1) % group == 0:
                feed_forward(number - 1 - group)
    for piece in range(pieces):
        feed.start(piece)

    def weight_grad(left, right, at):
        weight_grad_ref[:, at] = dot(left[...], right[...], (0, 0)).astype(jnp.bfloat16)

    works = [
        lambda: weight_grad(hidden, d_gate_ref, gate_at),
        lambda: weight_grad(hidden, d_up_ref, up_at),
        lambda: weight_grad(d_out_ref, active, down_at),
    ]
    gain_grad = jnp.zeros((1, width), jnp.float32)

    def back(piece, gain_grad):
        at = rows_of(piece)
        d_inner = two_sum[at].astype(jnp.float32)
        unit = normed[at]
        d_unit = d_inner * gain_ref[...]
        d_middle_ref[at] = d_out_ref[at].astype(jnp.float32) + scale[at, 0:1] * (
            d_unit - unit * (row_sum(d_unit * unit) / width)
        )
        return gain_grad + jnp.sum(d_inner * unit, axis=0, keepdims=True)

    for number in range(two.steps()):
        two.step(number)
        if number < len(works):
            works[number]()
        if number >= 2:
            two.ready(number - 2)
            gain_grad = back(number - 2, gain_grad)
        if number >= 3:
            feed.step(number - 3)
    gain_grad_ref[...] = jnp.broadcast_to(gain_grad, gain_grad_ref.shape)
    d_rounded = d_middle_ref[...].astype(jnp.bfloat16)
    d_mixed_ref[...] = dot(d_rounded, out_weight_ref[...])
    feed.step(two.steps() - 3)
    out_grad_ref[...] = dot(d_rounded, y_ref[...], (0, 0)).astype(jnp.bfloat16)
    for number in range(two.steps() - 2, feed.steps()):
        feed.step(number)
    for piece in range(pieces):
        feed.ready(piece)
        at = rows_of(piece)
        block_ref[at] = (middle[at] + feed_sum[at].astype(jnp.float32)).astype(
            block_ref.dtype
        )
    for line in lines:
        line.finish()


def middle_part(y, out_weight, x, d_out, gain, weight, axis, call, pieces, group):
    rows, width = x.shape
    units = weight.shape[1] // 3
    cols = y.shape[1]
    sems = pltpu.SemaphoreType.DMA((15 * pieces,))
    half, full = jnp.bfloat16, jnp.float32
    scratch = [pltpu.VMEM((rows, width), half) for _ in range(6)]
    scratch += [pltpu.VMEM((rows, width), full) for _ in range(2)]
    scratch += [pltpu.VMEM((rows, LANES), full), pltpu.VMEM((rows, width), half)]
    scratch += [pltpu.VMEM((rows, units), half) for _ in range(3)]
    scratch += [pltpu.VMEM((rows, units), full)]
    for _ in range(3):
        scratch += line_buffers(pieces, (rows, width), half)
    return pl.pallas_call(
        partial(middle_kernel, axis, pieces, group),
        out_shape=[
            jax.ShapeDtypeStruct((rows, width), half),
            jax.ShapeDtypeStruct((rows, width), full),
            jax.ShapeDtypeStruct((rows, cols), full),
            jax.ShapeDtypeStruct(weight.shape, half),
            jax.ShapeDtypeStruct(out_weight.shape, half),
            jax.ShapeDtypeStruct((8, width), full),
        ],
        in_specs=in_vmem(6),
        out_specs=in_vmem(6),
        scratch_shapes=scratch + [sems, sems],
        cost_estimate=pl.CostEstimate(
            flops=40000000000, bytes_accessed=200000000, transcendentals=0
        ),
        compiler_params=pltpu.CompilerParams(
            collective_id=call, has_side_effects=True, vmem_limit_bytes=24 * MIB
        ),
        name=f"middle_{call}",
    )(y, out_weight, x, d_out, gain, weight)


def apply_map(matrix, addend, incoming):
    return jnp.einsum("hde,hew->hdw", matrix, incoming, precision=HIGHEST) + addend


def local(
    tokens,
    segments,
    cotangent,
    mixer_gain,
    mlp_gain,
    query_weight,
    key_weight,
    value_weight,
    gate_weight,
    decay_weight,
    beta_weight,
    output_weight,
    conv_query,
    conv_key,
    conv_value,
    decay_log,
    decay_bias,
    head_gain,
    hidden_gate,
    hidden_up,
    hidden_down,
):
    width = tokens.shape[-1]
    inputs = tokens.reshape(-1, width).astype(jnp.float32)
    row_count = inputs.shape[0]
    query_cols = query_weight.shape[1]
    value_cols = value_weight.shape[1]
    head_count = decay_weight.shape[1]
    ff_cols = hidden_gate.shape[1]
    axes = ("dp", "ctx")
    used = 2 * query_cols + 2 * value_cols + 2 * head_count + 2
    pad_cols = -used % LANES
    own_rows = query_weight.shape[0]
    squared = lax.axis_size("dp") == 4 and lax.axis_size("ctx") == 2
    if squared:
        tail_rows = jnp.concatenate(
            [
                decay_weight.T,
                beta_weight.T,
                mixer_gain[None, :],
                mlp_gain[None, :],
                jnp.zeros((pad_cols, own_rows), jnp.bfloat16),
            ],
            0,
        )
        in_weights, full_output, gain_rows = gathered(
            [[query_weight, key_weight, value_weight, gate_weight], [output_weight]],
            tail_rows,
            axes,
            5,
        )
    else:
        in_weights = lax.all_gather(
            jnp.concatenate(
                [
                    query_weight,
                    key_weight,
                    value_weight,
                    gate_weight,
                    decay_weight,
                    beta_weight,
                    mixer_gain[:, None],
                    mlp_gain[:, None],
                    jnp.zeros((own_rows, pad_cols), jnp.bfloat16),
                ],
                1,
            ),
            axes,
            axis=0,
            tiled=True,
        )
        full_output = lax.all_gather(output_weight, axes, axis=0, tiled=True)
        gain_one = in_weights[:, used - 2].astype(jnp.float32)
        gain_two = in_weights[:, used - 1].astype(jnp.float32)
    unit_pad = ((0, 0), (0, -ff_cols % LANES))
    own_mlp = jnp.concatenate(
        [jnp.pad(part, unit_pad) for part in (hidden_gate, hidden_up, hidden_down)], 1
    )
    if squared:
        own_mlp, gain_rows = lax.optimization_barrier((own_mlp, gain_rows))
        gain_one = gain_rows[2 * head_count]
        gain_two = gain_rows[2 * head_count + 1]
    mlp_weights = lax.all_gather(own_mlp, axes, axis=0, tiled=True)
    conv_cols = 2 * query_cols + value_cols
    key_dim = query_cols // head_count
    rms_one = lax.rsqrt(jnp.mean(inputs * inputs, -1, keepdims=True) + EPSILON)
    normed_one = inputs * rms_one
    hidden_one = (normed_one * gain_one).astype(jnp.bfloat16)
    projected = jnp.dot(hidden_one, in_weights, preferred_element_type=jnp.float32)
    conv_weight = jnp.concatenate([conv_query, conv_key, conv_value], 1)
    taps = conv_weight.shape[0]
    margin = taps - 1
    last_rows = projected[row_count - EDGE :, :conv_cols].astype(jnp.bfloat16)
    edge_rows = passed_along(last_rows, "ctx", 1)
    seg_padded = jnp.concatenate([jnp.full((margin,), -1, jnp.int32), segments.reshape(-1)], 0)
    seg_ext = lax.dynamic_slice_in_dim(
        seg_padded, lax.axis_index("ctx") * row_count, row_count + margin
    )
    same_doc = jnp.stack(
        [
            (seg_ext[margin - lag : margin - lag + row_count] == seg_ext[margin:])
            for lag in range(taps)
        ],
        1,
    ).astype(jnp.float32)
    lane_pad = (0, LANES - head_count)
    params = jnp.stack([jnp.pad(decay_log, lane_pad), jnp.pad(decay_bias, lane_pad)])
    value_dim = value_cols // head_count
    ctx_size = lax.axis_size("ctx")
    chained = ctx_size > 2
    square = ((head_count, row_count, row_count), jnp.float32)
    tall_key = ((head_count, row_count, key_dim), jnp.float32)
    tall_value = ((head_count, row_count, value_dim), jnp.float32)
    flat_key = ((row_count, query_cols), jnp.float32)
    state = ((head_count, key_dim, value_dim), jnp.float32)
    entered = on_core(
        partial(enter_kernel, head_count, key_dim, chained),
        "mixer_enter",
        [
            ((row_count, conv_cols), jnp.float32),
            flat_key,
            flat_key,
            square,
            square,
            square,
            square,
            tall_key,
            tall_value,
            tall_key,
            tall_value,
            state,
            ((row_count, LANES), jnp.float32),
        ]
        + ([((head_count, key_dim, key_dim), jnp.float32)] if chained else []),
        [((EDGE + row_count, conv_cols), jnp.float32)],
    )(projected, edge_rows, same_doc, conv_weight, params)
    convolved, queries, key_rows, decay_pair, gram, score, inverse = entered[:7]
    from_key, from_value, carried, local_out, offset, mixer_cols = entered[7:13]

    initial = jnp.zeros_like(offset)
    for hop in range(ctx_size - 1):
        leaving = offset if hop == 0 else apply_map(entered[13], offset, initial)
        initial = passed_along(leaving, "ctx", 1)
    gain_row = head_gain[None, :]
    mixed_b, mixed = on_core(
        partial(leave_kernel, head_count),
        "mixer_leave",
        [((row_count, value_cols), jnp.bfloat16), ((row_count, value_cols), jnp.float32)],
    )(carried, local_out, initial, projected, gain_row)
    grad_rows = cotangent.reshape(-1, width)
    block_out, d_middle, d_mixed, mlp_grad, grad_output, gain_grad = middle_part(
        mixed_b,
        full_output,
        tokens.reshape(-1, width),
        grad_rows,
        gain_two[None, :],
        mlp_weights,
        "tp",
        0,
        4,
        2,
    )
    block_out = block_out.reshape(tokens.shape)
    grad_gain_two = gain_grad[0]

    def scattered(member):
        total = lax.psum_scatter(
            member.astype(jnp.bfloat16), axes, scatter_dimension=0, tiled=True
        )
        return total.astype(jnp.float32)

    mlp_own = scattered(mlp_grad)
    d_out, d_gate, d_head, init_grad = on_core(
        partial(leave_back_kernel, head_count),
        "mixer_leave_back",
        [
            ((row_count, value_cols), jnp.float32),
            ((row_count, value_cols), jnp.bfloat16),
            ((8, value_dim), jnp.float32),
            state,
        ],
    )(d_mixed, mixed, projected, gain_row, carried)
    d_head = d_head[0]
    end_grad = jnp.zeros_like(offset)
    for hop in range(ctx_size - 1):
        leaving = (
            init_grad
            if hop == 0
            else apply_map(jnp.swapaxes(entered[13], 1, 2), init_grad, end_grad)
        )
        end_grad = passed_along(leaving, "ctx", -1)
    edge_shape = ((EDGE, conv_cols), jnp.float32)
    d_proj, d_last, d_edge, d_conv, d_params = on_core(
        partial(enter_back_kernel, head_count, key_dim),
        "mixer_enter_back",
        [
            (projected.shape, jnp.bfloat16),
            edge_shape,
            edge_shape,
            ((8, conv_cols), jnp.float32),
            ((8, LANES), jnp.float32),
        ],
        [
            ((EDGE + row_count, conv_cols), jnp.float32),
            ((2 * EDGE + row_count, conv_cols), jnp.float32),
        ],
    )(
        d_out,
        d_gate,
        end_grad,
        initial,
        projected,
        edge_rows,
        same_doc,
        conv_weight,
        params,
        convolved,
        queries,
        key_rows,
        decay_pair,
        gram,
        score,
        inverse,
        from_key,
        from_value,
        mixer_cols,
    )
    d_conv = d_conv[:taps]
    d_log, d_bias = d_params[0, :head_count], d_params[1, :head_count]
    edge_back = passed_along(d_edge, "ctx", -1)
    d_proj = lax.dynamic_update_slice(
        d_proj, (d_last + edge_back).astype(jnp.bfloat16), (row_count - EDGE, 0)
    )
    grad_input = jnp.einsum("rd,rc->dc", hidden_one, d_proj, preferred_element_type=jnp.float32)
    one_part = jnp.einsum("rc,dc->rd", d_proj, in_weights, preferred_element_type=jnp.float32)
    small_width = max(conv_cols, width)

    def small_row(*members):
        member = jnp.concatenate([part.reshape(-1) for part in members])
        return jnp.pad(member, (0, small_width - member.shape[0]))[None, :]

    if squared:
        near = jnp.concatenate(
            [
                jnp.pad(d_conv, ((0, 0), (0, small_width - conv_cols))),
                small_row(d_log, d_bias),
                small_row(grad_gain_two),
            ],
            0,
        )
        wide = jnp.concatenate(
            [small_row(d_head), small_row(jnp.sum(one_part * normed_one, 0))], 0
        )
        lines = -(-near.shape[0] // 8) * 8
        small = jnp.concatenate(
            [
                jnp.pad(near, ((0, lines - near.shape[0]), (0, 0))),
                jnp.pad(wide, ((0, lines - wide.shape[0]), (0, 0))),
            ],
            0,
        )
        in_cols = grad_input.shape[1]
        first_cut = -(-in_cols // (2 * LANES)) * LANES
        cuts = ((0, 0, first_cut), (0, first_cut, in_cols - first_cut), (1, 0, value_cols))
        one_sum, input_own, output_own, small = last_sums(
            one_part.astype(jnp.bfloat16),
            grad_input.astype(jnp.bfloat16),
            grad_output.astype(jnp.bfloat16),
            small,
            axes,
            "tp",
            6,
            4,
            cuts,
        )
    else:
        one_part, mlp_own = lax.optimization_barrier((one_part, mlp_own))
        one_sum = summed(one_part.astype(jnp.bfloat16), "tp", 2)
    d_hidden_one = one_sum.astype(jnp.float32)
    dn_one = d_hidden_one * gain_one
    tokens_grad = d_middle + rms_one * (
        dn_one - normed_one * jnp.mean(dn_one * normed_one, -1, keepdims=True)
    )
    tokens_grad = tokens_grad.reshape(tokens.shape)
    edges = [
        0,
        query_cols,
        2 * query_cols,
        conv_cols,
        conv_cols + value_cols,
        conv_cols + value_cols + head_count,
        conv_cols + value_cols + 2 * head_count,
    ]

    if squared:
        begin = (lax.axis_index("dp") * 2 + lax.axis_index("ctx")) * own_rows
        gain_one_own = lax.dynamic_slice_in_dim(small[lines + 1], begin, own_rows)
        gain_two_own = lax.dynamic_slice_in_dim(small[taps + 1], begin, own_rows)
        conv_total = small[:taps, :conv_cols]
        log_total = small[taps, :head_count]
        bias_total = small[taps, head_count : 2 * head_count]
        head_total = small[lines, :value_dim]
    else:
        grad_gain_one = jnp.sum(d_hidden_one * normed_one, 0)
        column = jnp.arange(grad_input.shape[1])[None, :]
        grad_input = jnp.where(column == used - 2, grad_gain_one[:, None], grad_input)
        grad_input = jnp.where(column == used - 1, grad_gain_two[:, None], grad_input)
        output_own = scattered(grad_output)
        input_own = scattered(grad_input)
        gain_one_own = input_own[:, used - 2]
        gain_two_own = input_own[:, used - 1]
        rest = jnp.concatenate([d_head, d_log, d_bias])
        pad_row = jnp.zeros((-rest.shape[0] % conv_cols,), jnp.float32)
        rest = jnp.concatenate([rest, pad_row]).reshape(-1, conv_cols)
        packed = jnp.concatenate([d_conv, rest], 0)
        lines = packed.shape[0]
        packed = jnp.concatenate([packed, jnp.zeros((-lines % 8, conv_cols), jnp.float32)], 0)
        packed = small_sum(packed, ("dp", "ctx"), 3)
        conv_total = packed[:taps]
        rest = packed[taps:lines].reshape(-1)
        log_total = rest[value_dim : value_dim + head_count]
        bias_total = rest[value_dim + head_count : value_dim + 2 * head_count]
        head_total = small_sum(
            jnp.broadcast_to(rest[None, :value_dim], (8, value_dim)), ("tp",), 4
        )[0]
    units = mlp_own.shape[1] // 3
    reduced = (
        gain_one_own,
        gain_two_own,
        *(input_own[:, edges[i] : edges[i + 1]] for i in range(6)),
        output_own,
        *(mlp_own[:, i * units : i * units + ff_cols] for i in range(3)),
    )
    return (
        block_out,
        tokens_grad,
        reduced[0],
        reduced[1],
        reduced[2],
        reduced[3],
        reduced[4],
        reduced[5],
        reduced[6],
        reduced[7],
        reduced[8],
        conv_total[:, :query_cols],
        conv_total[:, query_cols : 2 * query_cols],
        conv_total[:, 2 * query_cols :],
        log_total,
        bias_total,
        head_total,
        reduced[9],
        reduced[10],
        reduced[11],
    )


def solution(mesh):
    return jax.shard_map(
        local,
        mesh=mesh,
        in_specs=(
            P("dp", "ctx", None),
            P("dp", None),
            P("dp", "ctx", None),
            P(("dp", "ctx")),
            P(("dp", "ctx")),
            P(("dp", "ctx"), "tp"),
            P(("dp", "ctx"), "tp"),
            P(("dp", "ctx"), "tp"),
            P(("dp", "ctx"), "tp"),
            P(("dp", "ctx"), "tp"),
            P(("dp", "ctx"), "tp"),
            P(("dp", "ctx"), "tp"),
            P(None, "tp"),
            P(None, "tp"),
            P(None, "tp"),
            P("tp"),
            P("tp"),
            P(),
            P(("dp", "ctx"), "tp"),
            P(("dp", "ctx"), "tp"),
            P(("dp", "ctx"), "tp"),
        ),
        out_specs=(
            P("dp", "ctx", None),
            P("dp", "ctx", None),
            P(("dp", "ctx")),
            P(("dp", "ctx")),
            P(("dp", "ctx"), "tp"),
            P(("dp", "ctx"), "tp"),
            P(("dp", "ctx"), "tp"),
            P(("dp", "ctx"), "tp"),
            P(("dp", "ctx"), "tp"),
            P(("dp", "ctx"), "tp"),
            P(("dp", "ctx"), "tp"),
            P(None, "tp"),
            P(None, "tp"),
            P(None, "tp"),
            P("tp"),
            P("tp"),
            P(),
            P(("dp", "ctx"), "tp"),
            P(("dp", "ctx"), "tp"),
            P(("dp", "ctx"), "tp"),
        ),
        check_vma=False,
    )
```

```python
from functools import partial

import jax
import jax.numpy as jnp
from jax import lax
from jax.experimental import pallas as pl
from jax.experimental.pallas import tpu as pltpu
from jax.sharding import PartitionSpec as P

EPSILON = 1e-06
HIGHEST = lax.Precision.HIGHEST
LANES = 128


def peer_of(axes, sizes, distance):
    flat = 0
    total = 1
    for axis, size in zip(axes, sizes):
        flat = flat * size + lax.axis_index(axis)
        total = total * size
    other = lax.rem(flat + distance, total)
    where = {}
    for axis, size in reversed(list(zip(axes, sizes))):
        where[axis] = lax.rem(other, size)
        other = other // size
    return where


def greet(axes, sizes, peers):
    barrier = pltpu.get_barrier_semaphore()
    for distance in range(1, peers + 1):
        pl.semaphore_signal(
            barrier,
            inc=1,
            device_id=peer_of(axes, sizes, distance),
            device_id_type=pl.DeviceIdType.MESH,
        )
    pl.semaphore_wait(barrier, peers)


def sum_kernel(axis, size, x_ref, out_ref, parts, mine, got, send, recv, send_two, recv_two):
    peers = size - 1
    me = lax.axis_index(axis)
    rows = x_ref.shape[0] // size
    greet((axis,), (size,), peers)

    def block(index):
        return pl.ds(pl.multiple_of(index * rows, rows), rows)

    copies = []
    for distance in range(1, size):
        other = lax.rem(me + distance, size)
        copy = pltpu.make_async_remote_copy(
            src_ref=x_ref.at[block(other)],
            dst_ref=parts.at[distance - 1],
            send_sem=send.at[distance - 1],
            recv_sem=recv.at[distance - 1],
            device_id={axis: other},
            device_id_type=pl.DeviceIdType.MESH,
        )
        copy.start()
        copies.append(copy)
    total = x_ref[block(me)].astype(jnp.float32)
    for distance in range(1, size):
        copies[distance - 1].wait_recv()
        total = total + parts[distance - 1].astype(jnp.float32)
    total = total.astype(out_ref.dtype)
    mine[...] = total
    out_ref[block(me)] = total
    more = []
    for distance in range(1, size):
        copy = pltpu.make_async_remote_copy(
            src_ref=mine,
            dst_ref=got.at[distance - 1],
            send_sem=send_two.at[distance - 1],
            recv_sem=recv_two.at[distance - 1],
            device_id={axis: lax.rem(me + distance, size)},
            device_id_type=pl.DeviceIdType.MESH,
        )
        copy.start()
        more.append(copy)
    for distance in range(1, size):
        more[distance - 1].wait_recv()
        out_ref[block(lax.rem(me + size - distance, size))] = got[distance - 1]
    for copy in copies + more:
        copy.wait_send()


def summed(value, axis, call):
    size = lax.axis_size(axis)
    if size == 1:
        return value
    rows, cols = value.shape
    if size == 4 and rows % 128 == 0:
        return line_summed(value, axis, call, 4)
    piece = (size - 1, rows // size, cols)
    sems = pltpu.SemaphoreType.DMA((size - 1,))
    return pl.pallas_call(
        partial(sum_kernel, axis, size),
        out_shape=jax.ShapeDtypeStruct(value.shape, value.dtype),
        in_specs=[pl.BlockSpec(memory_space=pltpu.VMEM)],
        out_specs=pl.BlockSpec(memory_space=pltpu.VMEM),
        scratch_shapes=[
            pltpu.VMEM(piece, value.dtype),
            pltpu.VMEM(piece[1:], value.dtype),
            pltpu.VMEM(piece, value.dtype),
            sems,
            sems,
            sems,
            sems,
        ],
        cost_estimate=pl.CostEstimate(
            flops=value.size * 40000, bytes_accessed=value.size * 300, transcendentals=0
        ),
        compiler_params=pltpu.CompilerParams(collective_id=call, has_side_effects=True),
        name=f"tp_sum_{call}",
    )(value)


def small_kernel(axes, sizes, peers, x_ref, out_ref, parts, send, recv):
    greet(axes, sizes, peers)
    copies = []
    for distance in range(1, peers + 1):
        copy = pltpu.make_async_remote_copy(
            src_ref=x_ref,
            dst_ref=parts.at[distance - 1],
            send_sem=send.at[distance - 1],
            recv_sem=recv.at[distance - 1],
            device_id=peer_of(axes, sizes, distance),
            device_id_type=pl.DeviceIdType.MESH,
        )
        copy.start()
        copies.append(copy)
    flat = 0
    for axis, size in zip(axes, sizes):
        flat = flat * size + lax.axis_index(axis)
    for copy in copies:
        copy.wait()
    parts[peers] = x_ref[...]
    total = jnp.zeros(x_ref.shape, jnp.float32)
    for owner in range(peers + 1):
        slot = lax.rem(flat + 2 * (peers + 1) - owner - 1, peers + 1)
        total = total + parts[slot]
    out_ref[...] = total


def small_sum(value, axes, call):
    sizes = tuple(lax.axis_size(axis) for axis in axes)
    peers = 1
    for size in sizes:
        peers = peers * size
    peers = peers - 1
    if peers == 0:
        return value
    return pl.pallas_call(
        partial(small_kernel, axes, sizes, peers),
        out_shape=jax.ShapeDtypeStruct(value.shape, value.dtype),
        in_specs=[pl.BlockSpec(memory_space=pltpu.VMEM)],
        out_specs=pl.BlockSpec(memory_space=pltpu.VMEM),
        scratch_shapes=[
            pltpu.VMEM((peers + 1,) + value.shape, value.dtype),
            pltpu.SemaphoreType.DMA((peers,)),
            pltpu.SemaphoreType.DMA((peers,)),
        ],
        cost_estimate=pl.CostEstimate(
            flops=1000000, bytes_accessed=20000000, transcendentals=0
        ),
        compiler_params=pltpu.CompilerParams(collective_id=call, has_side_effects=True),
        name=f"small_sum_{call}",
    )(value)


def passed_along(value, axis, by):
    devices = lax.axis_size(axis)
    pairs = [(i, i + by) for i in range(devices) if 0 <= i + by < devices]
    return lax.ppermute(value, axis, pairs)


EDGE = 16


def halves(value):
    high = value.astype(jnp.bfloat16)
    low = (value - high.astype(jnp.float32)).astype(jnp.bfloat16)
    return high, low


def product(left, right, over=(1, 0)):
    dims = (((over[0],), (over[1],)), ((), ()))

    def one(a, b):
        return lax.dot_general(a, b, dims, preferred_element_type=jnp.float32)

    return one(left[0], right[0]) + (one(left[0], right[1]) + one(left[1], right[0]))


def rough(left, right, over=(1, 0)):
    dims = (((over[0],), (over[1],)), ((), ()))
    return lax.dot_general(left[0], right[0], dims, preferred_element_type=jnp.float32)


def exact_sum(ones, value, over=(1, 0)):
    dims = (((over[0],), (over[1],)), ((), ()))
    high = value.astype(jnp.bfloat16)
    rest = value - high.astype(jnp.float32)
    middle = rest.astype(jnp.bfloat16)
    low = (rest - middle.astype(jnp.float32)).astype(jnp.bfloat16)
    total = None
    for part in (low, middle, high):
        term = lax.dot_general(ones, part, dims, preferred_element_type=jnp.float32)
        total = term if total is None else total + term
    return total


def logistic(value):
    return 1.0 / (1.0 + jnp.exp(-value))


def row_sum(value):
    return jnp.sum(value, axis=1, keepdims=True)


def iotas(count):
    row = lax.broadcasted_iota(jnp.int32, (count, count), 0)
    col = lax.broadcasted_iota(jnp.int32, (count, count), 1)
    return row, col


def in_lane(lane, index, column):
    return jnp.where(lane == index, column, 0.0)


def lower_inverse_of(lower, row, col):
    order = lower.shape[0]
    apart = row ^ col
    inverse = jnp.where(row == col, 1.0, 0.0) - jnp.where(apart == 1, lower, 0.0)
    level = 1
    while (1 << level) < order:
        cross = jnp.where((apart >> level) == 1, lower, 0.0)
        both = halves(inverse)
        inverse = inverse - product(both, halves(product(halves(cross), both)))
        level += 1
    return inverse


def head_params(params_ref, tail, heads, lane):
    softened = tail + params_ref[1:2, :]
    soft = jnp.maximum(softened, 0.0) + jnp.log1p(jnp.exp(-jnp.abs(softened)))
    rate = jnp.where(lane < heads, -jnp.exp(params_ref[0:1, :]) * soft, 0.0)
    return rate, softened


def enter_kernel(
    heads,
    key_dim,
    chained,
    proj_ref,
    edge_ref,
    same_ref,
    taps_ref,
    params_ref,
    conv_ref,
    query_ref,
    key_ref,
    decay_ref,
    gram_ref,
    score_ref,
    inverse_ref,
    from_key_ref,
    from_value_ref,
    carried_ref,
    local_ref,
    offset_ref,
    cols_ref,
    *rest,
    between=None,
):
    ext = rest[-1]
    rows, conv_cols = conv_ref.shape
    query_cols = heads * key_dim
    value_dim = from_value_ref.shape[2]
    ext[0:EDGE, :] = edge_ref[...].astype(jnp.float32)
    ext[EDGE : EDGE + rows, :] = (
        proj_ref[:, 0:conv_cols].astype(jnp.bfloat16).astype(jnp.float32)
    )
    convolved = taps_ref[0:1, :] * ext[EDGE : EDGE + rows, :]
    for lag in range(1, taps_ref.shape[0]):
        convolved = convolved + taps_ref[lag : lag + 1, :] * (
            ext[EDGE - lag : EDGE - lag + rows, :] * same_ref[:, lag : lag + 1]
        )
    conv_ref[...] = convolved
    conv_ref.send()
    lane = lax.broadcasted_iota(jnp.int32, (rows, LANES), 1)
    row, col = iotas(rows)
    tail = proj_ref[:, conv_cols + heads * value_dim :]
    rate, _ = head_params(params_ref, tail, heads, lane)
    beta_all = logistic(tail)
    summed_in = rate + in_lane(lane, heads, 1.0 - same_ref[:, 1:2])
    until = jnp.where(col <= row, 1.0, 0.0).astype(jnp.bfloat16)
    total = exact_sum(until, summed_in)
    total_rows = total.T
    counted = total[:, heads : heads + 1]
    same = (jnp.abs(counted - total_rows[heads : heads + 1, :]) < 0.5) & (col <= row)
    strict = same & (col < row)
    first = jnp.where(counted < 0.5, 1.0, 0.0)
    cols = jnp.zeros((rows, LANES), jnp.float32)
    for head in range(heads):
        keys_at = slice(head * key_dim, (head + 1) * key_dim)
        queries = convolved[:, keys_at]
        queries = queries * logistic(queries)
        queries = (
            queries * lax.rsqrt(row_sum(queries * queries) + EPSILON) * key_dim ** (-0.5)
        )
        keys = convolved[:, query_cols + head * key_dim : query_cols + (head + 1) * key_dim]
        keys = keys * logistic(keys)
        keys = keys * lax.rsqrt(row_sum(keys * keys) + EPSILON)
        base = 2 * query_cols + head * value_dim
        values = convolved[:, base : base + value_dim]
        values = values * logistic(values)
        query_ref[:, keys_at] = queries
        key_ref[:, keys_at] = keys
        cumulative = total[:, head : head + 1]
        spread = cumulative - total_rows[head : head + 1, :]
        decay = jnp.where(same, jnp.exp(jnp.where(same, spread, 0.0)), 0.0)
        anchor = jnp.exp(cumulative) * first
        beta = beta_all[:, heads + head : heads + head + 1]
        decay_ref[head] = decay
        key_parts = halves(keys)
        gram = jnp.where(strict, product(key_parts, key_parts, (1, 1)) * decay, 0.0)
        gram_ref[head] = gram
        score = product(halves(queries), key_parts, (1, 1)) * decay
        score_ref[head] = score
        inverse = lower_inverse_of(beta * gram, row, col)
        inverse_ref[head] = inverse
        inverse_parts = halves(inverse)
        from_key = product(inverse_parts, halves((-beta * anchor) * keys))
        from_value = product(inverse_parts, halves(beta * values))
        from_key_ref[head] = from_key
        from_value_ref[head] = from_value
        score_parts = halves(score)
        value_parts = halves(from_value)
        from_key_parts = halves(from_key)
        carried_ref[head] = product(score_parts, from_key_parts) + anchor * queries
        local_ref[head] = product(score_parts, value_parts)
        last_count = counted[rows - 1 : rows, :]
        last_total = cumulative[rows - 1 : rows, :]
        matches = jnp.abs(counted - last_count) < 0.5
        closing = jnp.where(
            matches, jnp.exp(jnp.where(matches, last_total - cumulative, 0.0)), 0.0
        )
        closed = halves(closing * keys)
        offset_ref[head] = product(closed, value_parts, (0, 0))
        if chained:
            transfer_row, transfer_col = iotas(key_dim)
            rest[0][head] = product(closed, from_key_parts, (0, 0)) + jnp.where(
                transfer_row == transfer_col, anchor[rows - 1 : rows, :], 0.0
            )
        cols = (
            cols
            + in_lane(lane, head, anchor)
            + in_lane(lane, heads + head, beta)
            + in_lane(lane, 2 * heads + head, closing)
        )
        made = [decay_ref, gram_ref, score_ref, inverse_ref, from_key_ref]
        made += [from_value_ref, carried_ref, local_ref, offset_ref]
        for ref in made + list(rest[:-1]):
            if isinstance(ref, Leaving):
                ref.send(head)
        if between is not None:
            between(head)
    cols_ref[...] = cols


def leave_kernel(
    heads,
    carried_ref,
    local_ref,
    initial_ref,
    proj_ref,
    gain_ref,
    y_ref,
    mixed_ref,
):
    rows = y_ref.shape[0]
    value_dim = local_ref.shape[2]
    first_col = proj_ref.shape[1] - LANES - heads * value_dim
    for head in range(heads):
        at = slice(head * value_dim, (head + 1) * value_dim)
        mixed = local_ref[head] + product(
            halves(carried_ref[head]), halves(initial_ref[head])
        )
        mixed_ref[:, at] = mixed
        scale = lax.rsqrt(row_sum(mixed * mixed) / value_dim + EPSILON)
        gate = proj_ref[:, first_col + head * value_dim : first_col + (head + 1) * value_dim]
        y_ref[:, at] = (
            mixed * scale * gain_ref[...] * (gate * logistic(gate))
        ).astype(jnp.bfloat16)


def leave_back_kernel(
    heads,
    d_y_ref,
    mixed_ref,
    proj_ref,
    gain_ref,
    carried_ref,
    d_mixed_ref,
    d_gate_ref,
    d_gain_ref,
    d_initial_ref,
):
    rows = d_y_ref.shape[0]
    value_dim = d_mixed_ref.shape[1] // heads
    first_col = proj_ref.shape[1] - LANES - heads * value_dim
    d_gain = jnp.zeros((1, value_dim), jnp.float32)
    for head in range(heads):
        at = slice(head * value_dim, (head + 1) * value_dim)
        mixed = mixed_ref[:, at]
        scale = lax.rsqrt(row_sum(mixed * mixed) / value_dim + EPSILON)
        normed = mixed * scale
        gate = proj_ref[:, first_col + head * value_dim : first_col + (head + 1) * value_dim]
        sigma = logistic(gate)
        d_y = d_y_ref[:, at]
        d_gain = d_gain + jnp.sum(d_y * normed * (gate * sigma), axis=0, keepdims=True)
        scaled = d_y * gain_ref[...]
        d_gate_ref[:, at] = (
            scaled * normed * (sigma * (1.0 + gate * (1.0 - sigma)))
        ).astype(jnp.bfloat16)
        d_normed = scaled * (gate * sigma)
        d_mixed = scale * (d_normed - normed * (row_sum(d_normed * normed) / value_dim))
        d_mixed_ref[:, at] = d_mixed
        d_initial_ref[head] = rough(
            halves(carried_ref[head]), halves(d_mixed), (0, 0)
        )
    d_gain_ref[...] = jnp.broadcast_to(d_gain, d_gain_ref.shape)


def enter_back_kernel(
    heads,
    key_dim,
    between,
    d_mixed_ref,
    d_gate_ref,
    d_end_ref,
    initial_ref,
    proj_ref,
    edge_ref,
    same_ref,
    taps_ref,
    params_ref,
    conv_ref,
    query_ref,
    key_ref,
    decay_ref,
    gram_ref,
    score_ref,
    inverse_ref,
    from_key_ref,
    from_value_ref,
    cols_ref,
    d_proj_ref,
    d_last_ref,
    d_edge_ref,
    d_taps_ref,
    d_params_ref,
    ext,
    d_ext,
):
    rows, conv_cols = conv_ref.shape
    query_cols = heads * key_dim
    value_dim = from_value_ref.shape[2]
    value_cols = heads * value_dim
    margin = taps_ref.shape[0]
    lane = lax.broadcasted_iota(jnp.int32, (rows, LANES), 1)
    row, col = iotas(rows)
    last_row = lax.broadcasted_iota(jnp.int32, (rows, 1), 0) == rows - 1
    d_total = jnp.zeros((rows, LANES), jnp.float32)
    d_tail = jnp.zeros((rows, LANES), jnp.float32)
    d_active = []
    for head in range(heads):
        keys_at = slice(head * key_dim, (head + 1) * key_dim)
        queries, keys = query_ref[:, keys_at], key_ref[:, keys_at]
        base = 2 * query_cols + head * value_dim
        values = conv_ref[:, base : base + value_dim]
        values = values * logistic(values)
        anchor = cols_ref[:, head : head + 1]
        beta = cols_ref[:, heads + head : heads + head + 1]
        closing = cols_ref[:, 2 * heads + head : 2 * heads + head + 1]
        decay, gram, score = decay_ref[head], gram_ref[head], score_ref[head]
        initial = initial_ref[head]
        d_end = d_end_ref[head]
        d_mixed = d_mixed_ref[:, head * value_dim : (head + 1) * value_dim]
        initial_parts, end_parts = halves(initial), halves(d_end)
        mixed_parts = halves(d_mixed)
        key_parts, query_parts = halves(keys), halves(queries)
        updates = from_value_ref[head] + product(halves(from_key_ref[head]), initial_parts)
        update_parts = halves(updates)
        key_state = product(key_parts, initial_parts)
        query_state = product(query_parts, initial_parts)
        d_updates = product(halves(score), mixed_parts, (0, 0)) + product(
            halves(closing * keys), end_parts
        )
        d_target = product(halves(inverse_ref[head]), halves(d_updates), (0, 0))
        d_delta = beta * d_target
        delta = values - anchor * key_state
        d_lower = -product(halves(d_target), update_parts, (1, 1))
        d_score = product(mixed_parts, update_parts, (1, 1))
        d_pair = halves(d_score * decay)
        d_lower_gram = d_lower * gram
        d_beta = row_sum(d_target * delta) + row_sum(d_lower_gram)
        d_gram = halves(jnp.where(col < row, d_lower * (beta * decay), 0.0))
        back = halves(anchor * d_delta)
        d_query = rough(d_pair, key_parts) + anchor * rough(
            mixed_parts, initial_parts, (1, 1)
        )
        d_closed = rough(update_parts, end_parts, (1, 1))
        d_key = (
            rough(d_pair, query_parts, (0, 0))
            + rough(d_gram, key_parts)
            + rough(d_gram, key_parts, (0, 0))
            + closing * d_closed
            - rough(back, initial_parts, (1, 1))
        )
        d_anchor = row_sum(d_mixed * query_state) - row_sum(d_delta * key_state)
        d_anchor = d_anchor + jnp.where(last_row, jnp.sum(d_end * initial), 0.0)
        d_closing = closing * row_sum(keys * d_closed)
        flow = d_score * score + beta * d_lower_gram
        into = jnp.broadcast_to(jnp.sum(flow, axis=0, keepdims=True), (LANES, rows)).T
        d_cumulative = row_sum(flow) - into[:, 0:1] + anchor * d_anchor - d_closing
        d_cumulative = d_cumulative + jnp.where(last_row, jnp.sum(d_closing), 0.0)
        d_total = d_total + in_lane(lane, head, d_cumulative)
        d_tail = d_tail + in_lane(lane, heads + head, d_beta * beta * (1.0 - beta))
        raw_query = conv_ref[:, keys_at]
        raw_key = conv_ref[:, query_cols + head * key_dim : query_cols + (head + 1) * key_dim]
        query_sigma, key_sigma = logistic(raw_query), logistic(raw_key)
        active = raw_query * query_sigma
        scale = lax.rsqrt(row_sum(active * active) + EPSILON)
        unit = active * scale
        d_unit = d_query * key_dim ** (-0.5)
        d_raw_query = (
            scale
            * (d_unit - unit * row_sum(d_unit * unit))
            * (query_sigma * (1.0 + raw_query * (1.0 - query_sigma)))
        )
        active = raw_key * key_sigma
        scale = lax.rsqrt(row_sum(active * active) + EPSILON)
        d_raw_key = (
            scale
            * (d_key - keys * row_sum(d_key * keys))
            * (key_sigma * (1.0 + raw_key * (1.0 - key_sigma)))
        )
        raw_value = conv_ref[:, base : base + value_dim]
        value_sigma = logistic(raw_value)
        d_raw_value = d_delta * (value_sigma * (1.0 + raw_value * (1.0 - value_sigma)))
        d_active.append((d_raw_query, d_raw_key, d_raw_value))
        if between is not None:
            between(head)
    tail = proj_ref[:, conv_cols + value_cols :]
    rate, softened = head_params(params_ref, tail, heads, lane)
    since = jnp.where(col >= row, 1.0, 0.0).astype(jnp.bfloat16)
    d_rate = exact_sum(since, d_total)
    d_decay = jnp.where(
        lane < heads, d_rate * (-jnp.exp(params_ref[0:1, :])) * logistic(softened), 0.0
    )
    d_params_ref[0:1, :] = jnp.sum(d_rate * rate, axis=0, keepdims=True)
    d_params_ref[1:2, :] = jnp.sum(d_decay, axis=0, keepdims=True)
    d_params_ref[2:, :] = jnp.zeros((d_params_ref.shape[0] - 2, LANES), jnp.float32)
    d_proj_ref[:, conv_cols + value_cols :] = (d_decay + d_tail).astype(jnp.bfloat16)
    d_proj_ref[:, conv_cols : conv_cols + value_cols] = d_gate_ref[...]
    d_convolved = jnp.concatenate(
        [part[0] for part in d_active]
        + [part[1] for part in d_active]
        + [part[2] for part in d_active],
        axis=1,
    )
    ext[0:EDGE, :] = edge_ref[...].astype(jnp.float32)
    ext[EDGE : EDGE + rows, :] = (
        proj_ref[:, 0:conv_cols].astype(jnp.bfloat16).astype(jnp.float32)
    )
    zeros = jnp.zeros((EDGE, conv_cols), jnp.float32)
    d_ext[0:EDGE, :] = zeros
    d_ext[EDGE + rows :, :] = zeros
    d_taps_ref[...] = jnp.zeros(d_taps_ref.shape, jnp.float32)
    d_taps_ref[0:1, :] = jnp.sum(
        d_convolved * ext[EDGE : EDGE + rows, :], axis=0, keepdims=True
    )
    d_pre = taps_ref[0:1, :] * d_convolved
    d_edge = zeros
    for lag in range(1, margin):
        kept = d_convolved * same_ref[:, lag : lag + 1]
        d_taps_ref[lag : lag + 1, :] = jnp.sum(
            kept * ext[EDGE - lag : EDGE - lag + rows, :], axis=0, keepdims=True
        )
        d_ext[EDGE : EDGE + rows, :] = kept
        weight = taps_ref[lag : lag + 1, :]
        d_pre = d_pre + weight * d_ext[EDGE + lag : EDGE + lag + rows, :]
        d_edge = d_edge + weight * d_ext[lag : lag + EDGE, :]
    d_proj_ref[:, 0:conv_cols] = d_pre.astype(jnp.bfloat16)
    d_last_ref[...] = d_pre[rows - EDGE :, :]
    d_edge_ref[...] = d_edge


MIB = 1024 * 1024


class Arriving:
    def __init__(self, ref, buf, sem):
        self.buf, self.copy, self.here = buf, pltpu.make_async_copy(ref, buf, sem), False
        self.shape, self.dtype = buf.shape, buf.dtype
        self.copy.start()

    def settle(self):
        if not self.here:
            self.copy.wait()
            self.here = True

    def __getitem__(self, index):
        self.settle()
        return self.buf[index]


class Leaving:
    def __init__(self, ref, buf, sems, first):
        self.ref, self.buf, self.sems, self.first, self.copies = ref, buf, sems, first, []
        self.shape, self.dtype = buf.shape, buf.dtype

    def __getitem__(self, index):
        return self.buf[index]

    def __setitem__(self, index, value):
        self.buf[index] = value

    def send(self, part=None, source=None):
        if source is None:
            source = self.buf if part is None else self.buf.at[part]
        target = self.ref if part is None else self.ref.at[part]
        sem = self.sems.at[self.first + len(self.copies)]
        self.copies.append(pltpu.make_async_copy(source, target, sem))
        self.copies[-1].start()

    def end(self):
        if not self.copies:
            self.send()
        for copy in self.copies:
            copy.wait()


PARTS = 4


def staged(kernel, ins, outs):
    def body(*refs):
        sems = refs[-1]
        given, made = refs[:ins], refs[ins : ins + outs]
        bufs = refs[ins + outs : 2 * (ins + outs)]
        arriving = [Arriving(given[i], bufs[i], sems.at[i]) for i in range(ins)]
        leaving = [
            Leaving(made[i], bufs[ins + i], sems, ins + PARTS * i) for i in range(outs)
        ]
        kernel(*arriving, *leaving, *refs[2 * (ins + outs) : -1])
        for member in arriving:
            member.settle()
        for member in leaving:
            member.end()

    return body


def staged_call(kernel, name, shapes, scratch, params):
    def call(*args):
        made = [jax.ShapeDtypeStruct(shape, dtype) for shape, dtype in shapes]
        return pl.pallas_call(
            staged(kernel, len(args), len(made)),
            out_shape=made,
            in_specs=[pl.BlockSpec(memory_space=pl.ANY)] * len(args),
            out_specs=[pl.BlockSpec(memory_space=pl.ANY)] * len(made),
            scratch_shapes=[pltpu.VMEM(x.shape, x.dtype) for x in (*args, *made)]
            + list(scratch)
            + [pltpu.SemaphoreType.DMA((len(args) + PARTS * len(made),))],
            compiler_params=params,
            name=name,
        )(*args)

    return call


def on_core(kernel, name, shapes, scratch=()):
    params = pltpu.CompilerParams(vmem_limit_bytes=56 * MIB)
    scratch = [pltpu.VMEM(shape, dtype) for shape, dtype in scratch]
    return staged_call(kernel, name, shapes, scratch, params)


MESH = pl.DeviceIdType.MESH


class Links:
    def __init__(self, send, recv):
        self.send, self.recv, self.used = send, recv, 0

    def take(self, count=1):
        first = self.used
        self.used = first + count
        return first

    def copy(self, index, source, target, where):
        return pltpu.make_async_remote_copy(
            src_ref=source,
            dst_ref=target,
            send_sem=self.send.at[index],
            recv_sem=self.recv.at[index],
            device_id=where,
            device_id_type=MESH,
        )


def meet(places):
    barrier = pltpu.get_barrier_semaphore()
    for place in places:
        pl.semaphore_signal(barrier, inc=1, device_id=place, device_id_type=MESH)
    pl.semaphore_wait(barrier, len(places))


def flipped(index, bit):
    step = 1 << bit
    return index + step - 2 * step * lax.rem(index // step, 2)


def line_places(axis):
    me = lax.axis_index(axis)
    return [{axis: lax.rem(me + distance, 4)} for distance in range(1, 4)]


class LineSum:
    def __init__(self, axis, pieces, x_ref, out_ref, bufs, links):
        self.pieces, self.x_ref, self.out_ref, self.links = pieces, x_ref, out_ref, links
        self.from_end, self.to_mate, self.from_mate, self.keep = bufs
        me = lax.axis_index(axis)
        self.inner = (me == 1) | (me == 2)
        self.partner = {axis: flipped(me, 0)}
        self.mate = {axis: 3 - me}
        self.mine = me // 2
        self.size = x_ref.shape[0] // pieces
        self.half = self.size // 2
        self.ends = links.take(pieces)
        self.pairs = links.take(pieces)
        self.totals = links.take(pieces)
        self.backs = links.take(pieces)
        self.others = links.take(pieces)

    def rows(self, piece, part):
        start = piece * self.size + part * self.half
        return pl.ds(pl.multiple_of(start, self.half), self.half)

    def end_copy(self, piece):
        return self.links.copy(
            self.ends + piece,
            self.x_ref.at[pl.ds(piece * self.size, self.size)],
            self.from_end.at[piece],
            self.partner,
        )

    def pair_copy(self, piece):
        return self.links.copy(
            self.pairs + piece, self.to_mate.at[piece], self.from_mate.at[piece], self.mate
        )

    def out_copy(self, base, piece, part, where):
        ref = self.out_ref.at[self.rows(piece, part)]
        return self.links.copy(base + piece, ref, ref, where)

    def start(self, piece):
        @pl.when(jnp.logical_not(self.inner))
        def _():
            self.end_copy(piece).start()

    def first(self, piece):
        @pl.when(self.inner)
        def _():
            self.end_copy(piece).wait_recv()
            arrived = self.from_end.at[piece]

            def pair(part):
                at = pl.ds(pl.multiple_of(part * self.half, self.half), self.half)
                return self.x_ref[self.rows(piece, part)].astype(jnp.float32) + arrived[
                    at
                ].astype(jnp.float32)

            self.to_mate[piece] = pair(1 - self.mine).astype(self.to_mate.dtype)
            self.pair_copy(piece).start()
            self.keep[piece] = pair(self.mine)

    def second(self, piece):
        @pl.when(self.inner)
        def _():
            self.pair_copy(piece).wait_recv()
            total = self.keep[piece] + self.from_mate[piece].astype(jnp.float32)
            self.out_ref[self.rows(piece, self.mine)] = total.astype(self.out_ref.dtype)
            self.out_copy(self.totals, piece, self.mine, self.mate).start()
            self.out_copy(self.backs, piece, self.mine, self.partner).start()

    def third(self, piece):
        @pl.when(self.inner)
        def _():
            self.out_copy(self.totals, piece, 1 - self.mine, self.mate).wait_recv()
            self.out_copy(self.others, piece, 1 - self.mine, self.partner).start()

    def step(self, number):
        if number < self.pieces:
            self.first(number)
        if 0 <= number - 1 < self.pieces:
            self.second(number - 1)
        if 0 <= number - 2 < self.pieces:
            self.third(number - 2)

    def steps(self):
        return self.pieces + 2

    def ready(self, piece):
        @pl.when(jnp.logical_not(self.inner))
        def _():
            self.out_copy(self.backs, piece, self.mine, self.partner).wait_recv()
            self.out_copy(self.others, piece, 1 - self.mine, self.partner).wait_recv()

    def finish(self):
        @pl.when(self.inner)
        def _():
            for piece in range(self.pieces):
                self.pair_copy(piece).wait_send()
                self.out_copy(self.totals, piece, self.mine, self.mate).wait_send()
                self.out_copy(self.backs, piece, self.mine, self.partner).wait_send()
                self.out_copy(self.others, piece, 1 - self.mine, self.partner).wait_send()

        @pl.when(jnp.logical_not(self.inner))
        def _():
            for piece in range(self.pieces):
                self.end_copy(piece).wait_send()


def line_buffers(pieces, shape, dtype):
    size = shape[0] // pieces
    return [
        pltpu.VMEM((pieces, size, shape[1]), dtype),
        pltpu.VMEM((pieces, size // 2, shape[1]), dtype),
        pltpu.VMEM((pieces, size // 2, shape[1]), dtype),
        pltpu.VMEM((pieces, size // 2, shape[1]), jnp.float32),
    ]


def line_kernel(axis, pieces, x_ref, out_ref, *rest):
    links = Links(rest[4], rest[5])
    meet(line_places(axis))
    line = LineSum(axis, pieces, x_ref, out_ref, rest[:4], links)
    for piece in range(pieces):
        line.start(piece)
    for number in range(line.steps()):
        line.step(number)
    for piece in range(pieces):
        line.ready(piece)
    line.finish()


def in_vmem(count):
    return [pl.BlockSpec(memory_space=pltpu.VMEM)] * count


def line_summed(value, axis, call, pieces):
    sems = pltpu.SemaphoreType.DMA((5 * pieces,))
    return pl.pallas_call(
        partial(line_kernel, axis, pieces),
        out_shape=jax.ShapeDtypeStruct(value.shape, value.dtype),
        in_specs=in_vmem(1),
        out_specs=in_vmem(1)[0],
        scratch_shapes=line_buffers(pieces, value.shape, value.dtype) + [sems, sems],
        cost_estimate=pl.CostEstimate(
            flops=value.size * 40000, bytes_accessed=value.size * 300, transcendentals=0
        ),
        compiler_params=pltpu.CompilerParams(
            collective_id=call, has_side_effects=True, vmem_limit_bytes=8 * MIB
        ),
        name=f"tp_line_{call}",
    )(value)


def square_places(axes):
    first, second = axes
    where, core = lax.axis_index(first), lax.axis_index(second)
    sibling = {second: 1 - core}
    beside = {first: flipped(where, 0)}
    across = {first: flipped(where, 1)}
    return where, core, sibling, beside, across


class SquareGather:
    def __init__(self, axes, out_refs, links):
        self.where, self.core, self.sibling, self.beside, self.across = square_places(axes)
        self.outs, self.links = out_refs, links
        self.rows = out_refs[0].shape[0] // 8
        begin = (self.where * 2 + self.core) * self.rows
        self.mine = pl.ds(pl.multiple_of(begin, self.rows), self.rows)
        self.started, self.siblings = [], []

    def go(self, out_ref, flip, place, start=0, size=None):
        size = size or self.rows
        owner = self.where
        for bit in range(2):
            if flip >> bit & 1:
                owner = flipped(owner, bit)
        begin = (owner * 2 + self.core) * self.rows + start
        ref = out_ref.at[pl.ds(pl.multiple_of(begin, size), size)]
        copy = self.links.copy(self.links.take(), ref, ref, place)
        copy.start()
        self.started.append(copy)
        return copy

    def start(self):
        self.from_beside, self.from_across, self.upper, self.lower = [], [], [], []
        for out_ref in self.outs:
            self.from_beside.append(self.go(out_ref, 0, self.beside))
            self.from_across.append(self.go(out_ref, 0, self.across))
        for out_ref in self.outs:
            self.siblings.append(self.go(out_ref, 0, self.sibling))

    def forward(self, number):
        out_ref, half = self.outs[number], self.rows // 2
        self.from_beside[number].wait_recv()
        self.upper.append(self.go(out_ref, 1, self.across, 0, half))
        self.siblings.append(self.go(out_ref, 1, self.sibling))
        self.from_across[number].wait_recv()
        self.lower.append(self.go(out_ref, 2, self.beside, half, half))
        self.siblings.append(self.go(out_ref, 2, self.sibling))

    def last(self, number):
        out_ref, half = self.outs[number], self.rows // 2
        self.upper[number].wait_recv()
        self.siblings.append(self.go(out_ref, 3, self.sibling, 0, half))
        self.lower[number].wait_recv()
        self.siblings.append(self.go(out_ref, 3, self.sibling, half, half))

    def finish(self):
        for copy in self.siblings:
            copy.wait_recv()
        for copy in self.started:
            copy.wait_send()

    def places(self):
        return [self.sibling, self.beside, self.across]


class SquareSum:
    def __init__(self, axes, g_ref, columns, out_ref, bufs, links):
        self.where, self.core, self.sibling, self.beside, self.across = square_places(axes)
        self.g_ref, self.out_ref, self.columns, self.links = g_ref, out_ref, columns, links
        self.from_core, self.sums, self.from_chip, self.ends = bufs
        self.rows = g_ref.shape[0] // 8
        self.half = self.rows // 2
        self.core_ids = links.take(4)
        self.chip_ids = links.take(4)
        self.end_ids = links.take(2)

    def block(self, flip, of_core):
        owner = self.where
        for bit in range(2):
            if flip >> bit & 1:
                owner = flipped(owner, bit)
        begin = (owner * 2 + of_core) * self.rows
        return pl.ds(pl.multiple_of(begin, self.rows), self.rows)

    def core_copy(self, flip):
        return self.links.copy(
            self.core_ids + flip,
            self.g_ref.at[self.block(flip, 1 - self.core), self.columns],
            self.from_core.at[flip],
            self.sibling,
        )

    def chip_copy(self, slot):
        flip, start, where = (
            (1, 0, self.beside),
            (3, 0, self.beside),
            (2, self.half, self.across),
            (3, self.half, self.across),
        )[slot]
        return self.links.copy(
            self.chip_ids + slot,
            self.sums.at[flip, pl.ds(start, self.half)],
            self.from_chip.at[slot],
            where,
        )

    def end_copy(self, slot):
        flip, start, where = ((2, 0, self.across), (1, self.half, self.beside))[slot]
        return self.links.copy(
            self.end_ids + slot,
            self.sums.at[flip, pl.ds(start, self.half)],
            self.ends.at[slot],
            where,
        )

    def start(self):
        for flip in (3, 1, 2, 0):
            self.core_copy(flip).start()

    def add_core(self, flip):
        self.core_copy(flip).wait_recv()
        own = self.g_ref[self.block(flip, self.core), self.columns].astype(jnp.float32)
        self.sums[flip] = (own + self.from_core[flip].astype(jnp.float32)).astype(
            self.sums.dtype
        )

    def first(self):
        self.add_core(3)
        self.chip_copy(1).start()
        self.chip_copy(3).start()
        self.add_core(1)
        self.chip_copy(0).start()
        self.add_core(2)
        self.chip_copy(2).start()
        self.core_copy(0).wait_recv()

    def second(self):
        half = self.half
        self.chip_copy(1).wait_recv()
        self.sums[2, 0:half] = (
            self.sums[2, 0:half].astype(jnp.float32) + self.from_chip[1].astype(jnp.float32)
        ).astype(self.sums.dtype)
        self.end_copy(0).start()
        self.chip_copy(3).wait_recv()
        self.sums[1, half:] = (
            self.sums[1, half:].astype(jnp.float32) + self.from_chip[3].astype(jnp.float32)
        ).astype(self.sums.dtype)
        self.end_copy(1).start()

    def third(self):
        half = self.half
        own = self.g_ref[self.block(0, self.core), self.columns].astype(jnp.float32)
        own = own + self.from_core[0].astype(jnp.float32)
        for slot, part in ((0, slice(0, half)), (1, slice(half, 2 * half))):
            self.chip_copy(2 * slot).wait_recv()
            self.end_copy(slot).wait_recv()
            total = (
                own[part]
                + self.from_chip[2 * slot].astype(jnp.float32)
                + self.ends[slot].astype(jnp.float32)
            )
            self.out_ref[part] = total[:, 0 : self.out_ref.shape[1]]

    def finish(self):
        for flip in range(4):
            self.core_copy(flip).wait_send()
        for slot in range(4):
            self.chip_copy(slot).wait_send()
        for slot in range(2):
            self.end_copy(slot).wait_send()


def square_buffers(rows, width):
    return [
        pltpu.VMEM((4, rows, width), jnp.bfloat16),
        pltpu.VMEM((4, rows, width), jnp.bfloat16),
        pltpu.VMEM((4, rows // 2, width), jnp.bfloat16),
        pltpu.VMEM((2, rows // 2, width), jnp.bfloat16),
    ]


def middle_kernel(
    axes,
    axis,
    pieces,
    group,
    y_ref,
    out_weight_ref,
    x_ref,
    d_out_ref,
    gain_ref,
    weight_ref,
    down_ref,
    block_ref,
    d_middle_ref,
    d_mixed_ref,
    out_grad_ref,
    gain_grad_ref,
    *rest,
):
    if axes is None:
        weight_grad_ref, rest = rest[0], rest[1:]
    else:
        owned, weight_grad_ref, rest = rest[:3], rest[3], rest[4:]
    part = rest[0]
    attention, two_part, two_sum, feed_part, feed_sum = rest[1:6]
    middle, normed, scale, hidden, active = rest[6:11]
    d_gate_ref, d_up_ref, d_active = rest[11:14]
    rest = rest[14:]
    rows, width = x_ref.shape
    units = weight_ref.shape[1] // 2
    size = rows // pieces
    gate_at, up_at, down_at = (slice(i * units, (i + 1) * units) for i in range(3))
    links = Links(rest[12], rest[13])
    lines = [
        LineSum(axis, pieces, source, target, rest[4 * i : 4 * i + 4], links)
        for i, (source, target) in enumerate(
            ((part, attention), (two_part, two_sum), (feed_part, feed_sum))
        )
    ]
    first, two, feed = lines
    squares = []
    if axes is not None:
        down_rows, down_ref = down_ref, rest[26]
        gather = SquareGather(axes, [down_ref], links)
        turn_in(down_ref, gather.mine, 0, units, down_rows)
        squares = [
            SquareSum(axes, weight_grad_ref, pl.ds(i * units, units), target, bufs, links)
            for i, target, bufs in zip(
                range(3), owned, (rest[14 + 4 * i : 18 + 4 * i] for i in range(3))
            )
        ]

    def dot(left, right, over=(1, 0)):
        dims = (((over[0],), (over[1],)), ((), ()))
        return lax.dot_general(left, right, dims, preferred_element_type=jnp.float32)

    def rows_of(piece, count=1):
        return slice(piece * size, (piece + count) * size)

    meet((list(square_places(axes)[2:]) if squares else []) + line_places(axis))
    if squares:
        gather.start()
    for start in range(0, pieces, group):
        at = rows_of(start, group)
        part[at] = dot(y_ref[at], out_weight_ref[...], (1, 1)).astype(part.dtype)
        for piece in range(start, start + group):
            first.start(piece)
    if not squares:
        d_active[...] = dot(d_out_ref[...], down_ref[...])

    def feed_forward(start):
        at = rows_of(start, group)
        mid = x_ref[at].astype(jnp.float32) + attention[at].astype(jnp.float32)
        factor = lax.rsqrt(row_sum(mid * mid) / width + EPSILON)
        unit = mid * factor
        middle[at] = mid
        normed[at] = unit
        scale[at] = jnp.broadcast_to(factor, (group * size, LANES))
        inner = (unit * gain_ref[...]).astype(jnp.bfloat16)
        hidden[at] = inner
        gate = dot(inner, weight_ref[:, gate_at])
        up = dot(inner, weight_ref[:, up_at])
        sigma = logistic(gate)
        swish = gate * sigma
        act = (swish * up).astype(jnp.bfloat16)
        active[at] = act
        d_act = d_active[at]
        d_gate = (d_act * up * sigma * (1.0 + gate * (1.0 - sigma))).astype(jnp.bfloat16)
        d_up = (d_act * swish).astype(jnp.bfloat16)
        d_gate_ref[at] = d_gate
        d_up_ref[at] = d_up
        back = dot(d_gate, weight_ref[:, gate_at], (1, 1)) + dot(
            d_up, weight_ref[:, up_at], (1, 1)
        )
        two_part[at] = back.astype(two_part.dtype)
        for piece in range(start, start + group):
            two.start(piece)
        feed_part[at] = dot(act, down_ref[...], (1, 1)).astype(feed_part.dtype)

    for number in range(first.steps()):
        first.step(number)
        if squares and number == 1:
            gather.forward(0)
        if number >= 2:
            first.ready(number - 2)
            if squares and number == 1 + group:
                gather.last(0)
                gather.finish()
                d_active[...] = dot(d_out_ref[...], down_ref[...])
            if (number - 1) % group == 0:
                feed_forward(number - 1 - group)
    for piece in range(pieces):
        feed.start(piece)

    def weight_grad(left, right, at):
        weight_grad_ref[:, at] = dot(left[...], right[...], (0, 0)).astype(jnp.bfloat16)

    def work(number):
        left = (hidden, hidden, d_out_ref)[number]
        right = (d_gate_ref, d_up_ref, active)[number]
        weight_grad(left, right, (gate_at, up_at, down_at)[number])
        if squares:
            squares[number].start()

    stages = ["first", "second", "third"]

    def square_step(number):
        for i, member in enumerate(squares):
            if 0 <= number - i < len(stages):
                getattr(member, stages[number - i])()

    gain_grad = jnp.zeros((1, width), jnp.float32)

    def back(piece, gain_grad):
        at = rows_of(piece)
        d_inner = two_sum[at].astype(jnp.float32)
        unit = normed[at]
        d_unit = d_inner * gain_ref[...]
        d_middle_ref[at] = d_out_ref[at].astype(jnp.float32) + scale[at, 0:1] * (
            d_unit - unit * (row_sum(d_unit * unit) / width)
        )
        return gain_grad + jnp.sum(d_inner * unit, axis=0, keepdims=True)

    for number in range(two.steps()):
        two.step(number)
        if number < 3:
            work(number)
        if number >= 2:
            two.ready(number - 2)
            gain_grad = back(number - 2, gain_grad)
        if number >= 3:
            feed.step(number - 3)
        if number >= 2:
            square_step(number - 2)
    gain_grad_ref[...] = jnp.broadcast_to(gain_grad, gain_grad_ref.shape)
    d_rounded = d_middle_ref[...].astype(jnp.bfloat16)
    d_mixed_ref[...] = dot(d_rounded, out_weight_ref[...])
    feed.step(two.steps() - 3)
    out_grad_ref[...] = dot(d_rounded, y_ref[...], (0, 0)).astype(jnp.bfloat16)
    for ref in (gain_grad_ref, d_middle_ref, d_mixed_ref, out_grad_ref):
        ref.send()
    for number in range(two.steps() - 2, feed.steps()):
        feed.step(number)
    square_step(two.steps() - 2)
    for ref in owned if squares else ():
        ref.send()
    for piece in range(pieces):
        feed.ready(piece)
        at = rows_of(piece)
        block_ref[at] = (middle[at] + feed_sum[at].astype(jnp.float32)).astype(
            block_ref.dtype
        )
    for line in lines + squares:
        line.finish()


def middle_part(y, out_weight, x, d_out, gain, weight, down, cuts, axes, axis, call, pieces, group):
    rows, width = x.shape
    units = weight.shape[1] // 2
    all_units = (weight.shape[0], 3 * units)
    cols = y.shape[1]
    half, full = jnp.bfloat16, jnp.float32
    shapes = [((rows, width), half), ((rows, width), full), ((rows, cols), full)]
    shapes += [(out_weight.shape, half), ((8, width), full)]
    scratch = []
    if axes is None:
        shapes += [(all_units, half)]
    else:
        owned = weight.shape[0] // 8
        shapes += [((owned, size), full) for size in cuts]
        scratch += [pltpu.VMEM(all_units, half)]
    scratch += [pltpu.VMEM((rows, width), half) for _ in range(6)]
    scratch += [pltpu.VMEM((rows, width), full) for _ in range(2)]
    scratch += [pltpu.VMEM((rows, LANES), full), pltpu.VMEM((rows, width), half)]
    scratch += [pltpu.VMEM((rows, units), half) for _ in range(3)]
    scratch += [pltpu.VMEM((rows, units), full)]
    for _ in range(3):
        scratch += line_buffers(pieces, (rows, width), half)
    sems = pltpu.SemaphoreType.DMA((15 * pieces + 39,))
    scratch += [sems, sems]
    if axes is not None:
        for _ in range(3):
            scratch += square_buffers(owned, units)
        scratch += [pltpu.VMEM((weight.shape[0], units), half)]
    return staged_call(
        partial(middle_kernel, axes, axis, pieces, group),
        f"middle_{call}",
        shapes,
        scratch,
        pltpu.CompilerParams(
            collective_id=call, has_side_effects=True, vmem_limit_bytes=58 * MIB
        ),
    )(y, out_weight, x, d_out, gain, weight, down)


TAIL_NAMES = ["d_mixed", "mixed", "gain", "carried", "proj", "hidden", "out_grad", "initial"]
TAIL_NAMES += ["query", "key", "from_key", "from_value", "cols", "score", "inverse", "gram"]
TAIL_NAMES += ["decay", "conv", "same", "taps", "params", "edge", "weights", "d_middle"]
TAIL_NAMES += ["tokens", "gain_one", "gain_two"]


def tail_kernel(heads, key_dim, axes, axis, pieces, *refs):
    names = TAIL_NAMES
    at = dict(zip(names, refs))
    refs = refs[len(names) :]
    tokens_out, query_out, key_out, value_out, gate_out, tail_out, output_out, small_out = refs[:8]
    refs = refs[8:]
    d_out, d_gate, d_head, d_initial, d_end, d_proj, d_last, d_edge, edge_in = refs[:9]
    d_taps, d_params, ext, d_ext, grad_in, part, one_sum = refs[9:16]
    line_bufs, refs = refs[16:20], refs[20:]
    square_bufs = [refs[4 * i : 4 * i + 4] for i in range(6)]
    here, there, send, recv = refs[24:28]
    rows, width = part.shape
    value_dim = at["from_value"].shape[2]
    query_cols, value_cols = heads * key_dim, heads * value_dim
    conv_cols = 2 * query_cols + value_cols
    where, core, sibling, beside, across = square_places(axes)
    me = lax.axis_index(axis)
    links = Links(send, recv)
    line = LineSum(axis, pieces, part, one_sum, line_bufs, links)

    def square(number, source, begin, target):
        columns = pl.ds(begin, target.shape[1])
        return SquareSum(axes, source, columns, target, square_bufs[number], links)

    square_out = square(0, at["out_grad"].buf, 0, output_out)
    square_gate = square(1, grad_in, conv_cols, gate_out)
    squares = [
        square(2, grad_in, 2 * query_cols, value_out),
        square(3, grad_in, 0, query_out),
        square(4, grad_in, query_cols, key_out),
        square(5, grad_in, conv_cols + value_cols, tail_out),
    ]
    steps = [sibling, beside, across, {axis: flipped(me, 0)}, {axis: flipped(me, 1)}]
    ids = links.take(len(steps))
    state = links.copy(links.take(), d_initial, d_end, sibling)
    edge = links.copy(links.take(), d_edge, edge_in, sibling)
    common = here.shape[1] // 2

    def small_copy(number):
        if number < 3:
            return links.copy(ids + number, here.at[number], there.at[number], steps[number])
        piece = pl.ds(common, common)
        return links.copy(
            ids + number, here.at[number, piece], there.at[number, piece], steps[number]
        )

    def small_step(number):
        small_copy(number).wait_recv()
        if number < 3:
            here[number + 1] = here[number] + there[number]
        else:
            here[number + 1, common:] = here[number, common:] + there[number, common:]
        if number + 1 < len(steps):
            small_copy(number + 1).start()

    def dot(left, right, over=(1, 0)):
        dims = (((over[0],), (over[1],)), ((), ()))
        return lax.dot_general(left, right, dims, preferred_element_type=jnp.float32)

    def to_earlier(copy, buf):
        @pl.when(core == 0)
        def _():
            copy.wait_recv()

        @pl.when(core == 1)
        def _():
            buf[...] = jnp.zeros(buf.shape, buf.dtype)

    def start_earlier(copy):
        @pl.when(core == 1)
        def _():
            copy.start()

    meet([sibling, beside, across] + line_places(axis))
    leave_back_kernel(
        heads,
        at["d_mixed"],
        at["mixed"],
        at["proj"],
        at["gain"],
        at["carried"],
        d_out,
        d_gate,
        d_head,
        d_initial,
    )
    start_earlier(state)
    at["out_grad"].settle()
    square_out.start()
    grad_in[:, conv_cols : conv_cols + value_cols] = dot(
        at["hidden"][...], d_gate[...], (0, 0)
    ).astype(grad_in.dtype)
    square_gate.start()
    square_out.first()
    to_earlier(state, d_end)

    def between(head):
        if head == 0:
            square_gate.first()
            square_out.second()
        if head == heads - 1:
            square_gate.second()
            square_out.third()
            output_out.send()

    enter_back_kernel(
        heads,
        key_dim,
        between,
        d_out,
        d_gate,
        d_end,
        at["initial"],
        at["proj"],
        at["edge"],
        at["same"],
        at["taps"],
        at["params"],
        at["conv"],
        at["query"],
        at["key"],
        at["decay"],
        at["gram"],
        at["score"],
        at["inverse"],
        at["from_key"],
        at["from_value"],
        at["cols"],
        d_proj,
        d_last,
        d_edge,
        d_taps,
        d_params,
        ext,
        d_ext,
    )
    start_earlier(edge)
    half = rows // 2
    gain_grad = jnp.zeros((1, width), jnp.float32)
    for begin in (0, half):
        if begin:
            to_earlier(edge, edge_in)
            d_proj[rows - EDGE :, 0:conv_cols] = (d_last[...] + edge_in[...]).astype(
                d_proj.dtype
            )
        these = slice(begin, begin + half)
        back = dot(d_proj[these], at["weights"][...], (1, 1))
        part[these] = back.astype(part.dtype)
        for piece in range(begin * pieces // rows, (begin + half) * pieces // rows):
            line.start(piece)
        x = at["tokens"][these].astype(jnp.float32)
        unit = x * lax.rsqrt(row_sum(x * x) / width + EPSILON)
        gain_grad = gain_grad + jnp.sum(back * unit, axis=0, keepdims=True)
    here[0] = jnp.zeros(here.shape[1:], here.dtype)
    margin = at["taps"].shape[0]
    here[0, 0:margin, 0:conv_cols] = d_taps[0:margin]
    here[0, margin : margin + 2, 0:LANES] = d_params[0:2]
    here[0, margin + 2 : margin + 3, 0:width] = at["gain_two"][0:1]
    here[0, common : common + 1, 0:value_dim] = d_head[0:1]
    here[0, common + 1 : common + 2, 0:width] = gain_grad
    small_copy(0).start()
    for member in squares:
        begin, size = member.columns.start, member.columns.size
        grad_in[:, begin : begin + size] = dot(
            at["hidden"][...], d_proj[:, begin : begin + size], (0, 0)
        ).astype(grad_in.dtype)
        member.start()
    square_gate.third()
    gate_out.send()

    def tokens_back(piece):
        these = slice(piece * rows // pieces, (piece + 1) * rows // pieces)
        x = at["tokens"][these].astype(jnp.float32)
        factor = lax.rsqrt(row_sum(x * x) / width + EPSILON)
        unit = x * factor
        d_unit = one_sum[these].astype(jnp.float32) * at["gain_one"][...]
        tokens_out[these] = at["d_middle"][these] + factor * (
            d_unit - unit * (row_sum(d_unit * unit) / width)
        )

    for number in range(line.steps()):
        line.step(number)
        if number < len(squares):
            squares[number].first()
        if number < len(steps):
            small_step(number)
        if number >= 3 and number - 3 < len(squares):
            squares[number - 3].second()
        if number >= 2:
            line.ready(number - 2)
            tokens_back(number - 2)
    tokens_out.send()
    for member in squares[line.steps() - 3 :]:
        member.second()
    for member in squares:
        member.third()
        member.out_ref.send()
    small_out[0:common, :] = here[3, 0:common]
    small_out[common:, :] = here[len(steps), common:]
    small_out.send()
    line.finish()
    for member in squares + [square_out, square_gate]:
        member.finish()
    for number in range(len(steps)):
        small_copy(number).wait_send()

    @pl.when(core == 1)
    def _():
        state.wait_send()
        edge.wait_send()


def tail_part(heads, key_dim, args, out_cols, axes, axis, call, pieces):
    proj, weights, taps = args["proj"], args["weights"], args["taps"]
    rows, width = args["tokens"].shape
    conv_cols = taps.shape[1]
    value_dim = args["from_value"].shape[2]
    value_cols = heads * value_dim
    query_cols = heads * key_dim
    owned = weights.shape[0] // 8
    common = -(-(taps.shape[0] + 3) // 8) * 8
    small = (2 * common, max(conv_cols, width))
    half, full = jnp.bfloat16, jnp.float32
    tail_cols = weights.shape[1] - conv_cols - value_cols
    shapes = [(rows, width)]
    cuts = [query_cols, query_cols, value_cols, value_cols, tail_cols, out_cols]
    shapes += [(owned, size) for size in cuts] + [small]
    state = (heads, key_dim, value_dim)
    scratch = [
        pltpu.VMEM((rows, value_cols), full),
        pltpu.VMEM((rows, value_cols), half),
        pltpu.VMEM((8, value_dim), full),
        pltpu.VMEM(state, full),
        pltpu.VMEM(state, full),
        pltpu.VMEM(proj.shape, half),
        pltpu.VMEM((EDGE, conv_cols), full),
        pltpu.VMEM((EDGE, conv_cols), full),
        pltpu.VMEM((EDGE, conv_cols), full),
        pltpu.VMEM((8, conv_cols), full),
        pltpu.VMEM((8, LANES), full),
        pltpu.VMEM((EDGE + rows, conv_cols), full),
        pltpu.VMEM((2 * EDGE + rows, conv_cols), full),
        pltpu.VMEM(weights.shape, half),
        pltpu.VMEM((rows, width), half),
        pltpu.VMEM((rows, width), half),
    ]
    scratch += line_buffers(pieces, (rows, width), half)
    for size in (out_cols, value_cols, value_cols, query_cols, query_cols, tail_cols):
        scratch += square_buffers(owned, size)
    sems = pltpu.SemaphoreType.DMA((5 * pieces + 10 * 6 + 7,))
    scratch += [pltpu.VMEM((6,) + small, full), pltpu.VMEM((5,) + small, full), sems, sems]
    return staged_call(
        partial(tail_kernel, heads, key_dim, axes, axis, pieces),
        f"tail_{call}",
        [(shape, full) for shape in shapes],
        scratch,
        pltpu.CompilerParams(
            collective_id=call, has_side_effects=True, vmem_limit_bytes=58 * MIB
        ),
    )(*[args[name] for name in TAIL_NAMES])


def finish_kernel(heads, axes, plain, turned, *refs):
    small, tail, refs = refs[0], refs[1], refs[2:]
    sources, refs = refs[: plain + turned], refs[plain + turned :]
    made, refs = refs[: plain + turned], refs[plain + turned :]
    gain_one, gain_two, decay, beta, query, key, value, log, bias, head = refs[:10]
    for number in range(plain):
        sources[number].settle()
        made[number].send(source=sources[number].buf)
    for number in range(plain, plain + turned):
        made[number][...] = sources[number][...].T
        made[number].send()
    common = small.shape[0] // 2
    margin = query.shape[0]
    owned = tail.shape[0]
    mine = lax.axis_index(axes[0]) * lax.axis_size(axes[1]) + lax.axis_index(axes[1])
    at = pl.ds(pl.multiple_of(mine * owned, owned), owned)
    gain_one[...] = small[common + 1 : common + 2, at]
    gain_two[...] = small[margin + 2 : margin + 3, at]
    columns = tail[...].T
    decay[...] = columns[0:heads]
    beta[...] = columns[heads : 2 * heads]
    begin = 0
    for ref in (query, key, value):
        ref[...] = small[0:margin, begin : begin + ref.shape[1]]
        begin += ref.shape[1]
    log[...] = small[margin : margin + 1, 0:heads]
    bias[...] = small[margin + 1 : margin + 2, 0:heads]
    head[...] = small[common : common + 1, 0 : head.shape[1]]


def finished(plain, turned, small, tail, heads, cuts, head_width, margin, axes):
    owned = tail.shape[0]
    shapes = [(x.shape, x.dtype) for x in plain]
    shapes += [(x.shape[::-1], x.dtype) for x in turned]
    little = [(1, owned)] * 2 + [(heads, owned)] * 2
    little += [(margin, size) for size in cuts]
    little += [(1, heads)] * 2 + [(1, head_width)]
    shapes += [(shape, jnp.float32) for shape in little]
    return staged_call(
        partial(finish_kernel, heads, axes, len(plain), len(turned)),
        "finish",
        shapes,
        [],
        pltpu.CompilerParams(vmem_limit_bytes=56 * MIB),
    )(small, tail, *plain, *turned)


def head_kernel(heads, key_dim, axes, *refs):
    shards, lines, refs = refs[:4], refs[4:8], refs[8:]
    out_shard, gate_rows, up_rows = refs[:3]
    tokens, same, tap_query, tap_key, tap_value, params, gain = refs[3:10]
    in_full, out_full, mlp_full, gain_one, gain_two, hidden, proj, edge, taps = refs[10:19]
    conv, query, key, decay, gram, score, inverse, from_key, from_value = refs[19:28]
    carried, cols, initial, y, mixed = refs[28:33]
    local, offset, edge_out, ext, tail_rows, send, recv = refs[33:]
    rows, width = tokens.shape
    conv_cols = conv.shape[1]
    core = lax.axis_index(axes[1])
    links = Links(send, recv)
    first = SquareGather(axes, [in_full.buf], links)
    later = SquareGather(axes, [out_full.buf, mlp_full.buf], links)
    mine = first.mine
    begin = 0
    for shard in shards:
        size = shard.shape[1]
        in_full[mine, begin : begin + size] = shard[...]
        begin += size
    tail_rows[...] = jnp.zeros(tail_rows.shape, tail_rows.dtype)
    line = 0
    for part in lines:
        tail_rows[line : line + part.shape[0]] = part[...].astype(jnp.float32)
        line += part.shape[0]
    in_full[mine, begin:] = tail_rows[...].T.astype(jnp.bfloat16)
    meet(first.places())
    first.start()
    begin = 0
    for number in range(3):
        begin = tap_at(taps, (tap_query, tap_key, tap_value)[number], begin)
    out_full[mine] = out_shard[...]
    units = mlp_full.shape[1] // 2
    turn_in(mlp_full, mine, 0, units, gate_rows)
    turn_in(mlp_full, mine, units, units, up_rows)
    x = tokens[...].astype(jnp.float32)
    unit = x * lax.rsqrt(row_sum(x * x) / width + EPSILON)
    first.forward(0)
    first.last(0)
    later.start()
    first.finish()
    in_full.send()
    tail_cols = tail_rows.shape[0]
    gains = in_full[:, in_full.shape[1] - tail_cols :].astype(jnp.float32).T
    gain_one[...] = gains[2 * heads : 2 * heads + 1]
    gain_two[...] = gains[2 * heads + 1 : 2 * heads + 2]
    hidden[...] = (unit * gain_one[...]).astype(jnp.bfloat16)
    hidden.send()
    edge_out[...] = lax.dot_general(
        hidden[rows - EDGE :],
        in_full[:, 0:conv_cols],
        (((1,), (0,)), ((), ())),
        preferred_element_type=jnp.float32,
    ).astype(jnp.bfloat16)
    edge_copy = links.copy(links.take(), edge_out, edge.buf, first.sibling)

    @pl.when(core == 0)
    def _():
        edge_copy.start()
        edge.buf[...] = jnp.zeros(edge.shape, edge.dtype)

    proj[...] = lax.dot_general(
        hidden[...],
        in_full[...],
        (((1,), (0,)), ((), ())),
        preferred_element_type=jnp.float32,
    )
    proj.send()

    @pl.when(core == 1)
    def _():
        edge_copy.wait_recv()

    def between(head):
        if head == 0:
            later.forward(0)
            later.forward(1)

    enter_kernel(
        heads,
        key_dim,
        False,
        proj,
        edge,
        same,
        taps,
        params,
        conv,
        query,
        key,
        decay,
        gram,
        score,
        inverse,
        from_key,
        from_value,
        carried,
        local,
        offset,
        cols,
        ext,
        between=between,
    )
    for ref in (query, key, cols, edge, taps):
        ref.send()
    state_copy = links.copy(links.take(), offset, initial.buf, first.sibling)

    @pl.when(core == 0)
    def _():
        state_copy.start()
        initial.buf[...] = jnp.zeros(initial.shape, initial.dtype)

    later.last(0)
    later.last(1)

    @pl.when(core == 1)
    def _():
        state_copy.wait_recv()

    initial.send()
    leave_kernel(heads, carried, local, initial, proj, gain, y, mixed)
    y.send()
    mixed.send()
    later.finish()

    @pl.when(core == 0)
    def _():
        edge_copy.wait_send()
        state_copy.wait_send()


def turn_in(target, mine, begin, units, turned):
    size = turned.shape[0]
    block = turned[...].astype(jnp.float32).T.astype(jnp.bfloat16)
    target[mine, begin : begin + size] = block
    if size < units:
        target[mine, begin + size : begin + units] = jnp.zeros(
            (block.shape[0], units - size), jnp.bfloat16
        )


def tap_at(taps, source, begin):
    size = source.shape[1]
    taps[:, begin : begin + size] = source[...]
    return begin + size


def head_part(heads, key_dim, args, padded, axes, call):
    query, value, out_shard = args[0], args[2], args[8]
    rows, width = args[11].shape
    tail_cols = -(-(2 * heads + 2) // LANES) * LANES
    owned, query_cols = query.shape
    value_cols = value.shape[1]
    conv_cols = 2 * query_cols + value_cols
    in_cols = conv_cols + value_cols + tail_cols
    value_dim = value_cols // heads
    half, full = jnp.bfloat16, jnp.float32
    square = ((heads, rows, rows), full)
    state = ((heads, key_dim, value_dim), full)
    shapes = [
        ((8 * owned, in_cols), half),
        ((8 * owned, out_shard.shape[1]), half),
        ((8 * owned, 2 * padded), half),
        ((1, 8 * owned), full),
        ((1, 8 * owned), full),
        ((rows, width), half),
        ((rows, in_cols), full),
        ((EDGE, conv_cols), half),
        ((args[13].shape[0], conv_cols), full),
        ((rows, conv_cols), full),
        ((rows, query_cols), full),
        ((rows, query_cols), full),
        square,
        square,
        square,
        square,
        ((heads, rows, key_dim), full),
        ((heads, rows, value_dim), full),
        ((heads, rows, key_dim), full),
        ((rows, LANES), full),
        state,
        ((rows, value_cols), half),
        ((rows, value_cols), full),
    ]
    sems = pltpu.SemaphoreType.DMA((29,))
    scratch = [
        pltpu.VMEM((heads, rows, value_dim), full),
        pltpu.VMEM(*state),
        pltpu.VMEM((EDGE, conv_cols), half),
        pltpu.VMEM((EDGE + rows, conv_cols), full),
        pltpu.VMEM((tail_cols, owned), full),
        sems,
        sems,
    ]
    return staged_call(
        partial(head_kernel, heads, key_dim, axes),
        f"head_{call}",
        shapes,
        scratch,
        pltpu.CompilerParams(
            collective_id=call, has_side_effects=True, vmem_limit_bytes=58 * MIB
        ),
    )(*args)


def apply_map(matrix, addend, incoming):
    return jnp.einsum("hde,hew->hdw", matrix, incoming, precision=HIGHEST) + addend


def local(
    tokens,
    segments,
    cotangent,
    mixer_gain,
    mlp_gain,
    query_weight,
    key_weight,
    value_weight,
    gate_weight,
    decay_weight,
    beta_weight,
    output_weight,
    conv_query,
    conv_key,
    conv_value,
    decay_log,
    decay_bias,
    head_gain,
    hidden_gate,
    hidden_up,
    hidden_down,
):
    width = tokens.shape[-1]
    inputs = tokens.reshape(-1, width).astype(jnp.float32)
    row_count = inputs.shape[0]
    query_cols = query_weight.shape[1]
    value_cols = value_weight.shape[1]
    head_count = decay_weight.shape[1]
    ff_cols = hidden_gate.shape[1]
    axes = ("dp", "ctx")
    used = 2 * query_cols + 2 * value_cols + 2 * head_count + 2
    pad_cols = -used % LANES
    own_rows = query_weight.shape[0]
    conv_cols = 2 * query_cols + value_cols
    key_dim = query_cols // head_count
    taps = conv_query.shape[0]
    margin = taps - 1
    value_dim = value_cols // head_count
    ctx_size = lax.axis_size("ctx")
    seg_padded = jnp.concatenate([jnp.full((margin,), -1, jnp.int32), segments.reshape(-1)], 0)
    seg_ext = lax.dynamic_slice_in_dim(
        seg_padded, lax.axis_index("ctx") * row_count, row_count + margin
    )
    same_doc = jnp.stack(
        [
            (seg_ext[margin - lag : margin - lag + row_count] == seg_ext[margin:])
            for lag in range(taps)
        ],
        1,
    ).astype(jnp.float32)
    lane_pad = (0, LANES - head_count)
    params = jnp.stack([jnp.pad(decay_log, lane_pad), jnp.pad(decay_bias, lane_pad)])
    gain_row = head_gain[None, :]
    squared = lax.axis_size("dp") == 4 and ctx_size == 2
    if squared:
        head_args = [
            query_weight,
            key_weight,
            value_weight,
            gate_weight,
            decay_weight.T,
            beta_weight.T,
            mixer_gain[None, :],
            mlp_gain[None, :],
            output_weight,
            hidden_gate.T,
            hidden_up.T,
            tokens.reshape(-1, width),
            same_doc,
            conv_query,
            conv_key,
            conv_value,
            params,
            gain_row,
        ]
        padded = -(-ff_cols // LANES) * LANES
        entered = head_part(head_count, key_dim, head_args, padded, axes, 5)
        in_weights, full_output, mlp_weights, gain_one_row, gain_two_row = entered[:5]
        down_weights = hidden_down.T
        hidden_one, projected, edge_rows, conv_weight, convolved = entered[5:10]
        queries, key_rows, decay_pair, gram, score, inverse = entered[10:16]
        from_key, from_value, carried, mixer_cols, initial, mixed_b, mixed = entered[16:]
    else:
        in_weights = lax.all_gather(
            jnp.concatenate(
                [
                    query_weight,
                    key_weight,
                    value_weight,
                    gate_weight,
                    decay_weight,
                    beta_weight,
                    mixer_gain[:, None],
                    mlp_gain[:, None],
                    jnp.zeros((own_rows, pad_cols), jnp.bfloat16),
                ],
                1,
            ),
            axes,
            axis=0,
            tiled=True,
        )
        full_output = lax.all_gather(output_weight, axes, axis=0, tiled=True)
        gain_one = in_weights[:, used - 2].astype(jnp.float32)
        gain_two = in_weights[:, used - 1].astype(jnp.float32)
        unit_pad = ((0, 0), (0, -ff_cols % LANES))
        own_mlp = jnp.concatenate(
            [jnp.pad(part, unit_pad) for part in (hidden_gate, hidden_up, hidden_down)], 1
        )
        mlp_weights = lax.all_gather(own_mlp, axes, axis=0, tiled=True)
        rms_one = lax.rsqrt(jnp.mean(inputs * inputs, -1, keepdims=True) + EPSILON)
        normed_one = inputs * rms_one
        hidden_one = (normed_one * gain_one).astype(jnp.bfloat16)
        projected = jnp.dot(hidden_one, in_weights, preferred_element_type=jnp.float32)
        conv_weight = jnp.concatenate([conv_query, conv_key, conv_value], 1)
        last_rows = projected[row_count - EDGE :, :conv_cols].astype(jnp.bfloat16)
        edge_rows = passed_along(last_rows, "ctx", 1)
        chained = ctx_size > 2
        square = ((head_count, row_count, row_count), jnp.float32)
        tall_key = ((head_count, row_count, key_dim), jnp.float32)
        tall_value = ((head_count, row_count, value_dim), jnp.float32)
        flat_key = ((row_count, query_cols), jnp.float32)
        state = ((head_count, key_dim, value_dim), jnp.float32)
        entered = on_core(
            partial(enter_kernel, head_count, key_dim, chained),
            "mixer_enter",
            [
                ((row_count, conv_cols), jnp.float32),
                flat_key,
                flat_key,
                square,
                square,
                square,
                square,
                tall_key,
                tall_value,
                tall_key,
                tall_value,
                state,
                ((row_count, LANES), jnp.float32),
            ]
            + ([((head_count, key_dim, key_dim), jnp.float32)] if chained else []),
            [((EDGE + row_count, conv_cols), jnp.float32)],
        )(projected, edge_rows, same_doc, conv_weight, params)
        convolved, queries, key_rows, decay_pair, gram, score, inverse = entered[:7]
        from_key, from_value, carried, local_out, offset, mixer_cols = entered[7:13]

        initial = jnp.zeros_like(offset)
        for hop in range(ctx_size - 1):
            leaving = offset if hop == 0 else apply_map(entered[13], offset, initial)
            initial = passed_along(leaving, "ctx", 1)
        mixed_b, mixed = on_core(
            partial(leave_kernel, head_count),
            "mixer_leave",
            [((row_count, value_cols), jnp.bfloat16), ((row_count, value_cols), jnp.float32)],
        )(carried, local_out, initial, projected, gain_row)
        gain_one_row, gain_two_row = gain_one[None, :], gain_two[None, :]
        units = mlp_weights.shape[1] // 3
        down_weights = mlp_weights[:, 2 * units :]
        mlp_weights = mlp_weights[:, : 2 * units]
    grad_rows = cotangent.reshape(-1, width)
    block_out, d_middle, d_mixed, grad_output, gain_grad, *mlp_own = middle_part(
        mixed_b,
        full_output,
        tokens.reshape(-1, width),
        grad_rows,
        gain_two_row,
        mlp_weights,
        down_weights,
        (ff_cols,) * 3,
        axes if squared else None,
        "tp",
        0,
        4,
        1,
    )
    grad_gain_two = gain_grad[0]

    def scattered(member):
        total = lax.psum_scatter(
            member.astype(jnp.bfloat16), axes, scatter_dimension=0, tiled=True
        )
        return total.astype(jnp.float32)

    if not squared:
        total = scattered(mlp_own[0])
        units = total.shape[1] // 3
        mlp_own = [total[:, i * units : i * units + ff_cols] for i in range(3)]
    if squared:
        tail_args = {
            "d_mixed": d_mixed,
            "mixed": mixed,
            "proj": projected,
            "gain": gain_row,
            "carried": carried,
            "initial": initial,
            "edge": edge_rows,
            "same": same_doc,
            "taps": conv_weight,
            "params": params,
            "conv": convolved,
            "query": queries,
            "key": key_rows,
            "decay": decay_pair,
            "gram": gram,
            "score": score,
            "inverse": inverse,
            "from_key": from_key,
            "from_value": from_value,
            "cols": mixer_cols,
            "hidden": hidden_one,
            "weights": in_weights,
            "out_grad": grad_output,
            "d_middle": d_middle,
            "tokens": tokens.reshape(-1, width),
            "gain_one": gain_one_row,
            "gain_two": gain_grad,
        }
        tokens_grad, query_own, key_own, value_own, gate_own, tail_own, output_own, small = (
            tail_part(head_count, key_dim, tail_args, value_cols, axes, "tp", 6, 4)
        )
        large = [block_out, tokens_grad, query_own, key_own, value_own, gate_own, output_own]
        cuts = (query_cols, query_cols, value_cols)
        ended = finished(
            large, mlp_own, small, tail_own, head_count, cuts, value_dim, taps, axes
        )
        block_out, tokens_grad, query_own, key_own, value_own, gate_own = ended[:6]
        output_own, mlp_own = ended[6], [member.T for member in ended[7:10]]
        gain_one_own, gain_two_own = ended[10].reshape(-1), ended[11].reshape(-1)
        projections = [query_own, key_own, value_own, gate_own, ended[12].T, ended[13].T]
        conv_totals = ended[14:17]
        log_total, bias_total, head_total = (member.reshape(-1) for member in ended[17:20])
    else:
        d_out, d_gate, d_head, init_grad = on_core(
            partial(leave_back_kernel, head_count),
            "mixer_leave_back",
            [
                ((row_count, value_cols), jnp.float32),
                ((row_count, value_cols), jnp.bfloat16),
                ((8, value_dim), jnp.float32),
                state,
            ],
        )(d_mixed, mixed, projected, gain_row, carried)
        d_head = d_head[0]
        end_grad = jnp.zeros_like(offset)
        for hop in range(ctx_size - 1):
            leaving = (
                init_grad
                if hop == 0
                else apply_map(jnp.swapaxes(entered[13], 1, 2), init_grad, end_grad)
            )
            end_grad = passed_along(leaving, "ctx", -1)
        edge_shape = ((EDGE, conv_cols), jnp.float32)
        d_proj, d_last, d_edge, d_conv, d_params = on_core(
            partial(enter_back_kernel, head_count, key_dim, None),
            "mixer_enter_back",
            [
                (projected.shape, jnp.bfloat16),
                edge_shape,
                edge_shape,
                ((8, conv_cols), jnp.float32),
                ((8, LANES), jnp.float32),
            ],
            [
                ((EDGE + row_count, conv_cols), jnp.float32),
                ((2 * EDGE + row_count, conv_cols), jnp.float32),
            ],
        )(
            d_out,
            d_gate,
            end_grad,
            initial,
            projected,
            edge_rows,
            same_doc,
            conv_weight,
            params,
            convolved,
            queries,
            key_rows,
            decay_pair,
            gram,
            score,
            inverse,
            from_key,
            from_value,
            mixer_cols,
        )
        d_conv = d_conv[:taps]
        d_log, d_bias = d_params[0, :head_count], d_params[1, :head_count]
        edge_back = passed_along(d_edge, "ctx", -1)
        d_proj = lax.dynamic_update_slice(
            d_proj, (d_last + edge_back).astype(jnp.bfloat16), (row_count - EDGE, 0)
        )
        grad_input = jnp.einsum("rd,rc->dc", hidden_one, d_proj, preferred_element_type=jnp.float32)
        one_part = jnp.einsum("rc,dc->rd", d_proj, in_weights, preferred_element_type=jnp.float32)
        one_part, mlp_own = lax.optimization_barrier((one_part, mlp_own))
        one_sum = summed(one_part.astype(jnp.bfloat16), "tp", 2)
        d_hidden_one = one_sum.astype(jnp.float32)
        dn_one = d_hidden_one * gain_one
        tokens_grad = d_middle + rms_one * (
            dn_one - normed_one * jnp.mean(dn_one * normed_one, -1, keepdims=True)
        )
        edges = [
            0,
            query_cols,
            2 * query_cols,
            conv_cols,
            conv_cols + value_cols,
            conv_cols + value_cols + head_count,
            conv_cols + value_cols + 2 * head_count,
        ]

        grad_gain_one = jnp.sum(d_hidden_one * normed_one, 0)
        column = jnp.arange(grad_input.shape[1])[None, :]
        grad_input = jnp.where(column == used - 2, grad_gain_one[:, None], grad_input)
        grad_input = jnp.where(column == used - 1, grad_gain_two[:, None], grad_input)
        output_own = scattered(grad_output)
        input_own = scattered(grad_input)
        gain_one_own = input_own[:, used - 2]
        gain_two_own = input_own[:, used - 1]
        rest = jnp.concatenate([d_head, d_log, d_bias])
        pad_row = jnp.zeros((-rest.shape[0] % conv_cols,), jnp.float32)
        rest = jnp.concatenate([rest, pad_row]).reshape(-1, conv_cols)
        packed = jnp.concatenate([d_conv, rest], 0)
        lines = packed.shape[0]
        packed = jnp.concatenate([packed, jnp.zeros((-lines % 8, conv_cols), jnp.float32)], 0)
        packed = small_sum(packed, ("dp", "ctx"), 3)
        conv_total = packed[:taps]
        rest = packed[taps:lines].reshape(-1)
        log_total = rest[value_dim : value_dim + head_count]
        bias_total = rest[value_dim + head_count : value_dim + 2 * head_count]
        head_total = small_sum(
            jnp.broadcast_to(rest[None, :value_dim], (8, value_dim)), ("tp",), 4
        )[0]
        projections = [input_own[:, edges[i] : edges[i + 1]] for i in range(6)]
        conv_totals = [
            conv_total[:, :query_cols],
            conv_total[:, query_cols : 2 * query_cols],
            conv_total[:, 2 * query_cols :],
        ]
    tokens_grad = tokens_grad.reshape(tokens.shape)
    block_out = block_out.reshape(tokens.shape)
    reduced = (
        gain_one_own,
        gain_two_own,
        *projections,
        output_own,
        *mlp_own,
    )
    return (
        block_out,
        tokens_grad,
        reduced[0],
        reduced[1],
        reduced[2],
        reduced[3],
        reduced[4],
        reduced[5],
        reduced[6],
        reduced[7],
        reduced[8],
        *conv_totals,
        log_total,
        bias_total,
        head_total,
        reduced[9],
        reduced[10],
        reduced[11],
    )


def solution(mesh):
    return jax.shard_map(
        local,
        mesh=mesh,
        in_specs=(
            P("dp", "ctx", None),
            P("dp", None),
            P("dp", "ctx", None),
            P(("dp", "ctx")),
            P(("dp", "ctx")),
            P(("dp", "ctx"), "tp"),
            P(("dp", "ctx"), "tp"),
            P(("dp", "ctx"), "tp"),
            P(("dp", "ctx"), "tp"),
            P(("dp", "ctx"), "tp"),
            P(("dp", "ctx"), "tp"),
            P(("dp", "ctx"), "tp"),
            P(None, "tp"),
            P(None, "tp"),
            P(None, "tp"),
            P("tp"),
            P("tp"),
            P(),
            P(("dp", "ctx"), "tp"),
            P(("dp", "ctx"), "tp"),
            P(("dp", "ctx"), "tp"),
        ),
        out_specs=(
            P("dp", "ctx", None),
            P("dp", "ctx", None),
            P(("dp", "ctx")),
            P(("dp", "ctx")),
            P(("dp", "ctx"), "tp"),
            P(("dp", "ctx"), "tp"),
            P(("dp", "ctx"), "tp"),
            P(("dp", "ctx"), "tp"),
            P(("dp", "ctx"), "tp"),
            P(("dp", "ctx"), "tp"),
            P(("dp", "ctx"), "tp"),
            P(None, "tp"),
            P(None, "tp"),
            P(None, "tp"),
            P("tp"),
            P("tp"),
            P(),
            P(("dp", "ctx"), "tp"),
            P(("dp", "ctx"), "tp"),
            P(("dp", "ctx"), "tp"),
        ),
        check_vma=False,
    )
```
